32 devices in a mesh: dp: 4 (over y, x), fsdp: 8 (over z, core).
Axes of the slice: x: 2, y: 2, z: 4, core: 2. Of those that a mesh axis runs over, the one named last changes fastest.
Arguments:
- tokens: bfloat16 [32, 256, 2048], P(None, ('dp', 'fsdp')), may hold values from -6 to 6
- cotangent: bfloat16 [32, 256, 2048], P(None, ('dp', 'fsdp')), may hold values from -6 to 6
- lengths: int32 [32], replicated, may hold values from 1 to 256, 6144 in all
- deal_order: int32 [32], replicated, may hold values from 0 to 31, each once
- norm_gain: float32 [2048], P(('dp', 'fsdp')), may hold values from 0.5 to 1.5
- in_weight: float32 [2048, 8192], P(('dp', 'fsdp')), may hold values from -0.125 to 0.125
- conv_weight: float32 [4096, 4], P(('dp', 'fsdp')), may hold values from -3 to 3
- conv_bias: float32 [4096], P(('dp', 'fsdp')), may hold values from -3 to 3
- x_weight: float32 [4096, 160], P(('dp', 'fsdp')), may hold values from -0.09375 to 0.09375
- dt_weight: float32 [4096, 128], P(('dp', 'fsdp')), may hold values from -0.5 to 0.5
- dt_bias: float32 [4096], P(('dp', 'fsdp')), may hold values from -6 to -2.5
- decay_log: float32 [4096, 16], P(('dp', 'fsdp')), may hold values from 0 to 2.77
- skip_gain: float32 [4096], P(('dp', 'fsdp')), may hold values from 0.5 to 1.5
- out_weight: float32 [4096, 2048], P(('dp', 'fsdp')), may hold values from -0.1875 to 0.1875
Outputs:
- output: bfloat16 [32, 256, 2048], P(None, ('dp', 'fsdp'))
- input_grad: bfloat16 [32, 256, 2048], P(None, ('dp', 'fsdp'))
- norm_gain_grad: float32 [2048], P(('dp', 'fsdp'))
- in_weight_grad: float32 [2048, 8192], P(('dp', 'fsdp'))
- conv_weight_grad: float32 [4096, 4], P(('dp', 'fsdp'))
- conv_bias_grad: float32 [4096], P(('dp', 'fsdp'))
- x_weight_grad: float32 [4096, 160], P(('dp', 'fsdp'))
- dt_weight_grad: float32 [4096, 128], P(('dp', 'fsdp'))
- dt_bias_grad: float32 [4096], P(('dp', 'fsdp'))
- decay_log_grad: float32 [4096, 16], P(('dp', 'fsdp'))
- skip_gain_grad: float32 [4096], P(('dp', 'fsdp'))
- out_weight_grad: float32 [4096, 2048], P(('dp', 'fsdp'))
The draws below stay inside these ranges and needn't reach their ends.
Inputs may be any that keep to these rules, and one draw needn't show every extreme that they name: lengths[j] is the number of live tokens of sequence deal_order[j]; its other slots of 256 are padding; the largest is exactly 256 and they sum to 6144. `deal_order`: each sequence appears once.
All inputs are finite; a program needn't handle non-finite values.
Results may differ from the reference program's by a relative error of at most 0.0055.
The reference program's roundings to bfloat16 on the way count: a program that leaves them out, or rounds other values in their place, can miss the bound.
Values may be sent and summed in bfloat16 or wider, within the bound.
A program may use at most 320 MiB of HBM per device.

```python
import math
import jax
import jax.numpy as jnp
import numpy as np
from jax import lax

D = 2048
INNER = 4096
STATE = 16
RANK = 128
CONV = 4
LEN = 256
SPAN = 32
SEQS = 32


def steps_of(stream_key, dims, cuts, smallest, largest):
    def one(dim, parts):
        heights = jax.random.uniform(jax.random.fold_in(jax.random.fold_in(stream_key, 6), dim), (parts,), jnp.float32, smallest / len(cuts), largest / len(cuts))
        return jnp.repeat(jnp.exp(heights), dims[dim] // parts).reshape((-1,) + (1,) * (len(dims) - dim - 1))

    gain = one(*cuts[0])
    for cut in cuts[1:]:
        gain = gain * one(*cut)
    return gain


def split_up(count, total, limit, lean):
    portions = [(1 << 20) // math.isqrt(grade ** lean) + 1 for grade in range(2, count + 1)]
    rest, holding = total - limit - (count - 1), [1] * (count - 1)
    while rest > 0:
        movable = [i for i in range(count - 1) if holding[i] < limit]
        mass, remaining = sum([portions[i] for i in movable]), rest
        for i in movable:
            addition = min(limit - holding[i], max(1, remaining * portions[i] // mass), rest)
            holding[i] = holding[i] + addition
            rest = rest - addition
    return np.array([limit] + holding)


def ragged_sizes(own_key, amount, total, limit, skew):
    if amount == 2:
        one = jax.random.randint(own_key, (), max(1, total - limit), min(limit, total - 1) + 1)
        return jnp.stack([one, total - one])
    tallies = jnp.asarray(split_up(amount, total, limit, skew), jnp.int32)
    twos = (amount - 1) // 2
    source_of, taker = tallies[1:1 + 2 * twos:2], tallies[2:2 + 2 * twos:2]
    room = jnp.minimum(source_of - 1, limit - taker)
    moved = jax.random.randint(jax.random.fold_in(own_key, 1), (twos,), 0, 1 << 20) % (room + 1)
    tallies = tallies.at[1:1 + 2 * twos:2].set(source_of - moved).at[2:2 + 2 * twos:2].set(taker + moved)
    return tallies[jax.random.permutation(jax.random.fold_in(own_key, 2), amount)]


def centred(rng, extent, scale, limit, cuts=(), kind=jnp.bfloat16):
    entries = scale * jax.random.normal(rng, extent, jnp.float32)
    if cuts:
        entries = entries * steps_of(rng, extent, cuts, -0.22, 0.18)
    return jnp.clip(entries, -limit, limit).astype(kind)


def setup_inputs(seed: int = 0) -> dict:
    keys = jax.random.split(jax.random.key(seed), 15)
    tokens = centred(keys[0], (SEQS, LEN, D), 1.0, 6.0, ((1, 32),))
    cotangent = centred(keys[1], (SEQS, LEN, D), 1.0, 6.0, ((1, 32),))
    lengths = ragged_sizes(keys[2], SEQS, SEQS * LEN * 3 // 4, LEN, 1).astype(jnp.int32)
    deal_order = jax.random.permutation(keys[3], SEQS).astype(jnp.int32)
    norm_gain = jnp.clip(1.0 + 0.1 * jax.random.normal(keys[4], (D,), jnp.float32), 0.5, 1.5)
    in_weight = centred(keys[5], (D, 2 * INNER), D ** -0.5, 0.125, ((0, 32),), jnp.float32)
    conv_weight = centred(keys[6], (INNER, CONV), CONV ** -0.5, 3.0, ((0, 32),), jnp.float32)
    conv_bias = centred(keys[7], (INNER,), 0.5, 3.0, ((0, 32),), jnp.float32)
    x_weight = centred(keys[8], (INNER, RANK + 2 * STATE), INNER ** -0.5, 0.09375, ((0, 32),), jnp.float32)
    dt_weight = centred(keys[9], (INNER, RANK), RANK ** -0.5, 0.5, ((0, 32),), jnp.float32)
    dt_bias = jnp.clip(-6.0 + 3.5 * jax.random.uniform(keys[10], (INNER,), jnp.float32) ** steps_of(keys[10], (INNER,), ((0, 32),), -0.2, 0.2), -6.0, -2.5)
    decay_log = jnp.clip(2.77 * jax.random.uniform(keys[11], (INNER, STATE), jnp.float32) ** steps_of(keys[11], (INNER, STATE), ((0, 32),), -0.2, 0.2), 0.0, 2.77)
    skip_gain = jnp.clip(0.5 + 1.0 * jax.random.uniform(keys[12], (INNER,), jnp.float32) ** steps_of(keys[12], (INNER,), ((0, 32),), -0.2, 0.2), 0.5, 1.5)
    out_weight = centred(keys[13], (INNER, D), (INNER // 4) ** -0.5, 0.1875, ((0, 32),), jnp.float32)
    return dict(tokens=tokens, cotangent=cotangent, lengths=lengths, deal_order=deal_order, norm_gain=norm_gain, in_weight=in_weight, conv_weight=conv_weight, conv_bias=conv_bias, x_weight=x_weight, dt_weight=dt_weight, dt_bias=dt_bias, decay_log=decay_log, skip_gain=skip_gain, out_weight=out_weight)


@jax.custom_vjp
def low(v):
    return lax.optimization_barrier(v.astype(jnp.bfloat16)).astype(jnp.float32)

@jax.custom_vjp
def low_back(v):
    return v

def low_keep(v):
    return (low(v), None)

def low_pass(kept, grad):
    return (grad,)

def back_keep(v):
    return (v, None)

def back_low(kept, grad):
    return (low(grad),)
low.defvjp(low_keep, low_pass)
low_back.defvjp(back_keep, back_low)
EPSILON = 1e-05
HIGHEST = lax.Precision.HIGHEST

def rms_scale(hidden, gain_vec):
    factor = lax.rsqrt(lax.optimization_barrier(jnp.mean(hidden * hidden, axis=-1, keepdims=True)) + EPSILON)
    return hidden * factor * gain_vec

def causal_conv(inner_part, kernel, shift_vec):
    kernel_width = kernel.shape[1]
    length = inner_part.shape[0]
    padded = jnp.pad(inner_part, ((kernel_width - 1, 0), (0, 0)))
    summed = jnp.zeros_like(inner_part) + shift_vec[None, :]
    for offset in range(kernel_width):
        summed = summed + kernel[:, offset][None, :] * padded[offset:offset + length]
    return jax.nn.silu(summed)

def span_pass(carried, pieces, decay_rate):
    delta_rate, drive_b, read_c, inputs = pieces
    results = []
    for position in range(delta_rate.shape[0]):
        factor = jnp.exp(delta_rate[position][None, :] * decay_rate)
        carried = factor * carried + (delta_rate[position] * inputs[position])[None, :] * drive_b[position][:, None]
        results.append(lax.optimization_barrier(jnp.sum(carried * read_c[position][:, None], axis=0)))
    return (carried, jnp.stack(results))

def selective_mix(dt_pre, dt_shift, log_rates, proj_bc, inputs, skip_vec, gate_pre):
    state_size = log_rates.shape[0]
    length, inner_dim = dt_pre.shape
    delta_rate = jax.nn.softplus(dt_pre + dt_shift[None, :])
    decay_rate = -jnp.exp(log_rates)
    blocks = length // SPAN

    def advance(carried, pieces):
        return span_pass(carried, pieces, decay_rate)
    advance = jax.checkpoint(advance)
    pieces = (delta_rate.reshape(blocks, SPAN, inner_dim), proj_bc[:, :state_size].reshape(blocks, SPAN, state_size), proj_bc[:, state_size:].reshape(blocks, SPAN, state_size), inputs.reshape(blocks, SPAN, inner_dim))
    _, results = lax.scan(advance, jnp.zeros((state_size, inner_dim), jnp.float32), pieces)
    mixed_out = results.reshape(length, inner_dim) + skip_vec[None, :] * inputs
    return mixed_out * jax.nn.silu(gate_pre)

def group_forward(weights, group_x, group_mask):
    gain_vec, in_mat, conv_mat, conv_shift, select_mat, rank_mat, dt_shift, log_rates, skip_vec, out_mat = weights
    inner_dim = conv_mat.shape[0]
    rank_dim = rank_mat.shape[1]
    normed = low(rms_scale(group_x, gain_vec))
    both = low_back(jnp.einsum('gld,df->glf', normed, in_mat, precision=HIGHEST))
    inner_part = both[..., :inner_dim]
    gate_pre = both[..., inner_dim:]
    inputs = low(jax.vmap(causal_conv, in_axes=(0, None, None))(inner_part, conv_mat, conv_shift))
    projected = low_back(jnp.einsum('gle,ek->glk', inputs, select_mat, precision=HIGHEST))
    dt_low = low(projected[..., :rank_dim])
    dt_pre = low_back(jnp.einsum('glr,er->gle', dt_low, rank_mat, precision=HIGHEST))
    gated = low(jax.vmap(selective_mix, in_axes=(0, None, None, 0, 0, None, 0))(dt_pre, dt_shift, log_rates.T, projected[..., rank_dim:], inputs, skip_vec, gate_pre))
    branch = low_back(jnp.einsum('gle,ed->gld', gated, out_mat, precision=HIGHEST))
    return group_x + group_mask * branch

def forward(tokens32, weights32, mask):
    weights = tuple((low(item) for item in weights32))
    seq_count, length, model_dim = tokens32.shape
    group_size = math.gcd(seq_count, max(1, 4096 // length))

    def step_group(carry, pieces):
        return (carry, group_forward(weights, pieces[0], pieces[1]))
    _, results = lax.scan(step_group, jnp.zeros((), jnp.float32), (tokens32.reshape(seq_count // group_size, group_size, length, model_dim), mask.reshape(seq_count // group_size, group_size, length, 1)))
    return results.reshape(seq_count, length, model_dim)

def reference(tokens, cotangent, lengths, deal_order, norm_gain, in_weight, conv_weight, conv_bias, x_weight, dt_weight, dt_bias, decay_log, skip_gain, out_weight):
    seq_count, length, model_dim = tokens.shape
    slots = jnp.arange(seq_count, dtype=jnp.int32)
    matches = (deal_order[:, None] == slots[None, :]).astype(jnp.int32)
    seq_len = lax.optimization_barrier(jnp.sum(matches * lengths[:, None], axis=0)).astype(jnp.int32)
    positions = jnp.arange(length, dtype=jnp.int32)
    mask = (positions[None, :] < seq_len[:, None]).astype(jnp.float32)[..., None]
    weights32 = (norm_gain, in_weight, conv_weight, conv_bias, x_weight, dt_weight, dt_bias, decay_log, skip_gain, out_weight)

    def whole_block(inputs32, params):
        return forward(inputs32, params, mask)
    result, pull = jax.vjp(whole_block, tokens.astype(jnp.float32), weights32)
    grad_tokens, grad_weights = pull(cotangent.astype(jnp.float32))
    return (result.astype(jnp.bfloat16), grad_tokens.astype(jnp.bfloat16), grad_weights[0], grad_weights[1], grad_weights[2], grad_weights[3], grad_weights[4], grad_weights[5], grad_weights[6], grad_weights[7], grad_weights[8], grad_weights[9])
```

```python
import functools
import jax
import jax.numpy as jnp
from jax import lax
from jax.experimental import pallas as pl
from jax.experimental.pallas import tpu as pltpu
from jax.sharding import PartitionSpec as P

EPSILON = 1e-05
STEPS = 32
LOG2E = 1.4426950408889634
BOTH = ("dp", "fsdp")
F32 = jnp.float32
BF16 = jnp.bfloat16
VMEM_BYTES = 60 * 1024 * 1024


def dot(a, b, dims=((1,), (0,))):
    return lax.dot_general(a, b, (dims, ((), ())), preferred_element_type=F32)


def sigmoid(v):
    return 1.0 / (1.0 + jnp.exp(-v))


def softplus(v):
    return jnp.maximum(v, 0.0) + jnp.log1p(jnp.exp(-jnp.abs(v)))


def rms_normed(x, gain):
    factor = lax.rsqrt(jnp.mean(x * x, axis=-1, keepdims=True) + EPSILON)
    return (x * factor * gain).astype(BF16)


def front_kernel(
    x_ref, gain_ref, win_ref, cw_ref, cb_ref, xw_ref, inner_ref, gate_ref, inp_ref, proj_ref, pad_ref, *, slots
):
    rows = x_ref.shape[0]
    width = inner_ref.shape[1]
    halo = 3 * slots
    normed = rms_normed(x_ref[...].astype(F32), gain_ref[...])
    both = dot(normed, win_ref[...])
    gate_ref[...] = both[:, width:]
    inner = both[:, :width]
    inner_ref[...] = inner

    @pl.when(pl.program_id(0) == 0)
    def _():
        pad_ref[0:halo, :] = jnp.zeros((halo, width), F32)

    pad_ref[halo : halo + rows, :] = inner
    total = jnp.broadcast_to(cb_ref[...], (rows, width))
    for tap in range(4):
        total = total + cw_ref[tap : tap + 1, :] * pad_ref[tap * slots : tap * slots + rows, :]
    inp = (total * sigmoid(total)).astype(BF16)
    inp_ref[...] = inp
    proj_ref[...] = dot(inp, xw_ref[...])
    pad_ref[0:halo, :] = pad_ref[rows : rows + halo, :]


def mix_kernel(
    dtl_ref, bc_ref, inp_ref, gate_ref, dtw_ref, dtb_ref, rate_ref, skip_ref, ow_ref,
    y_ref, ck_ref, br_ref, h_scr, delta_scr, u_scr, rate_scr, *, slots
):
    rows, width = inp_ref.shape
    steps = rows // slots
    states = rate_ref.shape[0]
    chunk = max(128, 2048 // slots)

    @pl.when(pl.program_id(0) == 0)
    def _():
        h_scr[...] = jnp.zeros_like(h_scr)
        for n in range(states):
            rate_scr[n] = jnp.broadcast_to(rate_ref[n : n + 1, :] * LOG2E, (slots, width))

    ck_ref[0] = h_scr[...]
    delta = softplus(dot(dtl_ref[...], dtw_ref[...], ((1,), (1,))) + dtb_ref[...])
    delta_scr[...] = delta
    u_scr[...] = delta * inp_ref[...].astype(F32)
    for first in range(0, width, chunk):
        lanes = slice(first, first + chunk)

        def step(t, held):
            at = pl.ds(pl.multiple_of(t * slots, slots), slots)
            d = delta_scr[at, lanes]
            u = u_scr[at, lanes]
            bc = bc_ref[at, :]
            y = jnp.zeros_like(d)
            after = []
            for n in range(states):
                h = jnp.exp2(d * rate_scr[n, :, lanes]) * held[n] + u * bc[:, n : n + 1]
                y = y + h * bc[:, states + n : states + n + 1]
                after.append(h)
            y_ref[at, lanes] = y
            return tuple(after)

        held = lax.fori_loop(0, steps, step, tuple(h_scr[n, :, lanes] for n in range(states)))
        for n in range(states):
            h_scr[n, :, lanes] = held[n]
    y = y_ref[...] + skip_ref[...] * inp_ref[...].astype(F32)
    y_ref[...] = y
    gate = gate_ref[...]
    gated = (y * (gate * sigmoid(gate))).astype(BF16)
    br_ref[...] = dot(gated, ow_ref[...]).astype(br_ref.dtype)


def lane_sums(parts):
    lane = lax.broadcasted_iota(jnp.int32, parts[0].shape, 1)
    bit = 1
    while len(parts) > 1:
        low = (lane & bit) == 0
        merged = []
        for j in range(0, len(parts), 2):
            kept = jnp.where(low, parts[j], parts[j + 1])
            moved = jnp.where(low, parts[j + 1], parts[j])
            merged.append(kept + pltpu.roll(moved, bit, 1))
        parts = merged
        bit *= 2
    total = parts[0]
    while bit < total.shape[1]:
        total = total + pltpu.roll(total, bit, 1)
        bit *= 2
    return total


def back_kernel(
    gb_ref, dtl_ref, bc_ref, inp_ref, gate_ref, y_ref, ck_ref, dtw_ref, dtb_ref, rate_ref, skip_ref, ow_ref,
    gis_ref, ggate_ref, gproj_ref, gout_ref, grank_ref, gdec_ref, gskip_ref, gbias_ref,
    lam_scr, dacc_scr, sacc_scr, bacc_scr, rate_scr, delta_scr, u_scr, gy_scr, gu_scr, gd_scr, h_scr, a_scr, gbc_scr, *, slots
):
    rows, width = inp_ref.shape
    steps = rows // slots
    states = rate_ref.shape[0]
    rank = dtl_ref.shape[1]
    chunk = 128
    step_id = pl.program_id(0)

    @pl.when(step_id == 0)
    def _():
        lam_scr[...] = jnp.zeros_like(lam_scr)
        dacc_scr[...] = jnp.zeros_like(dacc_scr)
        sacc_scr[...] = jnp.zeros_like(sacc_scr)
        bacc_scr[...] = jnp.zeros_like(bacc_scr)
        gout_ref[...] = jnp.zeros_like(gout_ref)
        grank_ref[...] = jnp.zeros_like(grank_ref)
        for n in range(states):
            rate_scr[n] = jnp.broadcast_to(rate_ref[n : n + 1, :] * LOG2E, (slots, width))

    gb = gb_ref[...]
    gate = gate_ref[...]
    sig = sigmoid(gate)
    silu = gate * sig
    y = y_ref[...]
    inp = inp_ref[...].astype(F32)
    g_gated = dot(gb, ow_ref[...], ((1,), (1,)))
    g_y = g_gated * silu
    gy_scr[...] = g_y
    ggate_ref[...] = (g_gated * y * (sig * (1.0 + gate * (1.0 - sig)))).astype(BF16)
    gout_ref[...] += dot((y * silu).astype(BF16), gb, ((0,), (0,)))
    sacc_scr[...] += jnp.sum((g_y * inp).reshape(steps, slots, width), axis=0)
    z = dot(dtl_ref[...], dtw_ref[...], ((1,), (1,))) + dtb_ref[...]
    delta = softplus(z)
    delta_scr[...] = delta
    u_scr[...] = delta * inp

    for first in range(0, width, chunk):
        lanes = slice(first, first + chunk)

        def replay(t, held):
            at = pl.ds(pl.multiple_of(t * slots, slots), slots)
            d = delta_scr[at, lanes]
            u = u_scr[at, lanes]
            gy = gy_scr[at, lanes]
            bc = bc_ref[at, :]
            after = []
            for n in range(states):
                h_scr[t, n] = held[n]
                a = jnp.exp2(d * rate_scr[n, :, lanes])
                a_scr[t, n] = a
                h = a * held[n] + u * bc[:, n : n + 1]
                part = h * gy
                if first:
                    part = part + gbc_scr[t, states + n]
                gbc_scr[t, states + n] = part
                after.append(h)
            return tuple(after)

        lax.fori_loop(0, steps, replay, tuple(ck_ref[0, n, :, lanes] for n in range(states)))

        def reverse(k, held):
            lams, sums = held
            t = steps - 1 - k
            at = pl.ds(pl.multiple_of(t * slots, slots), slots)
            d = delta_scr[at, lanes]
            u = u_scr[at, lanes]
            gy = gy_scr[at, lanes]
            bc = bc_ref[at, :]
            gu = jnp.zeros_like(d)
            gd = jnp.zeros_like(d)
            lams_after, sums_after = [], []
            for n in range(states):
                lam = lams[n] + gy * bc[:, states + n : states + n + 1]
                gu = gu + lam * bc[:, n : n + 1]
                part = lam * u
                if first:
                    part = part + gbc_scr[t, n]
                gbc_scr[t, n] = part
                carried = a_scr[t, n] * lam
                q = carried * h_scr[t, n]
                gd = gd + q * rate_scr[n, :, lanes]
                sums_after.append(sums[n] + q * d)
                lams_after.append(carried)
            gu_scr[at, lanes] = gu
            gd_scr[at, lanes] = gd
            return tuple(lams_after), tuple(sums_after)

        lams, sums = lax.fori_loop(
            0,
            steps,
            reverse,
            (
                tuple(lam_scr[n, :, lanes] for n in range(states)),
                tuple(dacc_scr[n, :, lanes] for n in range(states)),
            ),
        )
        for n in range(states):
            lam_scr[n, :, lanes] = lams[n]
            dacc_scr[n, :, lanes] = sums[n]

    def reduce_lanes(t, carry):
        at = pl.ds(pl.multiple_of(t * slots, slots), slots)
        total = lane_sums([gbc_scr[t, k] for k in range(2 * states)])
        gproj_ref[at, rank:] = total[:, : 2 * states]
        return carry

    lax.fori_loop(0, steps, reduce_lanes, 0)
    gu = gu_scr[...]
    gis_ref[...] = gu * delta_scr[...] + skip_ref[...] * gy_scr[...]
    g_pre = (gd_scr[...] * (1.0 / LOG2E) + gu * inp) * sigmoid(z)
    bacc_scr[...] += jnp.sum(g_pre.reshape(steps, slots, width), axis=0)
    g_low = g_pre.astype(BF16)
    grank_ref[...] += dot(g_low, dtl_ref[...], ((0,), (0,)))
    gproj_ref[:, :rank] = dot(g_low, dtw_ref[...])

    @pl.when(step_id == pl.num_programs(0) - 1)
    def _():
        for n in range(states):
            gdec_ref[n : n + 1, :] = jnp.sum(dacc_scr[n], axis=0, keepdims=True) * rate_ref[n : n + 1, :]
        gskip_ref[...] = jnp.sum(sacc_scr[...], axis=0, keepdims=True)
        gbias_ref[...] = jnp.sum(bacc_scr[...], axis=0, keepdims=True)


def tail_kernel(
    gproj_ref, inp_ref, gis_ref, ggate_ref, inner_ref, before_ref, x_ref, gain_ref, win_ref, xw_ref, cw_ref, cb_ref,
    gnorm_ref, gin_ref, gsel_ref, gcw_ref, gcb_ref, pad_scr, gpad_scr, wacc_scr, cacc_scr, *, slots
):
    rows, width = inp_ref.shape
    steps = rows // slots
    halo = 3 * slots
    step_id = pl.program_id(0)
    last = pl.num_programs(0) - 1

    @pl.when(step_id == 0)
    def _():
        gpad_scr[rows : rows + halo, :] = jnp.zeros((halo, width), F32)
        wacc_scr[...] = jnp.zeros_like(wacc_scr)
        cacc_scr[...] = jnp.zeros_like(cacc_scr)
        gin_ref[...] = jnp.zeros_like(gin_ref)
        gsel_ref[...] = jnp.zeros_like(gsel_ref)

    gproj = gproj_ref[...]
    gsel_ref[...] += dot(inp_ref[...], gproj, ((0,), (0,)))
    g_inputs = gis_ref[...] + dot(gproj, xw_ref[...], ((1,), (1,)))
    first = (step_id < last).astype(F32)
    pad_scr[0:halo, :] = before_ref[slots : slots + halo, :] * first
    pad_scr[halo : halo + rows, :] = inner_ref[...]
    total = jnp.broadcast_to(cb_ref[...], (rows, width))
    for tap in range(4):
        total = total + cw_ref[tap : tap + 1, :] * pad_scr[tap * slots : tap * slots + rows, :]
    sig = sigmoid(total)
    g_conv = g_inputs * (sig * (1.0 + total * (1.0 - sig)))
    gpad_scr[0:rows, :] = g_conv
    g_inner = jnp.zeros((rows, width), F32)
    for tap in range(4):
        back = (3 - tap) * slots
        g_inner = g_inner + cw_ref[tap : tap + 1, :] * gpad_scr[back : back + rows, :]
        wacc_scr[tap] += jnp.sum(
            (g_conv * pad_scr[tap * slots : tap * slots + rows, :]).reshape(steps, slots, width), axis=0
        )
    cacc_scr[...] += jnp.sum(g_conv.reshape(steps, slots, width), axis=0)
    gpad_scr[rows : rows + halo, :] = gpad_scr[0:halo, :]
    g_both = jnp.concatenate([g_inner.astype(BF16), ggate_ref[...]], axis=1)
    normed = rms_normed(x_ref[...].astype(F32), gain_ref[...])
    gin_ref[...] += dot(normed, g_both, ((0,), (0,)))
    gnorm_ref[...] = dot(g_both, win_ref[...], ((1,), (1,))).astype(gnorm_ref.dtype)

    @pl.when(step_id == last)
    def _():
        for tap in range(4):
            gcw_ref[tap : tap + 1, :] = jnp.sum(wacc_scr[tap], axis=0, keepdims=True)
        gcb_ref[...] = jnp.sum(cacc_scr[...], axis=0, keepdims=True)


def whole(shape):
    return pl.BlockSpec(shape, lambda i: (0,) * len(shape))


def params():
    return pltpu.CompilerParams(vmem_limit_bytes=VMEM_BYTES, dimension_semantics=("arbitrary",))


def body(
    tokens, cotangent, lengths, deal_order, norm_gain, in_weight, conv_weight, conv_bias,
    x_weight, dt_weight, dt_bias, decay_log, skip_gain, out_weight, *, n_dp, n_f
):
    seqs, own, model = tokens.shape
    slots = seqs // n_dp
    inner_rows, states = decay_log.shape
    rank = dt_weight.shape[1]
    proj_cols = x_weight.shape[1]
    width = inner_rows * n_dp
    length = own * n_dp * n_f
    d_rows = in_weight.shape[0]
    total_rows = length * slots
    group = lax.axis_index("dp")
    member = lax.axis_index("fsdp")

    low = lambda v: v.astype(BF16)
    slot_ids = jnp.arange(seqs, dtype=jnp.int32)
    seq_len = jnp.sum(jnp.where(deal_order[:, None] == slot_ids[None, :], lengths[:, None], 0), axis=0)
    own_pos = (group * n_f + member) * own + jnp.arange(own, dtype=jnp.int32)
    own_mask = own_pos[None, :] < seq_len[:, None]

    def spread(v):
        v = v.reshape(n_dp, slots, own, model).transpose(0, 2, 1, 3)
        v = lax.all_to_all(v, "dp", 0, 0, tiled=True)
        v = lax.all_gather(v, "fsdp", axis=0, tiled=False)
        return v.transpose(1, 0, 2, 3, 4).reshape(total_rows, model)

    def collect(v):
        v = v.reshape(n_dp, n_f, own, slots, model).transpose(1, 0, 2, 3, 4)
        v = lax.psum_scatter(v.reshape(total_rows, model), "fsdp", scatter_dimension=0, tiled=True)
        v = lax.all_to_all(v.reshape(n_dp, own, slots, model), "dp", 0, 0, tiled=True)
        return v.transpose(0, 2, 1, 3).reshape(seqs, own, model)

    x = spread(tokens)
    g_branch = spread(jnp.where(own_mask[:, :, None], cotangent, jnp.zeros_like(cotangent)))

    win = low(in_weight).reshape(d_rows, 2, n_dp, n_f, inner_rows).transpose(3, 0, 1, 2, 4)
    win = lax.all_to_all(win.reshape(n_f, d_rows, 2 * width), "fsdp", 0, 0, tiled=True)
    win = lax.all_gather(win.reshape(n_f * d_rows, 2 * width), "dp", axis=0, tiled=True)
    gain = lax.all_gather(low(norm_gain), BOTH, axis=0, tiled=True).astype(F32)[None, :]
    packed = jnp.concatenate(
        [
            low(v)
            for v in (
                out_weight, x_weight, dt_weight, decay_log, conv_weight,
                conv_bias[:, None], dt_bias[:, None], skip_gain[:, None],
            )
        ],
        axis=1,
    )
    packed = lax.all_gather(packed, "dp", axis=0, tiled=True)
    cuts = [model, proj_cols, rank, states, 4, 1, 1, 1]
    pieces, start = [], 0
    for cut in cuts:
        pieces.append(packed[:, start : start + cut])
        start += cut
    ow, xw, dtw, decay, cw, cb, dtb, skip = pieces
    rate = -jnp.exp(decay.astype(F32)).T
    cw, cb, dtb, skip = (v.astype(F32).T for v in (cw, cb, dtb, skip))

    rows = STEPS * slots
    blocks = length // STEPS
    grid = (blocks,)
    row_spec = lambda cols: pl.BlockSpec((rows, cols), lambda i: (i, 0))
    rev_spec = lambda cols: pl.BlockSpec((rows, cols), lambda i: (blocks - 1 - i, 0))
    like = jax.ShapeDtypeStruct

    inner, gate, inp, proj = pl.pallas_call(
        functools.partial(front_kernel, slots=slots),
        grid=grid,
        in_specs=[
            row_spec(model), whole((1, model)), whole((model, 2 * width)), whole((4, width)), whole((1, width)),
            whole((width, proj_cols)),
        ],
        out_specs=[row_spec(width), row_spec(width), row_spec(width), row_spec(proj_cols)],
        out_shape=[
            like((total_rows, width), F32), like((total_rows, width), F32), like((total_rows, width), BF16),
            like((total_rows, proj_cols), F32),
        ],
        scratch_shapes=[pltpu.VMEM((rows + 3 * slots, width), F32)],
        compiler_params=params(),
        name="front",
    )(x, gain, win, cw, cb, xw)

    proj = lax.psum(proj, "fsdp")
    dtl = low(proj[:, :rank])
    bc = proj[:, rank:]

    y, ck, branch = pl.pallas_call(
        functools.partial(mix_kernel, slots=slots),
        grid=grid,
        in_specs=[
            row_spec(rank), row_spec(2 * states), row_spec(width), row_spec(width), whole((width, rank)),
            whole((1, width)), whole((states, width)), whole((1, width)), whole((width, model)),
        ],
        out_specs=[
            row_spec(width), pl.BlockSpec((1, states, slots, width), lambda i: (i, 0, 0, 0)), row_spec(model),
        ],
        out_shape=[
            like((total_rows, width), F32), like((blocks, states, slots, width), F32), like((total_rows, model), BF16),
        ],
        scratch_shapes=[
            pltpu.VMEM((states, slots, width), F32), pltpu.VMEM((rows, width), F32), pltpu.VMEM((rows, width), F32),
            pltpu.VMEM((states, slots, width), F32),
        ],
        compiler_params=params(),
        name="mix",
    )(dtl, bc, inp, gate, dtw, dtb, rate, skip, ow)

    gis, ggate, gproj, gout, grank, gdec, gskip, gbias = pl.pallas_call(
        functools.partial(back_kernel, slots=slots),
        grid=grid,
        in_specs=[
            rev_spec(model), rev_spec(rank), rev_spec(2 * states), rev_spec(width), rev_spec(width), rev_spec(width),
            pl.BlockSpec((1, states, slots, width), lambda i: (blocks - 1 - i, 0, 0, 0)),
            whole((width, rank)), whole((1, width)), whole((states, width)), whole((1, width)), whole((width, model)),
        ],
        out_specs=[
            rev_spec(width), rev_spec(width), rev_spec(proj_cols), whole((width, model)), whole((width, rank)),
            whole((states, width)), whole((1, width)), whole((1, width)),
        ],
        out_shape=[
            like((total_rows, width), F32), like((total_rows, width), BF16), like((total_rows, proj_cols), F32),
            like((width, model), F32), like((width, rank), F32), like((states, width), F32), like((1, width), F32),
            like((1, width), F32),
        ],
        scratch_shapes=[
            pltpu.VMEM((states, slots, width), F32), pltpu.VMEM((states, slots, width), F32),
            pltpu.VMEM((slots, width), F32), pltpu.VMEM((slots, width), F32), pltpu.VMEM((states, slots, width), F32),
        ]
        + [pltpu.VMEM((rows, width), F32)] * 5
        + [
            pltpu.VMEM((STEPS, states, slots, 128), F32), pltpu.VMEM((STEPS, states, slots, 128), F32),
            pltpu.VMEM((STEPS, 2 * states, slots, 128), F32),
        ],
        compiler_params=params(),
        name="back",
    )(g_branch, dtl, bc, inp, gate, y, ck, dtw, dtb, rate, skip, ow)

    gproj = low(lax.psum(gproj, "fsdp"))

    gnorm, gin, gsel, gcw, gcb = pl.pallas_call(
        functools.partial(tail_kernel, slots=slots),
        grid=grid,
        in_specs=[
            rev_spec(proj_cols), rev_spec(width), rev_spec(width), rev_spec(width), rev_spec(width),
            pl.BlockSpec((4 * slots, width), lambda i: (jnp.maximum((blocks - 1 - i) * (STEPS // 4) - 1, 0), 0)),
            rev_spec(model), whole((1, model)), whole((model, 2 * width)), whole((width, proj_cols)), whole((4, width)),
            whole((1, width)),
        ],
        out_specs=[
            rev_spec(model), whole((model, 2 * width)), whole((width, proj_cols)), whole((4, width)), whole((1, width)),
        ],
        out_shape=[
            like((total_rows, model), BF16), like((model, 2 * width), F32), like((width, proj_cols), F32),
            like((4, width), F32), like((1, width), F32),
        ],
        scratch_shapes=[
            pltpu.VMEM((rows + 3 * slots, width), F32), pltpu.VMEM((rows + 3 * slots, width), F32),
            pltpu.VMEM((4, slots, width), F32), pltpu.VMEM((slots, width), F32),
        ],
        compiler_params=params(),
        name="tail",
    )(gproj, inp, gis, ggate, inner, inner, x, gain, win, xw, cw, cb)

    hidden = tokens.astype(F32)
    upstream = cotangent.astype(F32)
    output = (hidden + jnp.where(own_mask[:, :, None], collect(branch).astype(F32), 0.0)).astype(BF16)
    g_normed = collect(gnorm).astype(F32)
    factor = lax.rsqrt(jnp.mean(hidden * hidden, axis=-1, keepdims=True) + EPSILON)
    weighted = gain * g_normed
    input_grad = (
        upstream + factor * weighted - hidden * factor**3 * jnp.mean(hidden * weighted, axis=-1, keepdims=True)
    ).astype(BF16)
    gain_grad = lax.psum_scatter(
        jnp.sum(g_normed * hidden * factor, axis=(0, 1)), BOTH, scatter_dimension=0, tiled=True
    )

    gin = lax.psum_scatter(low(gin), "dp", scatter_dimension=0, tiled=True)
    gin = lax.all_to_all(gin.reshape(n_f, d_rows, 2 * width), "fsdp", 0, 0, tiled=True)
    gin = gin.reshape(n_f, d_rows, 2, n_dp, inner_rows).transpose(1, 2, 3, 0, 4).reshape(d_rows, -1).astype(F32)
    small = jnp.concatenate([gsel, grank, gdec.T, gcw.T, gcb.T, gbias.T, gskip.T], axis=1)
    small = lax.psum_scatter(jnp.concatenate([low(gout), low(small)], axis=1), "dp", scatter_dimension=0, tiled=True)
    small = small.astype(F32)
    cuts = [model, proj_cols, rank, states, 4, 1, 1, 1]
    pieces, start = [], 0
    for cut in cuts:
        pieces.append(small[:, start : start + cut])
        start += cut
    gout, gsel, grank, gdec, gcw, gcb, gbias, gskip = pieces
    return (
        output, input_grad, gain_grad, gin, gcw, gcb[:, 0], gsel, grank, gbias[:, 0], gdec, gskip[:, 0], gout,
    )


def solution(mesh):
    rows1, rows2, pos = P(BOTH), P(BOTH, None), P(None, BOTH, None)
    return jax.shard_map(
        functools.partial(body, n_dp=mesh.shape["dp"], n_f=mesh.shape["fsdp"]),
        mesh=mesh,
        in_specs=(pos, pos, P(), P(), rows1, rows2, rows2, rows1, rows2, rows2, rows1, rows2, rows1, rows2),
        out_specs=(pos, pos, rows1, rows2, rows2, rows1, rows2, rows2, rows1, rows2, rows1, rows2),
        check_vma=False,
    )
```

```python
import functools
import jax
import jax.numpy as jnp
from jax import lax
from jax.experimental import pallas as pl
from jax.experimental.pallas import tpu as pltpu
from jax.sharding import PartitionSpec as P

EPSILON = 1e-05
STEPS = 32
PAIR = 2
TOGETHER = 8
LOG2E = 1.4426950408889634
BOTH = ("dp", "fsdp")
F32 = jnp.float32
BF16 = jnp.bfloat16
VMEM_BYTES = 60 * 1024 * 1024


def dot(a, b, dims=((1,), (0,))):
    return lax.dot_general(a, b, (dims, ((), ())), preferred_element_type=F32)


def sigmoid(v):
    return 1.0 / (1.0 + jnp.exp(-v))


def softplus(v):
    return jnp.maximum(v, 0.0) + jnp.log1p(jnp.exp(-jnp.abs(v)))


def rms_normed(x, gain):
    factor = lax.rsqrt(jnp.mean(x * x, axis=-1, keepdims=True) + EPSILON)
    return (x * factor * gain).astype(BF16)


def front_kernel(
    x_ref, gain_ref, win_ref, cw_ref, cb_ref, xw_ref, inner_ref, gate_ref, inp_ref, proj_ref, pad_ref, *, slots
):
    rows = x_ref.shape[0]
    width = inner_ref.shape[1]
    halo = 3 * slots
    normed = rms_normed(x_ref[...].astype(F32), gain_ref[...])
    both = dot(normed, win_ref[...])
    gate_ref[...] = both[:, width:]
    inner = both[:, :width]
    inner_ref[...] = inner

    @pl.when(pl.program_id(0) == 0)
    def _():
        pad_ref[0:halo, :] = jnp.zeros((halo, width), F32)

    pad_ref[halo : halo + rows, :] = inner
    total = jnp.broadcast_to(cb_ref[...], (rows, width))
    for tap in range(4):
        total = total + cw_ref[tap : tap + 1, :] * pad_ref[tap * slots : tap * slots + rows, :]
    inp = (total * sigmoid(total)).astype(BF16)
    inp_ref[...] = inp
    proj_ref[...] = dot(inp, xw_ref[...])
    pad_ref[0:halo, :] = pad_ref[rows : rows + halo, :]


def spread_lanes(bc_ref, bcb_scr, slots):
    steps, count = bcb_scr.shape[0], bcb_scr.shape[1]
    together = TOGETHER

    def some(k, carry):
        for n in range(count):
            for j in range(together):
                t = k * together + j
                at = pl.ds(pl.multiple_of(t * slots, slots), slots)
                bcb_scr[t, n] = jnp.broadcast_to(bc_ref[at, n : n + 1], (slots, 128))
        return carry

    lax.fori_loop(0, steps // together, some, 0)


def widen(piece, width):
    return jnp.concatenate([piece] * (width // 128), axis=1)


def narrow(value):
    total = value[:, :128]
    for first in range(128, value.shape[1], 128):
        total = total + value[:, first : first + 128]
    return total


def mix_kernel(
    dtl_ref, bc_ref, inp_ref, gate_ref, dtw_ref, dtb_ref, rate_ref, skip_ref, ow_ref,
    y_ref, ck_ref, br_ref, h_scr, delta_scr, u_scr, rate_scr, bcb_scr, *, slots
):
    rows, width = inp_ref.shape
    steps = rows // slots
    states = rate_ref.shape[0]

    @pl.when(pl.program_id(0) == 0)
    def _():
        h_scr[...] = jnp.zeros_like(h_scr)
        for n in range(states):
            rate_scr[n] = jnp.broadcast_to(rate_ref[n : n + 1, :] * LOG2E, (slots, width))

    ck_ref[0] = h_scr[...]
    delta = softplus(dot(dtl_ref[...], dtw_ref[...], ((1,), (1,))) + dtb_ref[...])
    delta_scr[...] = delta
    u_scr[...] = delta * inp_ref[...].astype(F32)
    spread_lanes(bc_ref, bcb_scr, slots)

    def step(k, carry):
        ats, ds, us, ys = [], [], [], []
        for j in range(PAIR):
            at = pl.ds(pl.multiple_of((k * PAIR + j) * slots, slots), slots)
            ats.append(at)
            ds.append(delta_scr[at, :])
            us.append(u_scr[at, :])
            ys.append(None)
        for n in range(states):
            rate = rate_scr[n]
            h = h_scr[n]
            for j in range(PAIR):
                t = k * PAIR + j
                h = jnp.exp2(ds[j] * rate) * h + us[j] * widen(bcb_scr[t, n], width)
                term = h * widen(bcb_scr[t, states + n], width)
                ys[j] = term if n == 0 else ys[j] + term
            h_scr[n] = h
        for j in range(PAIR):
            y_ref[ats[j], :] = ys[j]
        return carry

    lax.fori_loop(0, steps // PAIR, step, 0)
    y = y_ref[...] + skip_ref[...] * inp_ref[...].astype(F32)
    y_ref[...] = y
    gate = gate_ref[...]
    gated = (y * (gate * sigmoid(gate))).astype(BF16)
    br_ref[...] = dot(gated, ow_ref[...]).astype(br_ref.dtype).reshape(br_ref.shape)


def lane_sums(parts):
    lane = lax.broadcasted_iota(jnp.int32, parts[0].shape, 1)
    bit = 1
    while len(parts) > 1:
        low = (lane & bit) == 0
        merged = []
        for j in range(0, len(parts), 2):
            kept = jnp.where(low, parts[j], parts[j + 1])
            moved = jnp.where(low, parts[j + 1], parts[j])
            merged.append(kept + pltpu.roll(moved, bit, 1))
        parts = merged
        bit *= 2
    total = parts[0]
    while bit < total.shape[1]:
        total = total + pltpu.roll(total, bit, 1)
        bit *= 2
    return total


def back_kernel(
    gb_ref, dtl_ref, bc_ref, inp_ref, gate_ref, y_ref, ck_ref, dtw_ref, dtb_ref, rate_ref, skip_ref, ow_ref,
    gis_ref, ggate_ref, gproj_ref, gout_ref, grank_ref, gdec_ref, gskip_ref, gbias_ref,
    lam_scr, dacc_scr, sacc_scr, bacc_scr, rate_scr, delta_scr, u_scr, gy_scr, gu_scr, gd_scr, h_scr, a_scr, gbc_scr, bcb_scr, h_now, *, slots
):
    rows, width = inp_ref.shape
    steps = rows // slots
    states = rate_ref.shape[0]
    rank = dtl_ref.shape[1]
    step_id = pl.program_id(0)

    @pl.when(step_id == 0)
    def _():
        lam_scr[...] = jnp.zeros_like(lam_scr)
        dacc_scr[...] = jnp.zeros_like(dacc_scr)
        sacc_scr[...] = jnp.zeros_like(sacc_scr)
        bacc_scr[...] = jnp.zeros_like(bacc_scr)
        gout_ref[...] = jnp.zeros_like(gout_ref)
        grank_ref[...] = jnp.zeros_like(grank_ref)
        for n in range(states):
            rate_scr[n] = jnp.broadcast_to(rate_ref[n : n + 1, :] * LOG2E, (slots, width))

    gb = gb_ref[...]
    gate = gate_ref[...]
    sig = sigmoid(gate)
    silu = gate * sig
    y = y_ref[...]
    inp = inp_ref[...].astype(F32)
    g_gated = dot(gb, ow_ref[...], ((1,), (1,)))
    g_y = g_gated * silu
    gy_scr[...] = g_y
    ggate_ref[...] = (g_gated * y * (sig * (1.0 + gate * (1.0 - sig)))).astype(BF16)
    gout_ref[...] += dot((y * silu).astype(BF16), gb, ((0,), (0,)))
    sacc_scr[...] += jnp.sum((g_y * inp).reshape(steps, slots, width), axis=0)
    z = dot(dtl_ref[...], dtw_ref[...], ((1,), (1,))) + dtb_ref[...]
    delta = softplus(z)
    delta_scr[...] = delta
    u_scr[...] = delta * inp

    spread_lanes(bc_ref, bcb_scr, slots)
    h_now[...] = ck_ref[0]

    def replay(k, carry):
        ds, us, gys = [], [], []
        for j in range(PAIR):
            at = pl.ds(pl.multiple_of((k * PAIR + j) * slots, slots), slots)
            ds.append(delta_scr[at, :])
            us.append(u_scr[at, :])
            gys.append(gy_scr[at, :])
        for n in range(states):
            rate = rate_scr[n]
            h = h_now[n]
            for j in range(PAIR):
                t = k * PAIR + j
                h_scr[t, n] = h
                decay = jnp.exp2(ds[j] * rate)
                a_scr[t, n] = decay
                h = decay * h + us[j] * widen(bcb_scr[t, n], width)
                gbc_scr[t, states + n] = narrow(h * gys[j])
            h_now[n] = h
        return carry

    lax.fori_loop(0, steps // PAIR, replay, 0)

    def reverse(k, carry):
        ats, ds, us, gys, gus, gds, ts = [], [], [], [], [], [], []
        for j in range(PAIR):
            t = steps - 1 - (k * PAIR + j)
            at = pl.ds(pl.multiple_of(t * slots, slots), slots)
            ts.append(t)
            ats.append(at)
            ds.append(delta_scr[at, :])
            us.append(u_scr[at, :])
            gys.append(gy_scr[at, :])
            gus.append(None)
            gds.append(None)
        for n in range(states):
            rate = rate_scr[n]
            carried = lam_scr[n]
            total = dacc_scr[n]
            for j in range(PAIR):
                t = ts[j]
                lam = carried + gys[j] * widen(bcb_scr[t, states + n], width)
                term = lam * widen(bcb_scr[t, n], width)
                gus[j] = term if n == 0 else gus[j] + term
                gbc_scr[t, n] = narrow(lam * us[j])
                carried = a_scr[t, n] * lam
                q = carried * h_scr[t, n]
                term = q * rate
                gds[j] = term if n == 0 else gds[j] + term
                total = total + q * ds[j]
            lam_scr[n] = carried
            dacc_scr[n] = total
        for j in range(PAIR):
            gu_scr[ats[j], :] = gus[j]
            gd_scr[ats[j], :] = gds[j]
        return carry

    lax.fori_loop(0, steps // PAIR, reverse, 0)

    def reduce_lanes(k, carry):
        for j in range(TOGETHER):
            t = k * TOGETHER + j
            at = pl.ds(pl.multiple_of(t * slots, slots), slots)
            total = lane_sums([gbc_scr[t, n] for n in range(2 * states)])
            gproj_ref[at, rank:] = total[:, : 2 * states]
        return carry

    lax.fori_loop(0, steps // TOGETHER, reduce_lanes, 0)
    gu = gu_scr[...]
    gis_ref[...] = gu * delta_scr[...] + skip_ref[...] * gy_scr[...]
    g_pre = (gd_scr[...] * (1.0 / LOG2E) + gu * inp) * sigmoid(z)
    bacc_scr[...] += jnp.sum(g_pre.reshape(steps, slots, width), axis=0)
    g_low = g_pre.astype(BF16)
    grank_ref[...] += dot(g_low, dtl_ref[...], ((0,), (0,)))
    gproj_ref[:, :rank] = dot(g_low, dtw_ref[...])

    @pl.when(step_id == pl.num_programs(0) - 1)
    def _():
        for n in range(states):
            gdec_ref[n : n + 1, :] = jnp.sum(dacc_scr[n], axis=0, keepdims=True) * rate_ref[n : n + 1, :]
        gskip_ref[...] = jnp.sum(sacc_scr[...], axis=0, keepdims=True)
        gbias_ref[...] = jnp.sum(bacc_scr[...], axis=0, keepdims=True)


def tail_kernel(
    gproj_ref, inp_ref, gis_ref, ggate_ref, inner_ref, before_ref, x_ref, gain_ref, win_ref, xw_ref, cw_ref, cb_ref,
    gnorm_ref, gin_ref, gsel_ref, gcw_ref, gcb_ref, pad_scr, gpad_scr, wacc_scr, cacc_scr, *, slots
):
    rows, width = inp_ref.shape
    steps = rows // slots
    halo = 3 * slots
    step_id = pl.program_id(0)
    last = pl.num_programs(0) - 1

    @pl.when(step_id == 0)
    def _():
        gpad_scr[rows : rows + halo, :] = jnp.zeros((halo, width), F32)
        wacc_scr[...] = jnp.zeros_like(wacc_scr)
        cacc_scr[...] = jnp.zeros_like(cacc_scr)
        gin_ref[...] = jnp.zeros_like(gin_ref)
        gsel_ref[...] = jnp.zeros_like(gsel_ref)

    gproj = gproj_ref[...]
    gsel_ref[...] += dot(inp_ref[...], gproj, ((0,), (0,)))
    g_inputs = gis_ref[...] + dot(gproj, xw_ref[...], ((1,), (1,)))
    first = (step_id < last).astype(F32)
    pad_scr[0:halo, :] = before_ref[slots : slots + halo, :] * first
    pad_scr[halo : halo + rows, :] = inner_ref[...]
    total = jnp.broadcast_to(cb_ref[...], (rows, width))
    for tap in range(4):
        total = total + cw_ref[tap : tap + 1, :] * pad_scr[tap * slots : tap * slots + rows, :]
    sig = sigmoid(total)
    g_conv = g_inputs * (sig * (1.0 + total * (1.0 - sig)))
    gpad_scr[0:rows, :] = g_conv
    g_inner = jnp.zeros((rows, width), F32)
    for tap in range(4):
        back = (3 - tap) * slots
        g_inner = g_inner + cw_ref[tap : tap + 1, :] * gpad_scr[back : back + rows, :]
        wacc_scr[tap] += jnp.sum(
            (g_conv * pad_scr[tap * slots : tap * slots + rows, :]).reshape(steps, slots, width), axis=0
        )
    cacc_scr[...] += jnp.sum(g_conv.reshape(steps, slots, width), axis=0)
    gpad_scr[rows : rows + halo, :] = gpad_scr[0:halo, :]
    g_both = jnp.concatenate([g_inner.astype(BF16), ggate_ref[...]], axis=1)
    normed = rms_normed(x_ref[...].astype(F32), gain_ref[...])
    gin_ref[...] += dot(normed, g_both, ((0,), (0,)))
    gnorm_ref[...] = dot(g_both, win_ref[...], ((1,), (1,))).astype(gnorm_ref.dtype).reshape(gnorm_ref.shape)

    @pl.when(step_id == last)
    def _():
        for tap in range(4):
            gcw_ref[tap : tap + 1, :] = jnp.sum(wacc_scr[tap], axis=0, keepdims=True)
        gcb_ref[...] = jnp.sum(cacc_scr[...], axis=0, keepdims=True)


def remote(src, dst, send, recv, where):
    return pltpu.make_async_remote_copy(
        src_ref=src, dst_ref=dst, send_sem=send, recv_sem=recv, device_id=where, device_id_type=pl.DeviceIdType.MESH
    )


def gather_kernel(
    tok_ref, win_ref, gain_ref, pk_ref, x_ref, w_ref, g_ref, p_ref,
    tok_buf, win_buf, gain_buf, pk_buf, local_sem,
    tdp_send, tdp_recv, up_send, up_recv, down_send, down_recv, core_send, core_recv,
    w1_send, w1_recv, w2_send, w2_recv, g1_send, g1_recv, g2_send, g2_recv, p_send, p_recv, *, n_dp, n_f
):
    d = lax.axis_index("dp")
    f = lax.axis_index("fsdp")
    n_z = n_f // 2
    z = f // 2
    core = f % 2
    partner = z * 2 + (1 - core)

    barrier = pltpu.get_barrier_semaphore()
    for k in range(1, n_f):
        pl.semaphore_signal(barrier, inc=1, device_id=(d, (f + k) % n_f), device_id_type=pl.DeviceIdType.MESH)
    for k in range(1, n_dp):
        pl.semaphore_signal(barrier, inc=1, device_id=((d + k) % n_dp, f), device_id_type=pl.DeviceIdType.MESH)
    pl.semaphore_wait(barrier, n_f + n_dp - 2)

    loads = (
        pltpu.make_async_copy(tok_ref.at[d], tok_buf, local_sem.at[0]),
        pltpu.make_async_copy(win_ref.at[f], win_buf, local_sem.at[1]),
        pltpu.make_async_copy(gain_ref, gain_buf, local_sem.at[2]),
        pltpu.make_async_copy(pk_ref, pk_buf, local_sem.at[3]),
    )
    stores = (
        pltpu.make_async_copy(tok_buf, x_ref.at[d, f], local_sem.at[4]),
        pltpu.make_async_copy(win_buf, w_ref.at[d, f], local_sem.at[5]),
        pltpu.make_async_copy(gain_buf, g_ref.at[d, f], local_sem.at[6]),
        pltpu.make_async_copy(pk_buf, p_ref.at[d], local_sem.at[7]),
    )
    for load in loads:
        load.start()

    def tok_dp(k):
        to = (d + k) % n_dp
        return remote(tok_ref.at[to], x_ref.at[d, f], tdp_send.at[k], tdp_recv.at[k], (to, f))

    def tok_dp_arrival(k):
        src = (d - k + n_dp) % n_dp
        return remote(tok_ref.at[d], x_ref.at[src, f], tdp_send.at[k], tdp_recv.at[k], (src, f))

    def w1(k):
        to = (f + k) % n_f
        return remote(win_ref.at[to], w_ref.at[d, f], w1_send.at[k], w1_recv.at[k], (d, to))

    def w1_arrival(k):
        src = (f - k + n_f) % n_f
        return remote(win_ref.at[f], w_ref.at[d, src], w1_send.at[k], w1_recv.at[k], (d, src))

    def g1(k):
        to = (f + k) % n_f
        return remote(gain_ref, g_ref.at[d, f], g1_send.at[k], g1_recv.at[k], (d, to))

    def g1_arrival(k):
        src = (f - k + n_f) % n_f
        return remote(gain_ref, g_ref.at[d, src], g1_send.at[k], g1_recv.at[k], (d, src))

    def w2(k):
        to = (d + k) % n_dp
        return remote(w_ref.at[d], w_ref.at[d], w2_send.at[k], w2_recv.at[k], (to, f))

    def w2_arrival(k):
        src = (d - k + n_dp) % n_dp
        return remote(w_ref.at[src], w_ref.at[src], w2_send.at[k], w2_recv.at[k], (src, f))

    def g2(k):
        to = (d + k) % n_dp
        return remote(g_ref.at[d], g_ref.at[d], g2_send.at[k], g2_recv.at[k], (to, f))

    def g2_arrival(k):
        src = (d - k + n_dp) % n_dp
        return remote(g_ref.at[src], g_ref.at[src], g2_send.at[k], g2_recv.at[k], (src, f))

    def pk(k):
        to = (d + k) % n_dp
        return remote(pk_ref, p_ref.at[d], p_send.at[k], p_recv.at[k], (to, f))

    def pk_arrival(k):
        src = (d - k + n_dp) % n_dp
        return remote(pk_ref, p_ref.at[src], p_send.at[k], p_recv.at[k], (src, f))

    def block(j, origin, side):
        at = (d - j + n_dp) % n_dp
        return x_ref.at[at, origin * 2 + side]

    def up(j, origin, src=None):
        ref = block(j, origin, core)
        return remote(ref if src is None else src, ref, up_send.at[origin, j], up_recv.at[origin, j], (d, f + 2))

    def down(j, origin, src=None):
        ref = block(j, origin, core)
        return remote(ref if src is None else src, ref, down_send.at[origin, j], down_recv.at[origin, j], (d, f - 2))

    def across(j, origin, src=None):
        ref = block(j, origin, core)
        return remote(
            ref if src is None else src, ref, core_send.at[origin, j], core_recv.at[origin, j], (d, partner)
        )

    def across_arrival(j, origin):
        ref = block(j, origin, 1 - core)
        return remote(ref, ref, core_send.at[origin, j], core_recv.at[origin, j], (d, partner))

    def launch(j, src=None):
        @pl.when(z < n_z - 1)
        def _():
            up(j, z, src).start()

        @pl.when(z > 0)
        def _():
            down(j, z, src).start()

        across(j, z, src).start()

    for k in range(1, n_f):
        w1(k).start()
    for k in range(1, n_dp):
        tok_dp(k).start()
    launch(0, tok_ref.at[d])
    for k in range(1, n_f):
        g1(k).start()
    for k in range(1, n_dp):
        pk(k).start()
    for load, store in zip(loads, stores):
        load.wait()
        store.start()
    for k in range(1, n_dp):
        tok_dp_arrival(k).wait_recv()
        launch(k)
    for store in stores:
        store.wait()
    for k in range(1, n_f):
        w1_arrival(k).wait_recv()
        g1_arrival(k).wait_recv()
    for k in range(1, n_dp):
        w2(k).start()
        g2(k).start()
    for far in range(1, n_z):
        for j in range(n_dp):

            @pl.when(z >= far)
            def _():
                origin = z - far
                up(j, origin).wait_recv()

                @pl.when(z < n_z - 1)
                def _():
                    up(j, origin).start()

                across(j, origin).start()

            @pl.when(z + far < n_z)
            def _():
                origin = z + far
                down(j, origin).wait_recv()

                @pl.when(z > 0)
                def _():
                    down(j, origin).start()

                across(j, origin).start()

    for origin in range(n_z):
        for j in range(n_dp):
            across_arrival(j, origin).wait_recv()
            across(j, origin).wait_send()
    for origin in range(n_z):
        for j in range(n_dp):

            @pl.when((origin <= z) & (z < n_z - 1))
            def _():
                up(j, origin).wait_send()

            @pl.when((origin >= z) & (z > 0))
            def _():
                down(j, origin).wait_send()

    for k in range(1, n_dp):
        pk_arrival(k).wait_recv()
        w2_arrival(k).wait_recv()
        g2_arrival(k).wait_recv()
        tok_dp(k).wait_send()
        w2(k).wait_send()
        g2(k).wait_send()
        pk(k).wait_send()
    for k in range(1, n_f):
        w1(k).wait_send()
        g1(k).wait_send()


def whole(shape):
    return pl.BlockSpec(shape, lambda i: (0,) * len(shape))


def params():
    return pltpu.CompilerParams(vmem_limit_bytes=VMEM_BYTES, dimension_semantics=("arbitrary",))


def body(
    tokens, cotangent, lengths, deal_order, norm_gain, in_weight, conv_weight, conv_bias,
    x_weight, dt_weight, dt_bias, decay_log, skip_gain, out_weight, *, n_dp, n_f
):
    seqs, own, model = tokens.shape
    slots = seqs // n_dp
    inner_rows, states = decay_log.shape
    rank = dt_weight.shape[1]
    proj_cols = x_weight.shape[1]
    width = inner_rows * n_dp
    length = own * n_dp * n_f
    d_rows = in_weight.shape[0]
    total_rows = length * slots
    group = lax.axis_index("dp")
    member = lax.axis_index("fsdp")

    low = lambda v: v.astype(BF16)
    slot_ids = jnp.arange(seqs, dtype=jnp.int32)
    seq_len = jnp.sum(jnp.where(deal_order[:, None] == slot_ids[None, :], lengths[:, None], 0), axis=0)
    own_pos = (group * n_f + member) * own + jnp.arange(own, dtype=jnp.int32)
    own_mask = own_pos[None, :] < seq_len[:, None]

    def spread(v):
        v = v.reshape(n_dp, slots, own, model).transpose(0, 2, 1, 3)
        v = lax.all_to_all(v, "dp", 0, 0, tiled=True)
        v = lax.all_gather(v, "fsdp", axis=0, tiled=False)
        return v.transpose(1, 0, 2, 3, 4).reshape(total_rows, model)

    def collect(v):
        v = lax.psum_scatter(v.reshape(total_rows, model), "fsdp", scatter_dimension=0, tiled=True)
        v = lax.all_to_all(v.reshape(n_dp, own, slots, model), "dp", 0, 0, tiled=True)
        return v.transpose(0, 2, 1, 3).reshape(seqs, own, model)

    g_branch = spread(jnp.where(own_mask[:, :, None], cotangent, jnp.zeros_like(cotangent)))

    tok = tokens.reshape(n_dp, slots, own, model).transpose(0, 2, 1, 3).reshape(n_dp, own * slots, model)
    win = low(in_weight).reshape(d_rows, 2, n_dp, n_f, inner_rows).transpose(3, 0, 1, 2, 4)
    win = win.reshape(n_f, d_rows, 2 * width)
    gain_tile = jnp.zeros((8, 128), F32).at[0, :d_rows].set(low(norm_gain).astype(F32))
    packed = jnp.concatenate(
        [
            low(v)
            for v in (
                out_weight, x_weight, dt_weight, decay_log, conv_weight,
                conv_bias[:, None], dt_bias[:, None], skip_gain[:, None],
            )
        ],
        axis=1,
    )
    packed = jnp.pad(packed, ((0, 0), (0, -packed.shape[1] % 128)))
    n_z = n_f // 2
    dma = pltpu.SemaphoreType.DMA
    hbm = pl.BlockSpec(memory_space=pl.ANY)
    x, win, gain, packed = pl.pallas_call(
        functools.partial(gather_kernel, n_dp=n_dp, n_f=n_f),
        in_specs=[hbm] * 4,
        out_specs=[hbm] * 4,
        out_shape=[
            jax.ShapeDtypeStruct((n_dp, n_f) + tok.shape[1:], BF16),
            jax.ShapeDtypeStruct((n_dp, n_f) + win.shape[1:], BF16),
            jax.ShapeDtypeStruct((n_dp, n_f, 8, 128), F32),
            jax.ShapeDtypeStruct((n_dp,) + packed.shape, BF16),
        ],
        scratch_shapes=[
            pltpu.VMEM(tok.shape[1:], BF16), pltpu.VMEM(win.shape[1:], BF16), pltpu.VMEM((8, 128), F32),
            pltpu.VMEM(packed.shape, BF16), dma((8,)), dma((n_dp,)), dma((n_dp,)),
        ]
        + [dma((n_z, n_dp))] * 6
        + [dma((n_f,)), dma((n_f,)), dma((n_dp,)), dma((n_dp,)), dma((n_f,)), dma((n_f,))]
        + [dma((n_dp,))] * 4,
        compiler_params=pltpu.CompilerParams(collective_id=1, has_side_effects=True),
        name="gather",
    )(tok, win, gain_tile, packed)
    x = x.reshape(total_rows, model)
    win = win.reshape(model, 2 * width)
    gain = gain[:, :, 0, :d_rows].reshape(1, model)
    packed = packed.reshape(width, -1)
    cuts = [model, proj_cols, rank, states, 4, 1, 1, 1]
    pieces, start = [], 0
    for cut in cuts:
        pieces.append(packed[:, start : start + cut])
        start += cut
    ow, xw, dtw, decay, cw, cb, dtb, skip = pieces
    rate = -jnp.exp(decay.astype(F32)).T
    cw, cb, dtb, skip = (v.astype(F32).T for v in (cw, cb, dtb, skip))

    rows = STEPS * slots
    blocks = length // STEPS
    grid = (blocks,)
    row_spec = lambda cols: pl.BlockSpec((rows, cols), lambda i: (i, 0))
    rev_spec = lambda cols: pl.BlockSpec((rows, cols), lambda i: (blocks - 1 - i, 0))
    like = jax.ShapeDtypeStruct
    held = STEPS // own
    per = n_f // held
    piece = (held, 1, own * slots, model)
    piece_spec = pl.BlockSpec(piece, lambda i: (i % per, i // per, 0, 0))
    rev_piece_spec = pl.BlockSpec(piece, lambda i: ((blocks - 1 - i) % per, (blocks - 1 - i) // per, 0, 0))
    pieces_shape = like((n_f, n_dp, own * slots, model), BF16)

    inner, gate, inp, proj = pl.pallas_call(
        functools.partial(front_kernel, slots=slots),
        grid=grid,
        in_specs=[
            row_spec(model), whole((1, model)), whole((model, 2 * width)), whole((4, width)), whole((1, width)),
            whole((width, proj_cols)),
        ],
        out_specs=[row_spec(width), row_spec(width), row_spec(width), row_spec(proj_cols)],
        out_shape=[
            like((total_rows, width), F32), like((total_rows, width), F32), like((total_rows, width), BF16),
            like((total_rows, proj_cols), F32),
        ],
        scratch_shapes=[pltpu.VMEM((rows + 3 * slots, width), F32)],
        compiler_params=params(),
        name="front",
    )(x, gain, win, cw, cb, xw)

    proj = lax.psum(proj, "fsdp")
    dtl = low(proj[:, :rank])
    bc = proj[:, rank:]

    y, ck, branch = pl.pallas_call(
        functools.partial(mix_kernel, slots=slots),
        grid=grid,
        in_specs=[
            row_spec(rank), row_spec(2 * states), row_spec(width), row_spec(width), whole((width, rank)),
            whole((1, width)), whole((states, width)), whole((1, width)), whole((width, model)),
        ],
        out_specs=[
            row_spec(width), pl.BlockSpec((1, states, slots, width), lambda i: (i, 0, 0, 0)), piece_spec,
        ],
        out_shape=[
            like((total_rows, width), F32), like((blocks, states, slots, width), F32), pieces_shape,
        ],
        scratch_shapes=[
            pltpu.VMEM((states, slots, width), F32), pltpu.VMEM((rows, width), F32), pltpu.VMEM((rows, width), F32),
            pltpu.VMEM((states, slots, width), F32), pltpu.VMEM((STEPS, 2 * states, slots, 128), F32),
        ],
        compiler_params=params(),
        name="mix",
    )(dtl, bc, inp, gate, dtw, dtb, rate, skip, ow)

    gis, ggate, gproj, gout, grank, gdec, gskip, gbias = pl.pallas_call(
        functools.partial(back_kernel, slots=slots),
        grid=grid,
        in_specs=[
            rev_spec(model), rev_spec(rank), rev_spec(2 * states), rev_spec(width), rev_spec(width), rev_spec(width),
            pl.BlockSpec((1, states, slots, width), lambda i: (blocks - 1 - i, 0, 0, 0)),
            whole((width, rank)), whole((1, width)), whole((states, width)), whole((1, width)), whole((width, model)),
        ],
        out_specs=[
            rev_spec(width), rev_spec(width), rev_spec(proj_cols), whole((width, model)), whole((width, rank)),
            whole((states, width)), whole((1, width)), whole((1, width)),
        ],
        out_shape=[
            like((total_rows, width), F32), like((total_rows, width), BF16), like((total_rows, proj_cols), F32),
            like((width, model), F32), like((width, rank), F32), like((states, width), F32), like((1, width), F32),
            like((1, width), F32),
        ],
        scratch_shapes=[
            pltpu.VMEM((states, slots, width), F32), pltpu.VMEM((states, slots, width), F32),
            pltpu.VMEM((slots, width), F32), pltpu.VMEM((slots, width), F32), pltpu.VMEM((states, slots, width), F32),
        ]
        + [pltpu.VMEM((rows, width), F32)] * 5
        + [
            pltpu.VMEM((STEPS, states, slots, width), F32), pltpu.VMEM((STEPS, states, slots, width), F32),
            pltpu.VMEM((STEPS, 2 * states, slots, 128), F32), pltpu.VMEM((STEPS, 2 * states, slots, 128), F32),
            pltpu.VMEM((states, slots, width), F32),
        ],
        compiler_params=params(),
        name="back",
    )(g_branch, dtl, bc, inp, gate, y, ck, dtw, dtb, rate, skip, ow)

    gproj = low(lax.psum(gproj, "fsdp"))

    gnorm, gin, gsel, gcw, gcb = pl.pallas_call(
        functools.partial(tail_kernel, slots=slots),
        grid=grid,
        in_specs=[
            rev_spec(proj_cols), rev_spec(width), rev_spec(width), rev_spec(width), rev_spec(width),
            pl.BlockSpec((4 * slots, width), lambda i: (jnp.maximum((blocks - 1 - i) * (STEPS // 4) - 1, 0), 0)),
            rev_spec(model), whole((1, model)), whole((model, 2 * width)), whole((width, proj_cols)), whole((4, width)),
            whole((1, width)),
        ],
        out_specs=[
            rev_piece_spec, whole((model, 2 * width)), whole((width, proj_cols)), whole((4, width)), whole((1, width)),
        ],
        out_shape=[
            pieces_shape, like((model, 2 * width), F32), like((width, proj_cols), F32),
            like((4, width), F32), like((1, width), F32),
        ],
        scratch_shapes=[
            pltpu.VMEM((rows + 3 * slots, width), F32), pltpu.VMEM((rows + 3 * slots, width), F32),
            pltpu.VMEM((4, slots, width), F32), pltpu.VMEM((slots, width), F32),
        ],
        compiler_params=params(),
        name="tail",
    )(gproj, inp, gis, ggate, inner, inner, x, gain, win, xw, cw, cb)

    hidden = tokens.astype(F32)
    upstream = cotangent.astype(F32)
    output = (hidden + jnp.where(own_mask[:, :, None], collect(branch).astype(F32), 0.0)).astype(BF16)
    g_normed = collect(gnorm).astype(F32)
    factor = lax.rsqrt(jnp.mean(hidden * hidden, axis=-1, keepdims=True) + EPSILON)
    weighted = gain * g_normed
    input_grad = (
        upstream + factor * weighted - hidden * factor**3 * jnp.mean(hidden * weighted, axis=-1, keepdims=True)
    ).astype(BF16)
    gain_grad = lax.psum_scatter(
        jnp.sum(g_normed * hidden * factor, axis=(0, 1)), BOTH, scatter_dimension=0, tiled=True
    )

    gin = lax.psum_scatter(low(gin), "dp", scatter_dimension=0, tiled=True)
    gin = lax.all_to_all(gin.reshape(n_f, d_rows, 2 * width), "fsdp", 0, 0, tiled=True)
    gin = gin.reshape(n_f, d_rows, 2, n_dp, inner_rows).transpose(1, 2, 3, 0, 4).reshape(d_rows, -1).astype(F32)
    small = jnp.concatenate([gsel, grank, gdec.T, gcw.T, gcb.T, gbias.T, gskip.T], axis=1)
    small = lax.psum_scatter(jnp.concatenate([low(gout), low(small)], axis=1), "dp", scatter_dimension=0, tiled=True)
    small = small.astype(F32)
    cuts = [model, proj_cols, rank, states, 4, 1, 1, 1]
    pieces, start = [], 0
    for cut in cuts:
        pieces.append(small[:, start : start + cut])
        start += cut
    gout, gsel, grank, gdec, gcw, gcb, gbias, gskip = pieces
    return (
        output, input_grad, gain_grad, gin, gcw, gcb[:, 0], gsel, grank, gbias[:, 0], gdec, gskip[:, 0], gout,
    )


def solution(mesh):
    rows1, rows2, pos = P(BOTH), P(BOTH, None), P(None, BOTH, None)
    return jax.shard_map(
        functools.partial(body, n_dp=mesh.shape["dp"], n_f=mesh.shape["fsdp"]),
        mesh=mesh,
        in_specs=(pos, pos, P(), P(), rows1, rows2, rows2, rows1, rows2, rows2, rows1, rows2, rows1, rows2),
        out_specs=(pos, pos, rows1, rows2, rows2, rows1, rows2, rows2, rows1, rows2, rows1, rows2),
        check_vma=False,
    )
```

```python
import functools
import jax
import jax.numpy as jnp
from jax import lax
from jax.experimental import pallas as pl
from jax.experimental.pallas import tpu as pltpu
from jax.sharding import PartitionSpec as P

EPSILON = 1e-05
STEPS = 32
PAIR = 2
TOGETHER = 8
LOG2E = 1.4426950408889634
BOTH = ("dp", "fsdp")
F32 = jnp.float32
BF16 = jnp.bfloat16
VMEM_BYTES = 60 * 1024 * 1024


def dot(a, b, dims=((1,), (0,))):
    return lax.dot_general(a, b, (dims, ((), ())), preferred_element_type=F32)


def sigmoid(v):
    return 1.0 / (1.0 + jnp.exp(-v))


def softplus(v):
    return jnp.maximum(v, 0.0) + jnp.log1p(jnp.exp(-jnp.abs(v)))


def rms_normed(x, gain):
    factor = lax.rsqrt(jnp.mean(x * x, axis=-1, keepdims=True) + EPSILON)
    return (x * factor * gain).astype(BF16)


def front_kernel(
    x_ref, gain_ref, win_ref, cw_ref, cb_ref, xw_ref, inner_ref, gate_ref, inp_ref, proj_ref, pad_ref, *, slots, length
):
    rows = x_ref.shape[0]
    width = inner_ref.shape[1]
    halo = 3 * slots
    normed = rms_normed(x_ref[...].astype(F32), gain_ref[...])
    both = dot(normed, win_ref[...])
    gate_ref[...] = both[:, width:]
    inner = both[:, :width]
    inner_ref[...] = inner

    @pl.when(pl.program_id(0) == 0)
    def _():
        pad_ref[0:halo, :] = jnp.zeros((halo, width), F32)

    pad_ref[halo : halo + rows, :] = inner
    total = jnp.broadcast_to(cb_ref[...], (rows, width))
    for tap in range(4):
        total = total + cw_ref[tap : tap + 1, :] * pad_ref[tap * slots : tap * slots + rows, :]
    inp = (total * sigmoid(total)).astype(BF16)
    inp_ref[...] = inp
    proj = dot(inp, xw_ref[...])
    pack_rows(proj_ref, proj[:, : proj.shape[1] - 32], proj[:, proj.shape[1] - 32 :], length)
    pad_ref[0:halo, :] = pad_ref[rows : rows + halo, :]


def spread_lanes(bc_ref, bcb_scr, slots):
    steps, count = bcb_scr.shape[0], bcb_scr.shape[1]
    together = TOGETHER

    def some(k, carry):
        for n in range(count):
            for j in range(together):
                t = k * together + j
                at = pl.ds(pl.multiple_of(t * slots, slots), slots)
                bcb_scr[t, n] = jnp.broadcast_to(bc_ref[at, n : n + 1], (slots, 128))
        return carry

    lax.fori_loop(0, steps // together, some, 0)


def widen(piece, width):
    return jnp.concatenate([piece] * (width // 128), axis=1)


def narrow(value):
    total = value[:, :128]
    for first in range(128, value.shape[1], 128):
        total = total + value[:, first : first + 128]
    return total


def mix_kernel(
    dtl_ref, bc_ref, inp_ref, gate_ref, dtw_ref, dtb_ref, rate_ref, skip_ref, ow_ref,
    y_ref, ck_ref, br_ref, h_scr, delta_scr, u_scr, rate_scr, bcb_scr, *, slots
):
    rows, width = inp_ref.shape
    steps = rows // slots
    states = rate_ref.shape[0]

    @pl.when(pl.program_id(0) == 0)
    def _():
        h_scr[...] = jnp.zeros_like(h_scr)
        for n in range(states):
            rate_scr[n] = jnp.broadcast_to(rate_ref[n : n + 1, :] * LOG2E, (slots, width))

    ck_ref[0] = h_scr[...]
    delta = softplus(dot(dtl_ref[...], dtw_ref[...], ((1,), (1,))) + dtb_ref[...])
    delta_scr[...] = delta
    u_scr[...] = delta * inp_ref[...].astype(F32)
    spread_lanes(bc_ref, bcb_scr, slots)

    def step(k, carry):
        ats, ds, us, ys = [], [], [], []
        for j in range(PAIR):
            at = pl.ds(pl.multiple_of((k * PAIR + j) * slots, slots), slots)
            ats.append(at)
            ds.append(delta_scr[at, :])
            us.append(u_scr[at, :])
            ys.append(None)
        for n in range(states):
            rate = rate_scr[n]
            h = h_scr[n]
            for j in range(PAIR):
                t = k * PAIR + j
                h = jnp.exp2(ds[j] * rate) * h + us[j] * widen(bcb_scr[t, n], width)
                term = h * widen(bcb_scr[t, states + n], width)
                ys[j] = term if n == 0 else ys[j] + term
            h_scr[n] = h
        for j in range(PAIR):
            y_ref[ats[j], :] = ys[j]
        return carry

    lax.fori_loop(0, steps // PAIR, step, 0)
    y = y_ref[...] + skip_ref[...] * inp_ref[...].astype(F32)
    y_ref[...] = y
    gate = gate_ref[...]
    gated = (y * (gate * sigmoid(gate))).astype(BF16)
    br_ref[...] = dot(gated, ow_ref[...]).astype(br_ref.dtype).reshape(br_ref.shape)


def lane_sums(parts):
    lane = lax.broadcasted_iota(jnp.int32, parts[0].shape, 1)
    bit = 1
    while len(parts) > 1:
        low = (lane & bit) == 0
        merged = []
        for j in range(0, len(parts), 2):
            kept = jnp.where(low, parts[j], parts[j + 1])
            moved = jnp.where(low, parts[j + 1], parts[j])
            merged.append(kept + pltpu.roll(moved, bit, 1))
        parts = merged
        bit *= 2
    total = parts[0]
    while bit < total.shape[1]:
        total = total + pltpu.roll(total, bit, 1)
        bit *= 2
    return total


def back_kernel(
    gb_ref, dtl_ref, bc_ref, inp_ref, gate_ref, y_ref, ck_ref, dtw_ref, dtb_ref, rate_ref, skip_ref, ow_ref,
    gis_ref, ggate_ref, gproj_ref, gout_ref, grank_ref, gdec_ref, gskip_ref, gbias_ref,
    lam_scr, dacc_scr, sacc_scr, bacc_scr, rate_scr, delta_scr, u_scr, gy_scr, gu_scr, gd_scr, h_scr, a_scr, gbc_scr, bcb_scr, h_now, gbc_ref, *, slots, length
):
    rows, width = inp_ref.shape
    steps = rows // slots
    states = rate_ref.shape[0]
    step_id = pl.program_id(0)

    @pl.when(step_id == 0)
    def _():
        lam_scr[...] = jnp.zeros_like(lam_scr)
        dacc_scr[...] = jnp.zeros_like(dacc_scr)
        sacc_scr[...] = jnp.zeros_like(sacc_scr)
        bacc_scr[...] = jnp.zeros_like(bacc_scr)
        gout_ref[...] = jnp.zeros_like(gout_ref)
        grank_ref[...] = jnp.zeros_like(grank_ref)
        for n in range(states):
            rate_scr[n] = jnp.broadcast_to(rate_ref[n : n + 1, :] * LOG2E, (slots, width))

    gb = gb_ref[...].reshape(rows, gb_ref.shape[-1])
    gate = gate_ref[...]
    sig = sigmoid(gate)
    silu = gate * sig
    y = y_ref[...]
    inp = inp_ref[...].astype(F32)
    g_gated = dot(gb, ow_ref[...], ((1,), (1,)))
    g_y = g_gated * silu
    gy_scr[...] = g_y
    ggate_ref[...] = (g_gated * y * (sig * (1.0 + gate * (1.0 - sig)))).astype(BF16)
    gout_ref[...] += dot((y * silu).astype(BF16), gb, ((0,), (0,)))
    sacc_scr[...] += jnp.sum((g_y * inp).reshape(steps, slots, width), axis=0)
    z = dot(dtl_ref[...], dtw_ref[...], ((1,), (1,))) + dtb_ref[...]
    delta = softplus(z)
    delta_scr[...] = delta
    u_scr[...] = delta * inp

    spread_lanes(bc_ref, bcb_scr, slots)
    h_now[...] = ck_ref[0]

    def replay(k, carry):
        ds, us, gys = [], [], []
        for j in range(PAIR):
            at = pl.ds(pl.multiple_of((k * PAIR + j) * slots, slots), slots)
            ds.append(delta_scr[at, :])
            us.append(u_scr[at, :])
            gys.append(gy_scr[at, :])
        for n in range(states):
            rate = rate_scr[n]
            h = h_now[n]
            for j in range(PAIR):
                t = k * PAIR + j
                h_scr[t, n] = h
                decay = jnp.exp2(ds[j] * rate)
                a_scr[t, n] = decay
                h = decay * h + us[j] * widen(bcb_scr[t, n], width)
                gbc_scr[t, states + n] = narrow(h * gys[j])
            h_now[n] = h
        return carry

    lax.fori_loop(0, steps // PAIR, replay, 0)

    def reverse(k, carry):
        ats, ds, us, gys, gus, gds, ts = [], [], [], [], [], [], []
        for j in range(PAIR):
            t = steps - 1 - (k * PAIR + j)
            at = pl.ds(pl.multiple_of(t * slots, slots), slots)
            ts.append(t)
            ats.append(at)
            ds.append(delta_scr[at, :])
            us.append(u_scr[at, :])
            gys.append(gy_scr[at, :])
            gus.append(None)
            gds.append(None)
        for n in range(states):
            rate = rate_scr[n]
            carried = lam_scr[n]
            total = dacc_scr[n]
            for j in range(PAIR):
                t = ts[j]
                lam = carried + gys[j] * widen(bcb_scr[t, states + n], width)
                term = lam * widen(bcb_scr[t, n], width)
                gus[j] = term if n == 0 else gus[j] + term
                gbc_scr[t, n] = narrow(lam * us[j])
                carried = a_scr[t, n] * lam
                q = carried * h_scr[t, n]
                term = q * rate
                gds[j] = term if n == 0 else gds[j] + term
                total = total + q * ds[j]
            lam_scr[n] = carried
            dacc_scr[n] = total
        for j in range(PAIR):
            gu_scr[ats[j], :] = gus[j]
            gd_scr[ats[j], :] = gds[j]
        return carry

    lax.fori_loop(0, steps // PAIR, reverse, 0)

    def reduce_lanes(k, carry):
        for j in range(TOGETHER):
            t = k * TOGETHER + j
            at = pl.ds(pl.multiple_of(t * slots, slots), slots)
            total = lane_sums([gbc_scr[t, n] for n in range(2 * states)])
            gbc_ref[at, :] = total[:, : 2 * states]
        return carry

    lax.fori_loop(0, steps // TOGETHER, reduce_lanes, 0)
    gu = gu_scr[...]
    gis_ref[...] = gu * delta_scr[...] + skip_ref[...] * gy_scr[...]
    g_pre = (gd_scr[...] * (1.0 / LOG2E) + gu * inp) * sigmoid(z)
    bacc_scr[...] += jnp.sum(g_pre.reshape(steps, slots, width), axis=0)
    g_low = g_pre.astype(BF16)
    grank_ref[...] += dot(g_low, dtl_ref[...], ((0,), (0,)))
    pack_rows(gproj_ref, dot(g_low, dtw_ref[...]), gbc_ref[...], length)

    @pl.when(step_id == pl.num_programs(0) - 1)
    def _():
        for n in range(states):
            gdec_ref[n : n + 1, :] = jnp.sum(dacc_scr[n], axis=0, keepdims=True) * rate_ref[n : n + 1, :]
        gskip_ref[...] = jnp.sum(sacc_scr[...], axis=0, keepdims=True)
        gbias_ref[...] = jnp.sum(bacc_scr[...], axis=0, keepdims=True)


def tail_kernel(
    gdtl_ref, gbc_ref, inp_ref, gis_ref, ggate_ref, inner_ref, before_ref, x_ref, gain_ref, win_ref, xw_ref, cw_ref,
    cb_ref, gnorm_ref, gin_ref, gsel_ref, gcw_ref, gcb_ref, ggain_ref,
    gin_scr, pad_scr, gpad_scr, wacc_scr, cacc_scr, *, slots
):
    rows, width = inp_ref.shape
    steps = rows // slots
    halo = 3 * slots
    step_id = pl.program_id(0)
    last = pl.num_programs(0) - 1

    @pl.when(step_id == 0)
    def _():
        gpad_scr[rows : rows + halo, :] = jnp.zeros((halo, width), F32)
        wacc_scr[...] = jnp.zeros_like(wacc_scr)
        cacc_scr[...] = jnp.zeros_like(cacc_scr)
        gin_scr[...] = jnp.zeros_like(gin_scr)
        ggain_ref[...] = jnp.zeros_like(ggain_ref)
        gsel_ref[...] = jnp.zeros_like(gsel_ref)

    gproj = jnp.concatenate([gdtl_ref[...], gbc_ref[...]], axis=1)
    gsel_ref[...] += dot(inp_ref[...], gproj, ((0,), (0,)))
    g_inputs = gis_ref[...] + dot(gproj, xw_ref[...], ((1,), (1,)))
    first = (step_id < last).astype(F32)
    pad_scr[0:halo, :] = before_ref[slots : slots + halo, :] * first
    pad_scr[halo : halo + rows, :] = inner_ref[...]
    total = jnp.broadcast_to(cb_ref[...], (rows, width))
    for tap in range(4):
        total = total + cw_ref[tap : tap + 1, :] * pad_scr[tap * slots : tap * slots + rows, :]
    sig = sigmoid(total)
    g_conv = g_inputs * (sig * (1.0 + total * (1.0 - sig)))
    gpad_scr[0:rows, :] = g_conv
    g_inner = jnp.zeros((rows, width), F32)
    for tap in range(4):
        back = (3 - tap) * slots
        g_inner = g_inner + cw_ref[tap : tap + 1, :] * gpad_scr[back : back + rows, :]
        wacc_scr[tap] += jnp.sum(
            (g_conv * pad_scr[tap * slots : tap * slots + rows, :]).reshape(steps, slots, width), axis=0
        )
    cacc_scr[...] += jnp.sum(g_conv.reshape(steps, slots, width), axis=0)
    gpad_scr[rows : rows + halo, :] = gpad_scr[0:halo, :]
    g_both = jnp.concatenate([g_inner.astype(BF16), ggate_ref[...]], axis=1)
    x = x_ref[...].astype(F32)
    scaled = x * lax.rsqrt(jnp.mean(x * x, axis=-1, keepdims=True) + EPSILON)
    gin_scr[...] += dot((scaled * gain_ref[...]).astype(BF16), g_both, ((0,), (0,)))
    g_normed = dot(g_both, win_ref[...], ((1,), (1,)))
    ggain_ref[...] += jnp.sum(g_normed * scaled, axis=0, keepdims=True)
    gnorm_ref[...] = g_normed.astype(gnorm_ref.dtype).reshape(gnorm_ref.shape)

    @pl.when(step_id == last)
    def _():
        for tap in range(4):
            gcw_ref[tap : tap + 1, :] = jnp.sum(wacc_scr[tap], axis=0, keepdims=True)
        gcb_ref[...] = jnp.sum(cacc_scr[...], axis=0, keepdims=True)
        gin_ref[...] = gin_scr[...].astype(gin_ref.dtype)


def remote(src, dst, send, recv, where):
    return pltpu.make_async_remote_copy(
        src_ref=src, dst_ref=dst, send_sem=send, recv_sem=recv, device_id=where, device_id_type=pl.DeviceIdType.MESH
    )


def gather_kernel(
    tok_ref, cot_ref, win_ref, gain_ref, pk_ref, x_ref, c_ref, w_ref, g_ref, p_ref,
    tok_buf, cot_buf, win_buf, gain_buf, pk_buf, local_sem,
    tdp_send, tdp_recv, cdp_send, cdp_recv, up_send, up_recv, down_send, down_recv, core_send, core_recv,
    w1_send, w1_recv, w2_send, w2_recv, g1_send, g1_recv, g2_send, g2_recv, p_send, p_recv, *, n_dp, n_f
):
    d = lax.axis_index("dp")
    f = lax.axis_index("fsdp")
    n_z = n_f // 2
    z = f // 2
    core = f % 2
    partner = z * 2 + (1 - core)

    barrier = pltpu.get_barrier_semaphore()
    for k in range(1, n_f):
        pl.semaphore_signal(barrier, inc=1, device_id=(d, (f + k) % n_f), device_id_type=pl.DeviceIdType.MESH)
    for k in range(1, n_dp):
        pl.semaphore_signal(barrier, inc=1, device_id=((d + k) % n_dp, f), device_id_type=pl.DeviceIdType.MESH)
    pl.semaphore_wait(barrier, n_f + n_dp - 2)

    loads = (
        pltpu.make_async_copy(tok_ref.at[d], tok_buf, local_sem.at[0]),
        pltpu.make_async_copy(win_ref.at[f], win_buf, local_sem.at[1]),
        pltpu.make_async_copy(gain_ref, gain_buf, local_sem.at[2]),
        pltpu.make_async_copy(pk_ref, pk_buf, local_sem.at[3]),
        pltpu.make_async_copy(cot_ref.at[d], cot_buf, local_sem.at[8]),
    )
    stores = (
        pltpu.make_async_copy(tok_buf, x_ref.at[d, f], local_sem.at[4]),
        pltpu.make_async_copy(win_buf, w_ref.at[d, f], local_sem.at[5]),
        pltpu.make_async_copy(gain_buf, g_ref.at[d, f], local_sem.at[6]),
        pltpu.make_async_copy(pk_buf, p_ref.at[d], local_sem.at[7]),
        pltpu.make_async_copy(cot_buf, c_ref.at[d], local_sem.at[9]),
    )
    for load in loads:
        load.start()

    def tok_dp(k):
        to = (d + k) % n_dp
        return remote(tok_ref.at[to], x_ref.at[d, f], tdp_send.at[k], tdp_recv.at[k], (to, f))

    def tok_dp_arrival(k):
        src = (d - k + n_dp) % n_dp
        return remote(tok_ref.at[d], x_ref.at[src, f], tdp_send.at[k], tdp_recv.at[k], (src, f))

    def cot_dp(k):
        to = (d + k) % n_dp
        return remote(cot_ref.at[to], c_ref.at[d], cdp_send.at[k], cdp_recv.at[k], (to, f))

    def cot_dp_arrival(k):
        src = (d - k + n_dp) % n_dp
        return remote(cot_ref.at[d], c_ref.at[src], cdp_send.at[k], cdp_recv.at[k], (src, f))

    def w1(k):
        to = (f + k) % n_f
        return remote(win_ref.at[to], w_ref.at[d, f], w1_send.at[k], w1_recv.at[k], (d, to))

    def w1_arrival(k):
        src = (f - k + n_f) % n_f
        return remote(win_ref.at[f], w_ref.at[d, src], w1_send.at[k], w1_recv.at[k], (d, src))

    def g1(k):
        to = (f + k) % n_f
        return remote(gain_ref, g_ref.at[d, f], g1_send.at[k], g1_recv.at[k], (d, to))

    def g1_arrival(k):
        src = (f - k + n_f) % n_f
        return remote(gain_ref, g_ref.at[d, src], g1_send.at[k], g1_recv.at[k], (d, src))

    def w2(k):
        to = (d + k) % n_dp
        return remote(w_ref.at[d], w_ref.at[d], w2_send.at[k], w2_recv.at[k], (to, f))

    def w2_arrival(k):
        src = (d - k + n_dp) % n_dp
        return remote(w_ref.at[src], w_ref.at[src], w2_send.at[k], w2_recv.at[k], (src, f))

    def g2(k):
        to = (d + k) % n_dp
        return remote(g_ref.at[d], g_ref.at[d], g2_send.at[k], g2_recv.at[k], (to, f))

    def g2_arrival(k):
        src = (d - k + n_dp) % n_dp
        return remote(g_ref.at[src], g_ref.at[src], g2_send.at[k], g2_recv.at[k], (src, f))

    def pk(k):
        to = (d + k) % n_dp
        return remote(pk_ref, p_ref.at[d], p_send.at[k], p_recv.at[k], (to, f))

    def pk_arrival(k):
        src = (d - k + n_dp) % n_dp
        return remote(pk_ref, p_ref.at[src], p_send.at[k], p_recv.at[k], (src, f))

    def block(j, origin, side):
        at = (d - j + n_dp) % n_dp
        return x_ref.at[at, origin * 2 + side]

    def up(j, origin, src=None):
        ref = block(j, origin, core)
        return remote(ref if src is None else src, ref, up_send.at[origin, j], up_recv.at[origin, j], (d, f + 2))

    def down(j, origin, src=None):
        ref = block(j, origin, core)
        return remote(ref if src is None else src, ref, down_send.at[origin, j], down_recv.at[origin, j], (d, f - 2))

    def across(j, origin, src=None):
        ref = block(j, origin, core)
        return remote(
            ref if src is None else src, ref, core_send.at[origin, j], core_recv.at[origin, j], (d, partner)
        )

    def across_arrival(j, origin):
        ref = block(j, origin, 1 - core)
        return remote(ref, ref, core_send.at[origin, j], core_recv.at[origin, j], (d, partner))

    def launch(j, src=None):
        @pl.when(z < n_z - 1)
        def _():
            up(j, z, src).start()

        @pl.when(z > 0)
        def _():
            down(j, z, src).start()

        across(j, z, src).start()

    for k in range(1, n_f):
        w1(k).start()
    for k in range(1, n_dp):
        tok_dp(k).start()
    launch(0, tok_ref.at[d])
    for k in range(1, n_f):
        g1(k).start()
    for k in range(1, n_dp):
        pk(k).start()
    for k in range(1, n_dp):
        cot_dp(k).start()
    for load, store in zip(loads, stores):
        load.wait()
        store.start()
    for k in range(1, n_dp):
        tok_dp_arrival(k).wait_recv()
        launch(k)
    for store in stores:
        store.wait()
    for k in range(1, n_f):
        w1_arrival(k).wait_recv()
        g1_arrival(k).wait_recv()
    for k in range(1, n_dp):
        w2(k).start()
        g2(k).start()
    for far in range(1, n_z):
        for j in range(n_dp):

            @pl.when(z >= far)
            def _():
                origin = z - far
                up(j, origin).wait_recv()

                @pl.when(z < n_z - 1)
                def _():
                    up(j, origin).start()

                across(j, origin).start()

            @pl.when(z + far < n_z)
            def _():
                origin = z + far
                down(j, origin).wait_recv()

                @pl.when(z > 0)
                def _():
                    down(j, origin).start()

                across(j, origin).start()

    for origin in range(n_z):
        for j in range(n_dp):
            across_arrival(j, origin).wait_recv()
            across(j, origin).wait_send()
    for origin in range(n_z):
        for j in range(n_dp):

            @pl.when((origin <= z) & (z < n_z - 1))
            def _():
                up(j, origin).wait_send()

            @pl.when((origin >= z) & (z > 0))
            def _():
                down(j, origin).wait_send()

    for k in range(1, n_dp):
        pk_arrival(k).wait_recv()
        cot_dp_arrival(k).wait_recv()
        cot_dp(k).wait_send()
        w2_arrival(k).wait_recv()
        g2_arrival(k).wait_recv()
        tok_dp(k).wait_send()
        w2(k).wait_send()
        g2(k).wait_send()
        pk(k).wait_send()
    for k in range(1, n_f):
        w1(k).wait_send()
        g1(k).wait_send()


def pack_rows(out_ref, main, rest, chunk):
    part = chunk // 4
    for q in range(main.shape[0] // chunk):
        out_ref[q, 0:chunk, :] = main[q * chunk : (q + 1) * chunk, :]
        for j in range(4):
            first = q * chunk + j * part
            out_ref[q, chunk : chunk + part, j * 32 : (j + 1) * 32] = rest[first : first + part, :]


def combine_kernel(
    part_ref, main_ref, rest_ref, one, sums, two, tops, rests,
    one_send, one_recv, two_send, two_recv, top_send, top_recv, rest_send, rest_recv,
    ctop_send, ctop_recv, crest_send, crest_recv, *, n_dp, n_f
):
    d = lax.axis_index("dp")
    f = lax.axis_index("fsdp")
    n_z = n_f // 2
    z = f // 2
    core = f % 2
    other = 1 - core
    partner = z * 2 + other
    chunk = tops.shape[2]

    barrier = pltpu.get_barrier_semaphore()
    pl.semaphore_signal(barrier, inc=1, device_id=(d, partner), device_id_type=pl.DeviceIdType.MESH)
    for k in range(1, n_z):
        pl.semaphore_signal(
            barrier, inc=1, device_id=(d, (z + k) % n_z * 2 + core), device_id_type=pl.DeviceIdType.MESH
        )
    pl.semaphore_wait(barrier, n_z)

    def first(k):
        to = (z + k) % n_z
        return remote(part_ref.at[to, other], one.at[to], one_send.at[k], one_recv.at[k], (d, partner))

    def second(k):
        to = (z + k) % n_z
        return remote(sums.at[to], two.at[k], two_send.at[k], two_recv.at[k], (d, to * 2 + core))

    def third(k):
        to = ((z + k) % n_z * 2 + core,)
        return (
            remote(tops.at[z, core], tops.at[z, core], top_send.at[k], top_recv.at[k], (d,) + to),
            remote(rests.at[z, core], rests.at[z, core], rest_send.at[k], rest_recv.at[k], (d,) + to),
        )

    def third_arrival(k):
        src = (z - k + n_z) % n_z
        to = (src * 2 + core,)
        return (
            remote(tops.at[src, core], tops.at[src, core], top_send.at[k], top_recv.at[k], (d,) + to),
            remote(rests.at[src, core], rests.at[src, core], rest_send.at[k], rest_recv.at[k], (d,) + to),
        )

    def fourth(k, side):
        src = (z - k + n_z) % n_z
        return (
            remote(tops.at[src, side], tops.at[src, side], ctop_send.at[k], ctop_recv.at[k], (d, partner)),
            remote(rests.at[src, side], rests.at[src, side], crest_send.at[k], crest_recv.at[k], (d, partner)),
        )

    order = list(range(1, n_z)) + [0]
    for k in order:
        first(k).start()
    for k in order:
        to = (z + k) % n_z
        first(k).wait_recv()
        sums[to] = (part_ref[to, core] + one[to]).astype(sums.dtype)
        if k:
            second(k).start()
    total = part_ref[z, core] + one[z]
    for k in range(1, n_z):
        second(k).wait_recv()
        total = total + two[k].astype(F32)
    tops[z, core] = total[0:chunk, :].astype(tops.dtype)
    rests[z, core] = total[chunk:, :].astype(rests.dtype)
    for k in range(1, n_z):
        for copy in third(k):
            copy.start()
    for copy in fourth(0, core):
        copy.start()
    for k in range(1, n_z):
        for copy in third_arrival(k):
            copy.wait_recv()
        for copy in fourth(k, core):
            copy.start()
    for k in range(n_z):
        for copy in fourth(k, other):
            copy.wait_recv()
    part = chunk // 4
    for a in range(n_z):
        for b in range(2):
            at = (a * 2 + b) * chunk
            main_ref[at : at + chunk, :] = tops[a, b]
            rest = rests[a, b]
            for j in range(4):
                rest_ref[at + j * part : at + (j + 1) * part, :] = rest[:, j * 32 : (j + 1) * 32]
    for k in range(n_z):
        first(k).wait_send()
        for copy in fourth(k, core):
            copy.wait_send()
        if k:
            second(k).wait_send()
            for copy in third(k):
                copy.wait_send()


def scatter_kernel(
    gn_ref, gin_ref, gg_ref, out_ref, gout_ref, ggout_ref,
    mine, theirs, rup, rdown, blocks, got, gsum, ggot, ggsum, local_sem,
    one_send, one_recv, up_send, up_recv, down_send, down_recv, dp_send, dp_recv,
    w1_send, w1_recv, w2_send, w2_recv, g1_send, g1_recv, g2_send, g2_recv, *, n_dp, n_f
):
    d = lax.axis_index("dp")
    f = lax.axis_index("fsdp")
    n_z = n_f // 2
    z = f // 2
    core = f % 2
    other = 1 - core
    partner = z * 2 + other

    barrier = pltpu.get_barrier_semaphore()
    for k in range(1, n_f):
        pl.semaphore_signal(barrier, inc=1, device_id=(d, (f + k) % n_f), device_id_type=pl.DeviceIdType.MESH)
    for k in range(1, n_dp):
        pl.semaphore_signal(barrier, inc=1, device_id=((d + k) % n_dp, f), device_id_type=pl.DeviceIdType.MESH)
    pl.semaphore_wait(barrier, n_f + n_dp - 2)

    def one(to, j):
        return remote(
            gn_ref.at[to * 2 + other, j], theirs.at[to, j], one_send.at[to, j], one_recv.at[to, j], (d, partner)
        )

    def up(to, j):
        return remote(mine.at[to, j], rup.at[to, j], up_send.at[to, j], up_recv.at[to, j], (d, f + 2))

    def down(to, j):
        return remote(mine.at[to, j], rdown.at[to, j], down_send.at[to, j], down_recv.at[to, j], (d, f - 2))

    def dp(k):
        to = (d + k) % n_dp
        return remote(blocks.at[to], out_ref.at[d], dp_send.at[k], dp_recv.at[k], (to, f))

    def dp_arrival(k):
        src = (d - k + n_dp) % n_dp
        return remote(blocks.at[src], out_ref.at[src], dp_send.at[k], dp_recv.at[k], (src, f))

    def w1(k):
        to = (d + k) % n_dp
        return remote(gin_ref.at[to], got.at[k], w1_send.at[k], w1_recv.at[k], (to, f))

    def g1(k):
        to = (d + k) % n_dp
        return remote(gg_ref.at[to], ggot.at[k], g1_send.at[k], g1_recv.at[k], (to, f))

    def w2(k):
        to = (f + k) % n_f
        return remote(gsum.at[to], gout_ref.at[f], w2_send.at[k], w2_recv.at[k], (d, to))

    def w2_arrival(k):
        src = (f - k + n_f) % n_f
        return remote(gsum.at[src], gout_ref.at[src], w2_send.at[k], w2_recv.at[k], (d, src))

    def g2(k):
        to = (f + k) % n_f
        return remote(ggsum.at[to], ggout_ref.at[f], g2_send.at[k], g2_recv.at[k], (d, to))

    def g2_arrival(k):
        src = (f - k + n_f) % n_f
        return remote(ggsum.at[src], ggout_ref.at[src], g2_send.at[k], g2_recv.at[k], (d, src))

    def load(to, j):
        return pltpu.make_async_copy(gn_ref.at[to * 2 + core, j], mine.at[to, j], local_sem.at[to, j])

    own_gin = pltpu.make_async_copy(gin_ref.at[d], got.at[0], local_sem.at[n_z, 0])
    own_gg = pltpu.make_async_copy(gg_ref.at[d], ggot.at[0], local_sem.at[n_z, 1])
    put_block = pltpu.make_async_copy(blocks.at[d], out_ref.at[d], local_sem.at[n_z, 2])
    put_gin = pltpu.make_async_copy(gsum.at[f], gout_ref.at[f], local_sem.at[n_z, 3])
    put_gg = pltpu.make_async_copy(ggsum.at[f], ggout_ref.at[f], local_sem.at[n_z + 1, 0])

    for far in range(n_z - 1, -1, -1):
        for j in range(n_dp):

            @pl.when(z + far < n_z)
            def _():
                one(z + far, j).start()
                load(z + far, j).start()

            if far:

                @pl.when(z >= far)
                def _():
                    one(z - far, j).start()
                    load(z - far, j).start()

    for k in range(1, n_dp):
        w1(k).start()
        g1(k).start()
    own_gin.start()
    own_gg.start()

    def pair(to, j):
        one(to, j).wait_recv()
        load(to, j).wait()
        return mine[to, j].astype(F32) + theirs[to, j].astype(F32)

    def weights():
        own_gin.wait()
        own_gg.wait()
        for k in range(1, n_dp):
            w1(k).wait_recv()
            g1(k).wait_recv()

        def add(q, carry):
            total = got[0, q].astype(F32)
            for k in range(1, n_dp):
                total = total + got[k, q].astype(F32)
            gsum[q] = total.astype(gsum.dtype)
            total = ggot[0, q]
            for k in range(1, n_dp):
                total = total + ggot[k, q]
            ggsum[q] = total
            return carry

        lax.fori_loop(0, n_f, add, 0)
        for k in range(1, n_f):
            w2(k).start()
            g2(k).start()
        put_gin.start()
        put_gg.start()

    for far in range(n_z - 1, 0, -1):
        for j in range(n_dp):

            @pl.when(z + far < n_z)
            def _():
                to = z + far
                total = pair(to, j)
                mine[to, j] = total.astype(mine.dtype)

                @pl.when(z > 0)
                def _():
                    up(to, j).wait_recv()
                    mine[to, j] = (mine[to, j].astype(F32) + rup[to, j].astype(F32)).astype(mine.dtype)

                up(to, j).start()

            @pl.when(z >= far)
            def _():
                to = z - far
                total = pair(to, j)
                mine[to, j] = total.astype(mine.dtype)

                @pl.when(z < n_z - 1)
                def _():
                    down(to, j).wait_recv()
                    mine[to, j] = (mine[to, j].astype(F32) + rdown[to, j].astype(F32)).astype(mine.dtype)

                down(to, j).start()

    weights()
    for j in range(n_dp):
        mine[z, j] = pair(z, j).astype(mine.dtype)

        @pl.when(z > 0)
        def _():
            up(z, j).wait_recv()
            mine[z, j] = (mine[z, j].astype(F32) + rup[z, j].astype(F32)).astype(mine.dtype)

        @pl.when(z < n_z - 1)
        def _():
            down(z, j).wait_recv()
            mine[z, j] = (mine[z, j].astype(F32) + rdown[z, j].astype(F32)).astype(mine.dtype)

        blocks[j] = mine[z, j]
    for k in range(1, n_dp):
        dp(k).start()
    put_block.start()

    for k in range(1, n_f):
        w2_arrival(k).wait_recv()
        g2_arrival(k).wait_recv()
    for k in range(1, n_dp):
        dp_arrival(k).wait_recv()
    put_block.wait()
    put_gin.wait()
    put_gg.wait()
    for k in range(1, n_f):
        w2(k).wait_send()
        g2(k).wait_send()
    for k in range(1, n_dp):
        w1(k).wait_send()
        g1(k).wait_send()
        dp(k).wait_send()
    for to in range(n_z):
        for j in range(n_dp):
            one(to, j).wait_send()

            @pl.when(z < to)
            def _():
                up(to, j).wait_send()

            @pl.when(z > to)
            def _():
                down(to, j).wait_send()


def whole(shape):
    return pl.BlockSpec(shape, lambda i: (0,) * len(shape))


def cost(micros):
    return pl.CostEstimate(flops=int(micros * 1.15e9), bytes_accessed=1 << 20, transcendentals=0)


def params():
    return pltpu.CompilerParams(vmem_limit_bytes=VMEM_BYTES, dimension_semantics=("arbitrary",))


def body(
    tokens, cotangent, lengths, deal_order, norm_gain, in_weight, conv_weight, conv_bias,
    x_weight, dt_weight, dt_bias, decay_log, skip_gain, out_weight, *, n_dp, n_f
):
    seqs, own, model = tokens.shape
    slots = seqs // n_dp
    inner_rows, states = decay_log.shape
    rank = dt_weight.shape[1]
    proj_cols = x_weight.shape[1]
    width = inner_rows * n_dp
    length = own * n_dp * n_f
    d_rows = in_weight.shape[0]
    total_rows = length * slots
    group = lax.axis_index("dp")
    member = lax.axis_index("fsdp")

    low = lambda v: v.astype(BF16)
    slot_ids = jnp.arange(seqs, dtype=jnp.int32)
    seq_len = jnp.sum(jnp.where(deal_order[:, None] == slot_ids[None, :], lengths[:, None], 0), axis=0)
    own_pos = (group * n_f + member) * own + jnp.arange(own, dtype=jnp.int32)
    own_mask = own_pos[None, :] < seq_len[:, None]

    def by_group(v):
        return v.reshape(n_dp, slots, own, model).transpose(0, 2, 1, 3).reshape(n_dp, own * slots, model)

    def collect(v):
        v = lax.psum_scatter(v.reshape(total_rows, model), "fsdp", scatter_dimension=0, tiled=True)
        v = lax.all_to_all(v.reshape(n_dp, own, slots, model), "dp", 0, 0, tiled=True)
        return v.transpose(0, 2, 1, 3).reshape(seqs, own, model)

    masked = by_group(jnp.where(own_mask[:, :, None], cotangent, jnp.zeros_like(cotangent)))

    tok = by_group(tokens)
    win = low(in_weight).reshape(d_rows, 2, n_dp, n_f, inner_rows).transpose(3, 0, 1, 2, 4)
    win = win.reshape(n_f, d_rows, 2 * width)
    gain_tile = jnp.zeros((8, 128), F32).at[0, :d_rows].set(low(norm_gain).astype(F32))
    packed = jnp.concatenate(
        [
            low(v)
            for v in (
                out_weight, x_weight, dt_weight, decay_log, conv_weight,
                conv_bias[:, None], dt_bias[:, None], skip_gain[:, None],
            )
        ],
        axis=1,
    )
    packed = jnp.pad(packed, ((0, 0), (0, -packed.shape[1] % 128)))
    n_z = n_f // 2
    dma = pltpu.SemaphoreType.DMA
    hbm = pl.BlockSpec(memory_space=pl.ANY)
    x, g_branch, win, gain, packed = pl.pallas_call(
        functools.partial(gather_kernel, n_dp=n_dp, n_f=n_f),
        in_specs=[hbm] * 5,
        out_specs=[hbm] * 5,
        out_shape=[
            jax.ShapeDtypeStruct((n_dp, n_f) + tok.shape[1:], BF16),
            jax.ShapeDtypeStruct(tok.shape, BF16),
            jax.ShapeDtypeStruct((n_dp, n_f) + win.shape[1:], BF16),
            jax.ShapeDtypeStruct((n_dp, n_f, 8, 128), F32),
            jax.ShapeDtypeStruct((n_dp,) + packed.shape, BF16),
        ],
        scratch_shapes=[
            pltpu.VMEM(tok.shape[1:], BF16), pltpu.VMEM(tok.shape[1:], BF16), pltpu.VMEM(win.shape[1:], BF16),
            pltpu.VMEM((8, 128), F32), pltpu.VMEM(packed.shape, BF16), dma((10,)),
            dma((n_dp,)), dma((n_dp,)), dma((n_dp,)), dma((n_dp,)),
        ]
        + [dma((n_z, n_dp))] * 6
        + [dma((n_f,)), dma((n_f,)), dma((n_dp,)), dma((n_dp,)), dma((n_f,)), dma((n_f,))]
        + [dma((n_dp,))] * 4,
        compiler_params=pltpu.CompilerParams(collective_id=1, has_side_effects=True),
        cost_estimate=cost(90),
        name="gather",
    )(tok, masked, win, gain_tile, packed)
    g_branch = lax.all_gather(g_branch, "fsdp", axis=0, tiled=False)
    x = x.reshape(total_rows, model)
    win = win.reshape(model, 2 * width)
    gain = gain[:, :, 0, :d_rows].reshape(1, model)
    packed = packed.reshape(width, -1)
    cuts = [model, proj_cols, rank, states, 4, 1, 1, 1]
    pieces, start = [], 0
    for cut in cuts:
        pieces.append(packed[:, start : start + cut])
        start += cut
    ow, xw, dtw, decay, cw, cb, dtb, skip = pieces
    rate = -jnp.exp(decay.astype(F32)).T
    cw, cb, dtb, skip = (v.astype(F32).T for v in (cw, cb, dtb, skip))

    rows = STEPS * slots
    blocks = length // STEPS
    grid = (blocks,)
    row_spec = lambda cols: pl.BlockSpec((rows, cols), lambda i: (i, 0))
    rev_spec = lambda cols: pl.BlockSpec((rows, cols), lambda i: (blocks - 1 - i, 0))
    like = jax.ShapeDtypeStruct
    held = STEPS // own
    per = n_f // held
    piece = (held, 1, own * slots, model)
    piece_spec = pl.BlockSpec(piece, lambda i: (i % per, i // per, 0, 0))
    rev_piece_spec = pl.BlockSpec(piece, lambda i: ((blocks - 1 - i) % per, (blocks - 1 - i) // per, 0, 0))
    pieces_shape = like((n_f, n_dp, own * slots, model), BF16)
    packed_rows = length + length // 4
    parts = rows // length
    part_spec = pl.BlockSpec((parts, packed_rows, 128), lambda i: (i, 0, 0))
    rev_part_spec = pl.BlockSpec((parts, packed_rows, 128), lambda i: (blocks - 1 - i, 0, 0))
    parts_shape = like((n_f, packed_rows, 128), F32)

    def combine(v, rest_type, number):
        vmem = pl.BlockSpec(memory_space=pltpu.VMEM)
        return pl.pallas_call(
            functools.partial(combine_kernel, n_dp=n_dp, n_f=n_f),
            in_specs=[vmem],
            out_specs=[vmem, vmem],
            out_shape=[like((total_rows, rank), BF16), like((total_rows, 2 * states), rest_type)],
            scratch_shapes=[
                pltpu.VMEM((n_z, packed_rows, 128), F32), pltpu.VMEM((n_z, packed_rows, 128), F32),
                pltpu.VMEM((n_z, packed_rows, 128), F32), pltpu.VMEM((n_z, 2, length, 128), BF16),
                pltpu.VMEM((n_z, 2, length // 4, 128), rest_type),
            ]
            + [dma((n_z,))] * 12,
            compiler_params=pltpu.CompilerParams(
                collective_id=number, has_side_effects=True, vmem_limit_bytes=VMEM_BYTES
            ),
            cost_estimate=cost(28),
        name="combine",
        )(v.reshape(n_z, 2, packed_rows, 128))

    inner, gate, inp, proj = pl.pallas_call(
        functools.partial(front_kernel, slots=slots, length=length),
        grid=grid,
        in_specs=[
            row_spec(model), whole((1, model)), whole((model, 2 * width)), whole((4, width)), whole((1, width)),
            whole((width, proj_cols)),
        ],
        out_specs=[row_spec(width), row_spec(width), row_spec(width), part_spec],
        out_shape=[
            like((total_rows, width), F32), like((total_rows, width), F32), like((total_rows, width), BF16),
            parts_shape,
        ],
        scratch_shapes=[pltpu.VMEM((rows + 3 * slots, width), F32)],
        compiler_params=params(),
        cost_estimate=cost(20),
        name="front",
    )(x, gain, win, cw, cb, xw)

    dtl, bc = combine(proj, F32, 2)

    y, ck, branch = pl.pallas_call(
        functools.partial(mix_kernel, slots=slots),
        grid=grid,
        in_specs=[
            row_spec(rank), row_spec(2 * states), row_spec(width), row_spec(width), whole((width, rank)),
            whole((1, width)), whole((states, width)), whole((1, width)), whole((width, model)),
        ],
        out_specs=[
            row_spec(width), pl.BlockSpec((1, states, slots, width), lambda i: (i, 0, 0, 0)), piece_spec,
        ],
        out_shape=[
            like((total_rows, width), F32), like((blocks, states, slots, width), F32), pieces_shape,
        ],
        scratch_shapes=[
            pltpu.VMEM((states, slots, width), F32), pltpu.VMEM((rows, width), F32), pltpu.VMEM((rows, width), F32),
            pltpu.VMEM((states, slots, width), F32), pltpu.VMEM((STEPS, 2 * states, slots, 128), F32),
        ],
        compiler_params=params(),
        cost_estimate=cost(42),
        name="mix",
    )(dtl, bc, inp, gate, dtw, dtb, rate, skip, ow)

    gis, ggate, gproj, gout, grank, gdec, gskip, gbias = pl.pallas_call(
        functools.partial(back_kernel, slots=slots, length=length),
        grid=grid,
        in_specs=[
            rev_piece_spec, rev_spec(rank), rev_spec(2 * states), rev_spec(width), rev_spec(width), rev_spec(width),
            pl.BlockSpec((1, states, slots, width), lambda i: (blocks - 1 - i, 0, 0, 0)),
            whole((width, rank)), whole((1, width)), whole((states, width)), whole((1, width)), whole((width, model)),
        ],
        out_specs=[
            rev_spec(width), rev_spec(width), rev_part_spec, whole((width, model)), whole((width, rank)),
            whole((states, width)), whole((1, width)), whole((1, width)),
        ],
        out_shape=[
            like((total_rows, width), F32), like((total_rows, width), BF16), parts_shape,
            like((width, model), F32), like((width, rank), F32), like((states, width), F32), like((1, width), F32),
            like((1, width), F32),
        ],
        scratch_shapes=[
            pltpu.VMEM((states, slots, width), F32), pltpu.VMEM((states, slots, width), F32),
            pltpu.VMEM((slots, width), F32), pltpu.VMEM((slots, width), F32), pltpu.VMEM((states, slots, width), F32),
        ]
        + [pltpu.VMEM((rows, width), F32)] * 5
        + [
            pltpu.VMEM((STEPS, states, slots, width), F32), pltpu.VMEM((STEPS, states, slots, width), F32),
            pltpu.VMEM((STEPS, 2 * states, slots, 128), F32), pltpu.VMEM((STEPS, 2 * states, slots, 128), F32),
            pltpu.VMEM((states, slots, width), F32), pltpu.VMEM((rows, 2 * states), F32),
        ],
        compiler_params=params(),
        cost_estimate=cost(104),
        name="back",
    )(g_branch, dtl, bc, inp, gate, y, ck, dtw, dtb, rate, skip, ow)

    gdtl, gbc = combine(gproj, BF16, 3)

    branch = collect(branch)
    branch, gdtl = lax.optimization_barrier((branch, gdtl))
    gnorm, gin, gsel, gcw, gcb, ggain = pl.pallas_call(
        functools.partial(tail_kernel, slots=slots),
        grid=grid,
        in_specs=[
            rev_spec(rank), rev_spec(2 * states), rev_spec(width), rev_spec(width), rev_spec(width), rev_spec(width),
            pl.BlockSpec((4 * slots, width), lambda i: (jnp.maximum((blocks - 1 - i) * (STEPS // 4) - 1, 0), 0)),
            rev_spec(model), whole((1, model)), whole((model, 2 * width)), whole((width, proj_cols)), whole((4, width)),
            whole((1, width)),
        ],
        out_specs=[
            rev_piece_spec, whole((model, 2 * width)), whole((width, proj_cols)), whole((4, width)), whole((1, width)),
            whole((1, model)),
        ],
        out_shape=[
            pieces_shape, like((model, 2 * width), BF16), like((width, proj_cols), F32),
            like((4, width), F32), like((1, width), F32), like((1, model), F32),
        ],
        scratch_shapes=[
            pltpu.VMEM((model, 2 * width), F32), pltpu.VMEM((rows + 3 * slots, width), F32),
            pltpu.VMEM((rows + 3 * slots, width), F32), pltpu.VMEM((4, slots, width), F32),
            pltpu.VMEM((slots, width), F32),
        ],
        compiler_params=params(),
        cost_estimate=cost(35),
        name="tail",
    )(gdtl, gbc, inp, gis, ggate, inner, inner, x, gain, win, xw, cw, cb)

    small = jnp.concatenate([gsel, grank, gdec.T, gcw.T, gcb.T, gbias.T, gskip.T], axis=1)
    small = lax.psum_scatter(jnp.concatenate([low(gout), low(small)], axis=1), "dp", scatter_dimension=0, tiled=True)
    small = small.astype(F32)

    gain_tiles = jnp.pad(ggain.reshape(n_dp, n_f, 1, d_rows), ((0, 0), (0, 0), (0, 7), (0, 128 - d_rows)))
    tile = own * slots
    g_normed, gin, gain_tiles = pl.pallas_call(
        functools.partial(scatter_kernel, n_dp=n_dp, n_f=n_f),
        in_specs=[hbm] * 3,
        out_specs=[hbm] * 3,
        out_shape=[
            like((n_dp, tile, model), BF16), like((n_f, d_rows, 2 * width), BF16), like((n_f, 8, 128), F32),
        ],
        scratch_shapes=[pltpu.VMEM((n_z, n_dp, tile, model), BF16)] * 4
        + [
            pltpu.VMEM((n_dp, tile, model), BF16), pltpu.VMEM((n_dp, n_f, d_rows, 2 * width), BF16),
            pltpu.VMEM((n_f, d_rows, 2 * width), BF16), pltpu.VMEM((n_dp, n_f, 8, 128), F32),
            pltpu.VMEM((n_f, 8, 128), F32), dma((n_z + 2, n_dp)),
        ]
        + [dma((n_z, n_dp))] * 6
        + [dma((n_dp,))] * 4
        + [dma((n_f,))] * 2
        + [dma((n_dp,))] * 2
        + [dma((n_f,))] * 2,
        compiler_params=pltpu.CompilerParams(collective_id=4, has_side_effects=True, vmem_limit_bytes=VMEM_BYTES),
        cost_estimate=cost(92),
        name="scatter",
    )(gnorm, gin.reshape(n_dp, n_f, d_rows, 2 * width), gain_tiles)

    hidden = tokens.astype(F32)
    upstream = cotangent.astype(F32)
    output = (hidden + jnp.where(own_mask[:, :, None], branch.astype(F32), 0.0)).astype(BF16)
    g_normed = g_normed.reshape(n_dp, own, slots, model).transpose(0, 2, 1, 3).reshape(seqs, own, model).astype(F32)
    factor = lax.rsqrt(jnp.mean(hidden * hidden, axis=-1, keepdims=True) + EPSILON)
    weighted = gain * g_normed
    input_grad = (
        upstream + factor * weighted - hidden * factor**3 * jnp.mean(hidden * weighted, axis=-1, keepdims=True)
    ).astype(BF16)
    gain_grad = jnp.sum(gain_tiles[:, 0, :d_rows], axis=0)
    gin = gin.reshape(n_f, d_rows, 2, n_dp, inner_rows).transpose(1, 2, 3, 0, 4).reshape(d_rows, -1).astype(F32)
    cuts = [model, proj_cols, rank, states, 4, 1, 1, 1]
    pieces, start = [], 0
    for cut in cuts:
        pieces.append(small[:, start : start + cut])
        start += cut
    gout, gsel, grank, gdec, gcw, gcb, gbias, gskip = pieces
    return (
        output, input_grad, gain_grad, gin, gcw, gcb[:, 0], gsel, grank, gbias[:, 0], gdec, gskip[:, 0], gout,
    )


def solution(mesh):
    rows1, rows2, pos = P(BOTH), P(BOTH, None), P(None, BOTH, None)
    return jax.shard_map(
        functools.partial(body, n_dp=mesh.shape["dp"], n_f=mesh.shape["fsdp"]),
        mesh=mesh,
        in_specs=(pos, pos, P(), P(), rows1, rows2, rows2, rows1, rows2, rows2, rows1, rows2, rows1, rows2),
        out_specs=(pos, pos, rows1, rows2, rows2, rows1, rows2, rows2, rows1, rows2, rows1, rows2),
        check_vma=False,
    )
```

```python
import functools
import jax
import jax.numpy as jnp
from jax import lax
from jax.experimental import pallas as pl
from jax.experimental.pallas import tpu as pltpu
from jax.sharding import PartitionSpec as P

EPSILON = 1e-05
STEPS = 32
PAIR = 2
LAG = 4
LANES = 8
TOGETHER = 8
LOG2E = 1.4426950408889634
BOTH = ("dp", "fsdp")
F32 = jnp.float32
BF16 = jnp.bfloat16
VMEM_BYTES = 60 * 1024 * 1024
FULL_VMEM = 63 * 1024 * 1024
DECAY, TAPS, CONV_BIAS, DT_BIAS, SKIP = 32, 48, 52, 53, 54


def dot(a, b, dims=((1,), (0,))):
    return lax.dot_general(a, b, (dims, ((), ())), preferred_element_type=F32)


def sigmoid(v):
    return 1.0 / (1.0 + jnp.exp(-v))


def softplus(v):
    return jnp.maximum(v, 0.0) + jnp.log1p(jnp.exp(-jnp.abs(v)))


def rms_normed(x, gain):
    factor = lax.rsqrt(jnp.mean(x * x, axis=-1, keepdims=True) + EPSILON)
    return (x * factor * gain).astype(BF16)


def front_kernel(
    x_ref, gain_ref, win_ref, xw_ref, misc_ref, inner_ref, gate_ref, inp_ref, proj_ref, pad_ref, misc_scr, *, slots, length
):
    rows = x_ref.shape[0]
    width = inner_ref.shape[1]
    halo = 3 * slots
    normed = rms_normed(x_ref[...].astype(F32), gain_ref[...])
    both = dot(normed, win_ref[...])
    gate_ref[...] = both[:, width:]
    inner = both[:, :width]
    inner_ref[...] = inner

    @pl.when(pl.program_id(0) == 0)
    def _():
        pad_ref[0:halo, :] = jnp.zeros((halo, width), F32)
        misc_scr[...] = jnp.transpose(misc_ref[...].astype(F32))

    pad_ref[halo : halo + rows, :] = inner
    total = jnp.broadcast_to(misc_scr[CONV_BIAS : CONV_BIAS + 1, :], (rows, width))
    for tap in range(4):
        total = total + misc_scr[TAPS + tap : TAPS + tap + 1, :] * pad_ref[tap * slots : tap * slots + rows, :]
    inp = (total * sigmoid(total)).astype(BF16)
    inp_ref[...] = inp
    pack_rows(proj_ref, dot(inp, xw_ref[...]), dot(inp, misc_ref[...])[:, :DECAY], length)
    pad_ref[0:halo, :] = pad_ref[rows : rows + halo, :]


def spread_lanes(bc_ref, out_ref, k, slots, steps):
    for j in range(PAIR):
        t = jnp.minimum(k * PAIR + j, steps - 1)
        at = pl.ds(pl.multiple_of(t * slots, slots), slots)
        for n in range(out_ref.shape[1]):
            out_ref[j, n] = jnp.broadcast_to(bc_ref[at, n : n + 1], (slots, 128))


def widen(piece, width):
    return jnp.concatenate([piece] * (width // 128), axis=1)


def narrow(value):
    total = value[:, :128]
    for first in range(128, value.shape[1], 128):
        total = total + value[:, first : first + 128]
    return total


def mix_kernel(
    dtl_ref, bc_ref, inp_ref, gate_ref, dtw_ref, misc_ref, ow_ref,
    y_ref, ck_ref, br_ref, h_scr, delta_scr, u_scr, rate_scr, even_scr, odd_scr, misc_scr, *, slots
):
    rows, width = inp_ref.shape
    steps = rows // slots
    states = h_scr.shape[0]

    @pl.when(pl.program_id(0) == 0)
    def _():
        h_scr[...] = jnp.zeros_like(h_scr)
        misc_scr[...] = jnp.transpose(misc_ref[...].astype(F32))
        for n in range(states):
            rate_scr[n] = jnp.broadcast_to(-jnp.exp(misc_scr[DECAY + n : DECAY + n + 1, :]) * LOG2E, (slots, width))

    ck_ref[0] = h_scr[...]
    delta = softplus(dot(dtl_ref[...], dtw_ref[...], ((1,), (1,))) + misc_scr[DT_BIAS : DT_BIAS + 1, :])
    delta_scr[...] = delta
    u_scr[...] = delta * inp_ref[...].astype(F32)
    spread_lanes(bc_ref, even_scr, 0, slots, steps)

    def step(k, bcb_scr, next_scr):
        spread_lanes(bc_ref, next_scr, k + 1, slots, steps)
        ats, ds, us, ys = [], [], [], []
        for j in range(PAIR):
            at = pl.ds(pl.multiple_of((k * PAIR + j) * slots, slots), slots)
            ats.append(at)
            ds.append(delta_scr[at, :])
            us.append(u_scr[at, :])
            ys.append(None)
        for n in range(states):
            rate = rate_scr[n]
            h = h_scr[n]
            for j in range(PAIR):
                h = jnp.exp2(ds[j] * rate) * h + us[j] * widen(bcb_scr[j, n], width)
                term = h * widen(bcb_scr[j, states + n], width)
                ys[j] = term if n == 0 else ys[j] + term
            h_scr[n] = h
        for j in range(PAIR):
            y_ref[ats[j], :] = ys[j]

    def steps_twice(k, carry):
        step(2 * k, even_scr, odd_scr)
        step(2 * k + 1, odd_scr, even_scr)
        return carry

    lax.fori_loop(0, steps // PAIR // 2, steps_twice, 0)
    y = y_ref[...] + misc_scr[SKIP : SKIP + 1, :] * inp_ref[...].astype(F32)
    y_ref[...] = y
    gate = gate_ref[...]
    gated = (y * (gate * sigmoid(gate))).astype(BF16)
    br_ref[...] = dot(gated, ow_ref[...]).astype(br_ref.dtype).reshape(br_ref.shape)


def lane_sums(parts):
    lane = lax.broadcasted_iota(jnp.int32, parts[0].shape, 1)
    bit = 1
    while len(parts) > 1:
        low = (lane & bit) == 0
        merged = []
        for j in range(0, len(parts), 2):
            kept = jnp.where(low, parts[j], parts[j + 1])
            moved = jnp.where(low, parts[j + 1], parts[j])
            merged.append(kept + pltpu.roll(moved, bit, 1))
        parts = merged
        bit *= 2
    total = parts[0]
    while bit < total.shape[1]:
        total = total + pltpu.roll(total, bit, 1)
        bit *= 2
    return total


def back_kernel(
    gb_ref, dtl_ref, bc_ref, inp_ref, gate_ref, y_ref, ck_ref, dtw_ref, misc_ref, ow_ref,
    gis_ref, ggate_ref, gproj_ref, gout_ref, gmisc_ref,
    lam_scr, dacc_scr, sacc_scr, bacc_scr, rate_scr, delta_scr, u_scr, gy_scr, gu_scr, gd_scr, h_scr, a_scr, gbt_scr,
    even_scr, odd_scr, sums_scr, h_now, gbc_ref, misc_scr, back_scr, gout_scr, *, slots, length
):
    rows, width = inp_ref.shape
    steps = rows // slots
    states = lam_scr.shape[0]
    rank = dtl_ref.shape[1]
    step_id = pl.program_id(0)

    @pl.when(step_id == 0)
    def _():
        lam_scr[...] = jnp.zeros_like(lam_scr)
        dacc_scr[...] = jnp.zeros_like(dacc_scr)
        sacc_scr[...] = jnp.zeros_like(sacc_scr)
        bacc_scr[...] = jnp.zeros_like(bacc_scr)
        gout_scr[...] = jnp.zeros_like(gout_scr)
        gmisc_ref[...] = jnp.zeros_like(gmisc_ref)
        misc_scr[...] = jnp.transpose(misc_ref[...].astype(F32))
        for n in range(states):
            rate_scr[n] = jnp.broadcast_to(-jnp.exp(misc_scr[DECAY + n : DECAY + n + 1, :]) * LOG2E, (slots, width))

    gb = gb_ref[...].reshape(rows, gb_ref.shape[-1])
    gate = gate_ref[...]
    sig = sigmoid(gate)
    silu = gate * sig
    y = y_ref[...]
    inp = inp_ref[...].astype(F32)
    g_gated = dot(gb, ow_ref[...], ((1,), (1,)))
    g_y = g_gated * silu
    gy_scr[...] = g_y
    ggate_ref[...] = (g_gated * y * (sig * (1.0 + gate * (1.0 - sig)))).astype(BF16)
    gout_scr[...] += dot((y * silu).astype(BF16), gb, ((0,), (0,)))
    sacc_scr[...] += jnp.sum((g_y * inp).reshape(steps, slots, width), axis=0)
    z = dot(dtl_ref[...], dtw_ref[...], ((1,), (1,))) + misc_scr[DT_BIAS : DT_BIAS + 1, :]
    delta = softplus(z)
    delta_scr[...] = delta
    u_scr[...] = delta * inp

    last = steps // PAIR - 1
    spread_lanes(bc_ref, even_scr, 0, slots, steps)
    h_now[...] = ck_ref[0]

    def replay(k, bcb_scr, next_scr):
        spread_lanes(bc_ref, next_scr, k + 1, slots, steps)
        ds, us, gys = [], [], []
        for j in range(PAIR):
            at = pl.ds(pl.multiple_of((k * PAIR + j) * slots, slots), slots)
            ds.append(delta_scr[at, :])
            us.append(u_scr[at, :])
            gys.append(gy_scr[at, :])
        for n in range(states):
            rate = rate_scr[n]
            h = h_now[n]
            for j in range(PAIR):
                t = k * PAIR + j
                h_scr[t, n] = h
                decay = jnp.exp2(ds[j] * rate)
                a_scr[t, n] = decay
                h = decay * h + us[j] * widen(bcb_scr[j, n], width)
                gbt_scr[states + n, pl.ds(pl.multiple_of(t * slots, slots), slots), :] = narrow(h * gys[j])
            h_now[n] = h

    def replay_twice(k, carry):
        replay(2 * k, even_scr, odd_scr)
        replay(2 * k + 1, odd_scr, even_scr)
        return carry

    lax.fori_loop(0, steps // PAIR // 2, replay_twice, 0)
    spread_lanes(bc_ref, even_scr, last, slots, steps)

    def reverse(k, bcb_scr, next_scr):
        spread_lanes(bc_ref, next_scr, jnp.maximum(k - 1, 0), slots, steps)
        ats, ds, us, gys, gus, gds, ts = [], [], [], [], [], [], []
        for j in range(PAIR):
            t = k * PAIR + j
            at = pl.ds(pl.multiple_of(t * slots, slots), slots)
            ts.append(t)
            ats.append(at)
            ds.append(delta_scr[at, :])
            us.append(u_scr[at, :])
            gys.append(gy_scr[at, :])
            gus.append(None)
            gds.append(None)
        for n in range(states):
            rate = rate_scr[n]
            carried = lam_scr[n]
            total = dacc_scr[n]
            for j in reversed(range(PAIR)):
                t = ts[j]
                lam = carried + gys[j] * widen(bcb_scr[j, states + n], width)
                term = lam * widen(bcb_scr[j, n], width)
                gus[j] = term if n == 0 else gus[j] + term
                gbt_scr[n, ats[j], :] = narrow(lam * us[j])
                carried = a_scr[t, n] * lam
                q = carried * h_scr[t, n]
                term = q * rate
                gds[j] = term if n == 0 else gds[j] + term
                total = total + q * ds[j]
            lam_scr[n] = carried
            dacc_scr[n] = total
        for j in range(PAIR):
            gu_scr[ats[j], :] = gus[j]
            gd_scr[ats[j], :] = gds[j]

    def reverse_twice(i, carry):
        k = last - 2 * i
        reverse(k, even_scr, odd_scr)
        reverse(k - 1, odd_scr, even_scr)
        return carry

    lax.fori_loop(0, steps // PAIR // 2, reverse_twice, 0)

    def reduce_lanes(k, carry):
        for j in range(LANES):
            n = k * LANES + j
            sums_scr[pl.ds(n, 1), :] = jnp.sum(jnp.transpose(gbt_scr[n]), axis=0, keepdims=True)
        return carry

    lax.fori_loop(0, 2 * states // LANES, reduce_lanes, 0)
    gbc_ref[...] = jnp.transpose(sums_scr[...])
    gu = gu_scr[...]
    gis_ref[...] = gu * delta_scr[...] + misc_scr[SKIP : SKIP + 1, :] * gy_scr[...]
    g_pre = (gd_scr[...] * (1.0 / LOG2E) + gu * inp) * sigmoid(z)
    bacc_scr[...] += jnp.sum(g_pre.reshape(steps, slots, width), axis=0)
    g_low = g_pre.astype(BF16)
    gmisc_ref[:, :rank] += dot(g_low, dtl_ref[...], ((0,), (0,)))
    pack_rows(gproj_ref, dot(g_low, dtw_ref[...]), gbc_ref[...], length)

    @pl.when(step_id == pl.num_programs(0) - 1)
    def _():
        back_scr[...] = jnp.zeros_like(back_scr)
        for n in range(states):
            rate = -jnp.exp(misc_scr[DECAY + n : DECAY + n + 1, :])
            back_scr[DECAY + n : DECAY + n + 1, :] = jnp.sum(dacc_scr[n], axis=0, keepdims=True) * rate
        back_scr[SKIP : SKIP + 1, :] = jnp.sum(sacc_scr[...], axis=0, keepdims=True)
        back_scr[DT_BIAS : DT_BIAS + 1, :] = jnp.sum(bacc_scr[...], axis=0, keepdims=True)
        gmisc_ref[:, rank:] = jnp.transpose(back_scr[...])
        gout_ref[...] = gout_scr[...].astype(gout_ref.dtype)


def remote(src, dst, send, recv, where):
    return pltpu.make_async_remote_copy(
        src_ref=src, dst_ref=dst, send_sem=send, recv_sem=recv, device_id=where, device_id_type=pl.DeviceIdType.MESH
    )


def gather_kernel(
    tok_ref, cot_ref, win_ref, gain_ref, pk_ref, x_ref, c_ref, w_ref, g_ref, p_ref,
    tok_buf, cot_buf, win_buf, gain_buf, pk_buf, local_sem,
    tdp_send, tdp_recv, cdp_send, cdp_recv, up_send, up_recv, down_send, down_recv, core_send, core_recv,
    w1_send, w1_recv, w2_send, w2_recv, g1_send, g1_recv, g2_send, g2_recv, p_send, p_recv, *, n_dp, n_f
):
    d = lax.axis_index("dp")
    f = lax.axis_index("fsdp")
    n_z = n_f // 2
    z = f // 2
    core = f % 2
    partner = z * 2 + (1 - core)

    barrier = pltpu.get_barrier_semaphore()
    for k in range(1, n_f):
        pl.semaphore_signal(barrier, inc=1, device_id=(d, (f + k) % n_f), device_id_type=pl.DeviceIdType.MESH)
    for k in range(1, n_dp):
        pl.semaphore_signal(barrier, inc=1, device_id=((d + k) % n_dp, f), device_id_type=pl.DeviceIdType.MESH)
    pl.semaphore_wait(barrier, n_f + n_dp - 2)

    loads = (
        pltpu.make_async_copy(tok_ref.at[d], tok_buf, local_sem.at[0]),
        pltpu.make_async_copy(win_ref.at[f], win_buf, local_sem.at[1]),
        pltpu.make_async_copy(gain_ref, gain_buf, local_sem.at[2]),
        pltpu.make_async_copy(pk_ref, pk_buf, local_sem.at[3]),
        pltpu.make_async_copy(cot_ref.at[d], cot_buf, local_sem.at[8]),
    )
    stores = (
        pltpu.make_async_copy(tok_buf, x_ref.at[d, f], local_sem.at[4]),
        pltpu.make_async_copy(win_buf, w_ref.at[d, f], local_sem.at[5]),
        pltpu.make_async_copy(gain_buf, g_ref.at[d, f], local_sem.at[6]),
        pltpu.make_async_copy(pk_buf, p_ref.at[d], local_sem.at[7]),
        pltpu.make_async_copy(cot_buf, c_ref.at[d], local_sem.at[9]),
    )
    for load in loads:
        load.start()

    def tok_dp(k):
        to = (d + k) % n_dp
        return remote(tok_ref.at[to], x_ref.at[d, f], tdp_send.at[k], tdp_recv.at[k], (to, f))

    def tok_dp_arrival(k):
        src = (d - k + n_dp) % n_dp
        return remote(tok_ref.at[d], x_ref.at[src, f], tdp_send.at[k], tdp_recv.at[k], (src, f))

    def cot_dp(k):
        to = (d + k) % n_dp
        return remote(cot_ref.at[to], c_ref.at[d], cdp_send.at[k], cdp_recv.at[k], (to, f))

    def cot_dp_arrival(k):
        src = (d - k + n_dp) % n_dp
        return remote(cot_ref.at[d], c_ref.at[src], cdp_send.at[k], cdp_recv.at[k], (src, f))

    def w1(k):
        to = (f + k) % n_f
        return remote(win_ref.at[to], w_ref.at[d, f], w1_send.at[k], w1_recv.at[k], (d, to))

    def w1_arrival(k):
        src = (f - k + n_f) % n_f
        return remote(win_ref.at[f], w_ref.at[d, src], w1_send.at[k], w1_recv.at[k], (d, src))

    def g1(k):
        to = (f + k) % n_f
        return remote(gain_ref, g_ref.at[d, f], g1_send.at[k], g1_recv.at[k], (d, to))

    def g1_arrival(k):
        src = (f - k + n_f) % n_f
        return remote(gain_ref, g_ref.at[d, src], g1_send.at[k], g1_recv.at[k], (d, src))

    def w2(k):
        to = (d + k) % n_dp
        return remote(w_ref.at[d], w_ref.at[d], w2_send.at[k], w2_recv.at[k], (to, f))

    def w2_arrival(k):
        src = (d - k + n_dp) % n_dp
        return remote(w_ref.at[src], w_ref.at[src], w2_send.at[k], w2_recv.at[k], (src, f))

    def g2(k):
        to = (d + k) % n_dp
        return remote(g_ref.at[d], g_ref.at[d], g2_send.at[k], g2_recv.at[k], (to, f))

    def g2_arrival(k):
        src = (d - k + n_dp) % n_dp
        return remote(g_ref.at[src], g_ref.at[src], g2_send.at[k], g2_recv.at[k], (src, f))

    def pk(k):
        to = (d + k) % n_dp
        return remote(pk_ref, p_ref.at[d], p_send.at[k], p_recv.at[k], (to, f))

    def pk_arrival(k):
        src = (d - k + n_dp) % n_dp
        return remote(pk_ref, p_ref.at[src], p_send.at[k], p_recv.at[k], (src, f))

    def block(j, origin, side):
        at = (d - j + n_dp) % n_dp
        return x_ref.at[at, origin * 2 + side]

    def up(j, origin, src=None):
        ref = block(j, origin, core)
        return remote(ref if src is None else src, ref, up_send.at[origin, j], up_recv.at[origin, j], (d, f + 2))

    def down(j, origin, src=None):
        ref = block(j, origin, core)
        return remote(ref if src is None else src, ref, down_send.at[origin, j], down_recv.at[origin, j], (d, f - 2))

    def across(j, origin, src=None):
        ref = block(j, origin, core)
        return remote(
            ref if src is None else src, ref, core_send.at[origin, j], core_recv.at[origin, j], (d, partner)
        )

    def across_arrival(j, origin):
        ref = block(j, origin, 1 - core)
        return remote(ref, ref, core_send.at[origin, j], core_recv.at[origin, j], (d, partner))

    def launch(j, src=None):
        @pl.when(z < n_z - 1)
        def _():
            up(j, z, src).start()

        @pl.when(z > 0)
        def _():
            down(j, z, src).start()

        across(j, z, src).start()

    for k in range(1, n_f):
        w1(k).start()
    for k in range(1, n_dp):
        tok_dp(k).start()
    launch(0, tok_ref.at[d])
    for k in range(1, n_f):
        g1(k).start()
    for k in range(1, n_dp):
        pk(k).start()
    for k in range(1, n_dp):
        cot_dp(k).start()
    for load, store in zip(loads, stores):
        load.wait()
        store.start()
    for k in range(1, n_dp):
        tok_dp_arrival(k).wait_recv()
        launch(k)
    for store in stores:
        store.wait()
    for k in range(1, n_f):
        w1_arrival(k).wait_recv()
        g1_arrival(k).wait_recv()
    for k in range(1, n_dp):
        w2(k).start()
        g2(k).start()
    for far in range(1, n_z):
        for j in range(n_dp):

            @pl.when(z >= far)
            def _():
                origin = z - far
                up(j, origin).wait_recv()

                @pl.when(z < n_z - 1)
                def _():
                    up(j, origin).start()

                across(j, origin).start()

            @pl.when(z + far < n_z)
            def _():
                origin = z + far
                down(j, origin).wait_recv()

                @pl.when(z > 0)
                def _():
                    down(j, origin).start()

                across(j, origin).start()

    for origin in range(n_z):
        for j in range(n_dp):
            across_arrival(j, origin).wait_recv()
            across(j, origin).wait_send()
    for origin in range(n_z):
        for j in range(n_dp):

            @pl.when((origin <= z) & (z < n_z - 1))
            def _():
                up(j, origin).wait_send()

            @pl.when((origin >= z) & (z > 0))
            def _():
                down(j, origin).wait_send()

    for k in range(1, n_dp):
        pk_arrival(k).wait_recv()
        cot_dp_arrival(k).wait_recv()
        cot_dp(k).wait_send()
        w2_arrival(k).wait_recv()
        g2_arrival(k).wait_recv()
        tok_dp(k).wait_send()
        w2(k).wait_send()
        g2(k).wait_send()
        pk(k).wait_send()
    for k in range(1, n_f):
        w1(k).wait_send()
        g1(k).wait_send()


def pack_rows(out_ref, main, rest, chunk):
    part = chunk // 4
    for q in range(main.shape[0] // chunk):
        out_ref[q, 0:chunk, :] = main[q * chunk : (q + 1) * chunk, :]
        for j in range(4):
            first = q * chunk + j * part
            out_ref[q, chunk : chunk + part, j * 32 : (j + 1) * 32] = rest[first : first + part, :]


def combine_kernel(
    part_ref, main_ref, rest_ref, one, sums, two, tops, rests,
    one_send, one_recv, two_send, two_recv, top_send, top_recv, rest_send, rest_recv,
    ctop_send, ctop_recv, crest_send, crest_recv, *, n_dp, n_f
):
    d = lax.axis_index("dp")
    f = lax.axis_index("fsdp")
    n_z = n_f // 2
    z = f // 2
    core = f % 2
    other = 1 - core
    partner = z * 2 + other
    chunk = tops.shape[2]

    barrier = pltpu.get_barrier_semaphore()
    pl.semaphore_signal(barrier, inc=1, device_id=(d, partner), device_id_type=pl.DeviceIdType.MESH)
    for k in range(1, n_z):
        pl.semaphore_signal(
            barrier, inc=1, device_id=(d, (z + k) % n_z * 2 + core), device_id_type=pl.DeviceIdType.MESH
        )
    pl.semaphore_wait(barrier, n_z)

    def first(k):
        to = (z + k) % n_z
        return remote(part_ref.at[to, other], one.at[to], one_send.at[k], one_recv.at[k], (d, partner))

    def second(k):
        to = (z + k) % n_z
        return remote(sums.at[to], two.at[k], two_send.at[k], two_recv.at[k], (d, to * 2 + core))

    def third(k):
        to = ((z + k) % n_z * 2 + core,)
        return (
            remote(tops.at[z, core], tops.at[z, core], top_send.at[k], top_recv.at[k], (d,) + to),
            remote(rests.at[z, core], rests.at[z, core], rest_send.at[k], rest_recv.at[k], (d,) + to),
        )

    def third_arrival(k):
        src = (z - k + n_z) % n_z
        to = (src * 2 + core,)
        return (
            remote(tops.at[src, core], tops.at[src, core], top_send.at[k], top_recv.at[k], (d,) + to),
            remote(rests.at[src, core], rests.at[src, core], rest_send.at[k], rest_recv.at[k], (d,) + to),
        )

    def fourth(k, side):
        src = (z - k + n_z) % n_z
        return (
            remote(tops.at[src, side], tops.at[src, side], ctop_send.at[k], ctop_recv.at[k], (d, partner)),
            remote(rests.at[src, side], rests.at[src, side], crest_send.at[k], crest_recv.at[k], (d, partner)),
        )

    order = list(range(1, n_z)) + [0]
    for k in order:
        first(k).start()
    for k in order:
        to = (z + k) % n_z
        first(k).wait_recv()
        sums[to] = (part_ref[to, core] + one[to]).astype(sums.dtype)
        if k:
            second(k).start()
    total = part_ref[z, core] + one[z]
    for k in range(1, n_z):
        second(k).wait_recv()
        total = total + two[k].astype(F32)
    tops[z, core] = total[0:chunk, :].astype(tops.dtype)
    rests[z, core] = total[chunk:, :].astype(rests.dtype)
    for k in range(1, n_z):
        for copy in third(k):
            copy.start()
    for copy in fourth(0, core):
        copy.start()
    for k in range(1, n_z):
        for copy in third_arrival(k):
            copy.wait_recv()
        for copy in fourth(k, core):
            copy.start()
    for k in range(n_z):
        for copy in fourth(k, other):
            copy.wait_recv()
    part = chunk // 4
    for a in range(n_z):
        for b in range(2):
            at = (a * 2 + b) * chunk
            main_ref[at : at + chunk, :] = tops[a, b]
            rest = rests[a, b]
            for j in range(4):
                rest_ref[at + j * part : at + (j + 1) * part, :] = rest[:, j * 32 : (j + 1) * 32]
    for k in range(n_z):
        first(k).wait_send()
        for copy in fourth(k, core):
            copy.wait_send()
        if k:
            second(k).wait_send()
            for copy in third(k):
                copy.wait_send()


def finish_kernel(
    gdtl_ref, gbc_ref, inp_ref, gis_ref, ggate_ref, inner_ref, before_ref, x_ref, gain_ref, win_ref, xw_ref, misc_ref,
    gout_ref, gback_ref, out_ref, gin_out, gout_out, gback_out, gtail_out, gg_out,
    misc_scr, tail_scr, gin_scr, gsel_scr, grest_scr, ggain_scr, pad_scr, gpad_scr, wacc_scr, cacc_scr,
    mine, theirs, passed, gin_low, gin_got, gin_sum, gin_all, gout_got, gback_got, gtail_low, gtail_got,
    gg_low, gg_got, gg_sum, gg_all, local_sem,
    one_send, one_recv, up_send, up_recv, down_send, down_recv, dp_send, dp_recv,
    w_send, w_recv, o_send, o_recv, b_send, b_recv, t_send, t_recv, g_send, g_recv,
    w2_send, w2_recv, g2_send, g2_recv, *, slots, n_dp, n_f
):
    d = lax.axis_index("dp")
    f = lax.axis_index("fsdp")
    n_z = n_f // 2
    z = f // 2
    core = f % 2
    other = 1 - core
    partner = z * 2 + other
    rows, width = inp_ref.shape
    steps = rows // slots
    halo = 3 * slots
    i = pl.program_id(0)
    blocks = mine.shape[0] * mine.shape[1] * mine.shape[2] // rows
    last = blocks - 1
    tile = mine.shape[2]
    held = rows // tile
    per = n_f // held
    pairs = held // 2
    rank = gdtl_ref.shape[1]
    d_rows, inner_rows = gin_out.shape[0], gout_out.shape[0]

    def place(q):
        return (last - q) // per, (last - q) % per * pairs

    def one(to, j):
        return remote(
            mine.at[to * 2 + other, j], theirs.at[to, j], one_send.at[to, j], one_recv.at[to, j], (d, partner)
        )

    def up(to, j):
        return remote(
            mine.at[to * 2 + core, j], passed.at[to + 1, j], up_send.at[to, j], up_recv.at[to, j], (d, f + 2)
        )

    def down(to, j):
        return remote(
            mine.at[to * 2 + core, j], passed.at[to, j], down_send.at[to, j], down_recv.at[to, j], (d, f - 2)
        )

    def dp(k):
        to = (d + k) % n_dp
        return remote(mine.at[f, to], out_ref.at[d], dp_send.at[k], dp_recv.at[k], (to, f))

    def dp_arrival(k):
        src = (d - k + n_dp) % n_dp
        return remote(mine.at[f, src], out_ref.at[src], dp_send.at[k], dp_recv.at[k], (src, f))

    def over_dp(src, dst, send, recv):
        return [
            remote(src.at[(d + k) % n_dp], dst.at[k], send.at[k], recv.at[k], ((d + k) % n_dp, f))
            for k in range(1, n_dp)
        ]

    def over_f(src, dst, send, recv, k):
        to = (f + k) % n_f
        return remote(src.at[to], dst.at[f], send.at[k], recv.at[k], (d, to))

    def over_f_arrival(src, dst, send, recv, k):
        to = (f - k + n_f) % n_f
        return remote(src.at[to], dst.at[to], send.at[k], recv.at[k], (d, to))

    outs = lambda: over_dp(gout_ref, gout_got, o_send, o_recv)
    backs = lambda: over_dp(gback_ref, gback_got, b_send, b_recv)
    ins = lambda: over_dp(gin_low, gin_got, w_send, w_recv)
    tails = lambda: over_dp(gtail_low, gtail_got, t_send, t_recv)
    gains = lambda: over_dp(gg_low, gg_got, g_send, g_recv)
    own_out = pltpu.make_async_copy(gout_ref.at[d], gout_got.at[0], local_sem.at[0])
    own_back = pltpu.make_async_copy(gback_ref.at[d], gback_got.at[0], local_sem.at[1])
    put = pltpu.make_async_copy(mine.at[f, d], out_ref.at[d], local_sem.at[2])

    def send_halves(q):
        j, first = place(q)
        for a in range(pairs):
            one(first + a, j).start()

    def pair(to, j):
        one(to, j).wait_recv()
        return mine[to * 2 + core, j].astype(F32) + theirs[to, j].astype(F32)

    def hops(step):
        q_up = step - 1 - LAG * z
        q_down = step - 1 - LAG * (n_z - 1 - z)
        q_end = step - 1 - LAG * jnp.maximum(z, n_z - 1 - z)

        @pl.when((q_up >= 0) & (q_up < blocks))
        def _():
            j, first = place(q_up)
            for a in range(pairs):
                to = first + a

                @pl.when(to > z)
                def _():
                    mine[to * 2 + core, j] = pair(to, j).astype(mine.dtype)

                    @pl.when(z > 0)
                    def _():
                        up(to, j).wait_recv()
                        mine[to * 2 + core, j] = (
                            mine[to * 2 + core, j].astype(F32) + passed[to + 1, j].astype(F32)
                        ).astype(mine.dtype)

            for a in range(pairs):

                @pl.when(first + a > z)
                def _():
                    up(first + a, j).start()

        @pl.when((q_down >= 0) & (q_down < blocks))
        def _():
            j, first = place(q_down)
            for a in range(pairs):
                to = first + a

                @pl.when(to < z)
                def _():
                    mine[to * 2 + core, j] = pair(to, j).astype(mine.dtype)

                    @pl.when(z < n_z - 1)
                    def _():
                        down(to, j).wait_recv()
                        mine[to * 2 + core, j] = (
                            mine[to * 2 + core, j].astype(F32) + passed[to, j].astype(F32)
                        ).astype(mine.dtype)

            for a in range(pairs):

                @pl.when(first + a < z)
                def _():
                    down(first + a, j).start()

        @pl.when((q_end >= 0) & (q_end < blocks))
        def _():
            j, first = place(q_end)

            @pl.when((z >= first) & (z < first + pairs))
            def _():
                mine[f, j] = pair(z, j).astype(mine.dtype)

                @pl.when(z > 0)
                def _():
                    up(z, j).wait_recv()
                    mine[f, j] = (mine[f, j].astype(F32) + passed[z + 1, j].astype(F32)).astype(mine.dtype)

                @pl.when(z < n_z - 1)
                def _():
                    down(z, j).wait_recv()
                    mine[f, j] = (mine[f, j].astype(F32) + passed[z, j].astype(F32)).astype(mine.dtype)

                for k in range(n_dp):

                    @pl.when(j == (d + k) % n_dp)
                    def _():
                        if k:
                            dp(k).start()
                        else:
                            put.start()

    @pl.when(i == 0)
    def _():
        barrier = pltpu.get_barrier_semaphore()
        for k in range(1, n_f):
            pl.semaphore_signal(barrier, inc=1, device_id=(d, (f + k) % n_f), device_id_type=pl.DeviceIdType.MESH)
        for k in range(1, n_dp):
            pl.semaphore_signal(barrier, inc=1, device_id=((d + k) % n_dp, f), device_id_type=pl.DeviceIdType.MESH)
        pl.semaphore_wait(barrier, n_f + n_dp - 2)
        for copy in outs() + backs():
            copy.start()
        own_out.start()
        own_back.start()
        gpad_scr[rows : rows + halo, :] = jnp.zeros((halo, width), F32)
        wacc_scr[...] = jnp.zeros_like(wacc_scr)
        cacc_scr[...] = jnp.zeros_like(cacc_scr)
        gin_scr[...] = jnp.zeros_like(gin_scr)
        gsel_scr[...] = jnp.zeros_like(gsel_scr)
        grest_scr[...] = jnp.zeros_like(grest_scr)
        ggain_scr[...] = jnp.zeros_like(ggain_scr)
        misc_scr[...] = jnp.transpose(misc_ref[...].astype(F32))

    @pl.when(i > 0)
    def _():
        send_halves(i - 1)

    gdtl = gdtl_ref[...]
    gbc = gbc_ref[...]
    inp = inp_ref[...]
    gsel_scr[...] += dot(inp, gdtl, ((0,), (0,)))
    grest_scr[:, :DECAY] += dot(inp, gbc, ((0,), (0,)))
    g_inputs = (
        gis_ref[...]
        + dot(gdtl, xw_ref[...], ((1,), (1,)))
        + dot(gbc, misc_ref[:, :DECAY], ((1,), (1,)))
    )
    pad_scr[0:halo, :] = before_ref[slots : slots + halo, :] * (i < last).astype(F32)
    pad_scr[halo : halo + rows, :] = inner_ref[...]
    total = jnp.broadcast_to(misc_scr[CONV_BIAS : CONV_BIAS + 1, :], (rows, width))
    for tap in range(4):
        total = total + misc_scr[TAPS + tap : TAPS + tap + 1, :] * pad_scr[tap * slots : tap * slots + rows, :]
    sig = sigmoid(total)
    g_conv = g_inputs * (sig * (1.0 + total * (1.0 - sig)))
    gpad_scr[0:rows, :] = g_conv
    g_inner = jnp.zeros((rows, width), F32)
    for tap in range(4):
        back = (3 - tap) * slots
        g_inner = g_inner + misc_scr[TAPS + tap : TAPS + tap + 1, :] * gpad_scr[back : back + rows, :]
        wacc_scr[tap] += jnp.sum(
            (g_conv * pad_scr[tap * slots : tap * slots + rows, :]).reshape(steps, slots, width), axis=0
        )
    cacc_scr[...] += jnp.sum(g_conv.reshape(steps, slots, width), axis=0)
    gpad_scr[rows : rows + halo, :] = gpad_scr[0:halo, :]
    g_both = jnp.concatenate([g_inner.astype(BF16), ggate_ref[...]], axis=1)
    x = x_ref[...].astype(F32)
    scaled = x * lax.rsqrt(jnp.mean(x * x, axis=-1, keepdims=True) + EPSILON)
    gin_scr[...] += dot((scaled * gain_ref[...]).astype(BF16), g_both, ((0,), (0,)))
    g_normed = dot(g_both, win_ref[...], ((1,), (1,)))
    ggain_scr[...] += jnp.sum(g_normed * scaled, axis=0, keepdims=True)
    block, first = place(i)
    for a in range(held):
        mine[first * 2 + a, block] = g_normed[a * tile : (a + 1) * tile, :].astype(mine.dtype)
    hops(i)

    @pl.when(i == last)
    def _():
        for a in range(n_dp):
            for b in range(n_f):
                at = (a * n_f + b) * d_rows
                gin_low[a, b] = gin_scr[at : at + d_rows, :].astype(gin_low.dtype)
                gg_low[a, b] = jnp.zeros((8, 128), F32)
                gg_low[a, b, 0:1, 0:d_rows] = ggain_scr[:, at : at + d_rows]
        tail_scr[...] = jnp.zeros_like(tail_scr)
        for tap in range(4):
            tail_scr[TAPS + tap : TAPS + tap + 1, :] = jnp.sum(wacc_scr[tap], axis=0, keepdims=True)
        tail_scr[CONV_BIAS : CONV_BIAS + 1, :] = jnp.sum(cacc_scr[...], axis=0, keepdims=True)
        grest_scr[:, DECAY:] = jnp.transpose(tail_scr[...])[:, DECAY:]
        for a in range(n_dp):
            at = a * inner_rows
            gtail_low[a, :, :rank] = gsel_scr[at : at + inner_rows, :]
            gtail_low[a, :, rank:] = grest_scr[at : at + inner_rows, :]
        send_halves(last)
        hops(blocks)
        for copy in ins() + tails() + gains():
            copy.start()
        own_out.wait()
        own_back.wait()
        for copy in outs() + backs():
            copy.wait_recv()
        total = gout_got[0].astype(F32)
        for k in range(1, n_dp):
            total = total + gout_got[k].astype(F32)
        gout_out[...] = total
        total = gback_got[0]
        for k in range(1, n_dp):
            total = total + gback_got[k]
        gback_out[...] = total

        def drain(step, carry):
            hops(step)
            return carry

        lax.fori_loop(blocks + 1, blocks + 1 + LAG * (n_z - 1), drain, 0)

        for copy in ins() + tails() + gains():
            copy.wait_recv()

        def add(q, carry):
            total = gin_low[d, q].astype(F32)
            for k in range(1, n_dp):
                total = total + gin_got[k, q].astype(F32)
            gin_sum[q] = total.astype(gin_sum.dtype)
            total = gg_low[d, q]
            for k in range(1, n_dp):
                total = total + gg_got[k, q]
            gg_sum[q] = total
            return carry

        lax.fori_loop(0, n_f, add, 0)
        for k in range(1, n_f):
            over_f(gin_sum, gin_all, w2_send, w2_recv, k).start()
            over_f(gg_sum, gg_all, g2_send, g2_recv, k).start()
        gin_all[f] = gin_sum[f]
        gg_all[f] = gg_sum[f]
        total = gtail_low[d]
        for k in range(1, n_dp):
            total = total + gtail_got[k]
        gtail_out[...] = total
        for k in range(1, n_f):
            over_f_arrival(gin_sum, gin_all, w2_send, w2_recv, k).wait_recv()
            over_f_arrival(gg_sum, gg_all, g2_send, g2_recv, k).wait_recv()
        total = gg_all[0]
        for b in range(1, n_f):
            total = total + gg_all[b]
        gg_out[...] = total
        for b in range(n_f):
            for h in range(2):
                for a in range(n_dp):
                    to = (h * n_dp + a) * n_f * inner_rows + b * inner_rows
                    at = (h * n_dp + a) * inner_rows
                    gin_out[:, to : to + inner_rows] = gin_all[b, :, at : at + inner_rows].astype(F32)
        for k in range(1, n_dp):
            dp_arrival(k).wait_recv()
            dp(k).wait_send()
        put.wait()
        for copy in outs() + backs() + ins() + tails() + gains():
            copy.wait_send()
        for k in range(1, n_f):
            over_f(gin_sum, gin_all, w2_send, w2_recv, k).wait_send()
            over_f(gg_sum, gg_all, g2_send, g2_recv, k).wait_send()
        for to in range(n_z):
            for j in range(n_dp):
                one(to, j).wait_send()

                @pl.when(z < to)
                def _():
                    up(to, j).wait_send()

                @pl.when(z > to)
                def _():
                    down(to, j).wait_send()


def whole(shape):
    return pl.BlockSpec(shape, lambda i: (0,) * len(shape))


def cost(micros):
    return pl.CostEstimate(flops=int(micros * 1.15e9), bytes_accessed=1 << 20, transcendentals=0)


def params():
    return pltpu.CompilerParams(vmem_limit_bytes=VMEM_BYTES, dimension_semantics=("arbitrary",))


def body(
    tokens, cotangent, lengths, deal_order, norm_gain, in_weight, conv_weight, conv_bias,
    x_weight, dt_weight, dt_bias, decay_log, skip_gain, out_weight, *, n_dp, n_f
):
    seqs, own, model = tokens.shape
    slots = seqs // n_dp
    inner_rows, states = decay_log.shape
    rank = dt_weight.shape[1]
    width = inner_rows * n_dp
    length = own * n_dp * n_f
    d_rows = in_weight.shape[0]
    total_rows = length * slots
    group = lax.axis_index("dp")
    member = lax.axis_index("fsdp")

    low = lambda v: v.astype(BF16)
    slot_ids = jnp.arange(seqs, dtype=jnp.int32)
    seq_len = jnp.sum(jnp.where(deal_order[:, None] == slot_ids[None, :], lengths[:, None], 0), axis=0)
    own_pos = (group * n_f + member) * own + jnp.arange(own, dtype=jnp.int32)
    own_mask = own_pos[None, :] < seq_len[:, None]

    def by_group(v):
        return v.reshape(n_dp, slots, own, model).transpose(0, 2, 1, 3).reshape(n_dp, own * slots, model)

    def collect(v):
        v = lax.psum_scatter(v.reshape(total_rows, model), "fsdp", scatter_dimension=0, tiled=True)
        v = lax.all_to_all(v.reshape(n_dp, own, slots, model), "dp", 0, 0, tiled=True)
        return v.transpose(0, 2, 1, 3).reshape(seqs, own, model)

    masked = by_group(jnp.where(own_mask[:, :, None], cotangent, jnp.zeros_like(cotangent)))

    tok = by_group(tokens)
    win = low(in_weight).reshape(d_rows, 2, n_dp, n_f, inner_rows).transpose(3, 0, 1, 2, 4)
    win = win.reshape(n_f, d_rows, 2 * width)
    gain_tile = jnp.zeros((8, 128), F32).at[0, :d_rows].set(low(norm_gain).astype(F32))
    misc = jnp.concatenate(
        [x_weight[:, rank:], decay_log, conv_weight, conv_bias[:, None], dt_bias[:, None], skip_gain[:, None]], axis=1
    )
    misc = jnp.pad(misc, ((0, 0), (0, 128 - misc.shape[1])))
    packed = low(jnp.concatenate([out_weight, x_weight[:, :rank], misc, dt_weight], axis=1))
    n_z = n_f // 2
    dma = pltpu.SemaphoreType.DMA
    hbm = pl.BlockSpec(memory_space=pl.ANY)
    x, g_branch, win, gain, packed = pl.pallas_call(
        functools.partial(gather_kernel, n_dp=n_dp, n_f=n_f),
        in_specs=[hbm] * 5,
        out_specs=[hbm] * 5,
        out_shape=[
            jax.ShapeDtypeStruct((n_dp, n_f) + tok.shape[1:], BF16),
            jax.ShapeDtypeStruct(tok.shape, BF16),
            jax.ShapeDtypeStruct((n_dp, n_f) + win.shape[1:], BF16),
            jax.ShapeDtypeStruct((n_dp, n_f, 8, 128), F32),
            jax.ShapeDtypeStruct((n_dp,) + packed.shape, BF16),
        ],
        scratch_shapes=[
            pltpu.VMEM(tok.shape[1:], BF16), pltpu.VMEM(tok.shape[1:], BF16), pltpu.VMEM(win.shape[1:], BF16),
            pltpu.VMEM((8, 128), F32), pltpu.VMEM(packed.shape, BF16), dma((10,)),
            dma((n_dp,)), dma((n_dp,)), dma((n_dp,)), dma((n_dp,)),
        ]
        + [dma((n_z, n_dp))] * 6
        + [dma((n_f,)), dma((n_f,)), dma((n_dp,)), dma((n_dp,)), dma((n_f,)), dma((n_f,))]
        + [dma((n_dp,))] * 4,
        compiler_params=pltpu.CompilerParams(collective_id=1, has_side_effects=True),
        cost_estimate=cost(90),
        name="gather",
    )(tok, masked, win, gain_tile, packed)
    g_branch = lax.all_gather(g_branch, "fsdp", axis=0, tiled=False)
    x = x.reshape(total_rows, model)
    win = win.reshape(model, 2 * width)
    gain = gain[:, :, 0, :d_rows].reshape(1, model)
    packed = packed.reshape(width, -1)
    rows = STEPS * slots
    blocks = length // STEPS
    grid = (blocks,)
    row_spec = lambda cols: pl.BlockSpec((rows, cols), lambda i: (i, 0))
    rev_spec = lambda cols: pl.BlockSpec((rows, cols), lambda i: (blocks - 1 - i, 0))
    once = dict(pipeline_mode=pl.Buffered(1))
    ow_spec = pl.BlockSpec((width, model), lambda i: (0, 0), **once)
    xw_spec = pl.BlockSpec((width, 128), lambda i: (0, model // 128), **once)
    misc_spec = pl.BlockSpec((width, 128), lambda i: (0, model // 128 + 1), **once)
    dtw_spec = pl.BlockSpec((width, 128), lambda i: (0, model // 128 + 2), **once)
    win_spec = pl.BlockSpec((model, 2 * width), lambda i: (0, 0), **once)
    misc_shape = pltpu.VMEM((128, width), F32)
    like = jax.ShapeDtypeStruct
    held = STEPS // own
    per = n_f // held
    piece = (held, 1, own * slots, model)
    piece_spec = pl.BlockSpec(piece, lambda i: (i % per, i // per, 0, 0))
    rev_piece_spec = pl.BlockSpec(piece, lambda i: ((blocks - 1 - i) % per, (blocks - 1 - i) // per, 0, 0))
    pieces_shape = like((n_f, n_dp, own * slots, model), BF16)
    packed_rows = length + length // 4
    parts = rows // length
    part_spec = pl.BlockSpec((parts, packed_rows, 128), lambda i: (i, 0, 0))
    rev_part_spec = pl.BlockSpec((parts, packed_rows, 128), lambda i: (blocks - 1 - i, 0, 0))
    parts_shape = like((n_f, packed_rows, 128), F32)

    def combine(v, rest_type, number):
        vmem = pl.BlockSpec(memory_space=pltpu.VMEM)
        return pl.pallas_call(
            functools.partial(combine_kernel, n_dp=n_dp, n_f=n_f),
            in_specs=[vmem],
            out_specs=[vmem, vmem],
            out_shape=[like((total_rows, rank), BF16), like((total_rows, 2 * states), rest_type)],
            scratch_shapes=[
                pltpu.VMEM((n_z, packed_rows, 128), F32), pltpu.VMEM((n_z, packed_rows, 128), BF16),
                pltpu.VMEM((n_z, packed_rows, 128), BF16), pltpu.VMEM((n_z, 2, length, 128), BF16),
                pltpu.VMEM((n_z, 2, length // 4, 128), rest_type),
            ]
            + [dma((n_z,))] * 12,
            compiler_params=pltpu.CompilerParams(
                collective_id=number, has_side_effects=True, vmem_limit_bytes=VMEM_BYTES
            ),
            cost_estimate=cost(28),
        name="combine",
        )(v.reshape(n_z, 2, packed_rows, 128))

    inner, gate, inp, proj = pl.pallas_call(
        functools.partial(front_kernel, slots=slots, length=length),
        grid=grid,
        in_specs=[
            row_spec(model), whole((1, model)), win_spec, xw_spec, misc_spec,
        ],
        out_specs=[row_spec(width), row_spec(width), row_spec(width), part_spec],
        out_shape=[
            like((total_rows, width), F32), like((total_rows, width), F32), like((total_rows, width), BF16),
            parts_shape,
        ],
        scratch_shapes=[pltpu.VMEM((rows + 3 * slots, width), F32), misc_shape],
        compiler_params=params(),
        cost_estimate=cost(20),
        name="front",
    )(x, gain, win, packed, packed)

    dtl, bc = combine(proj, F32, 2)

    y, ck, branch = pl.pallas_call(
        functools.partial(mix_kernel, slots=slots),
        grid=grid,
        in_specs=[
            row_spec(rank), row_spec(2 * states), row_spec(width), row_spec(width), dtw_spec, misc_spec, ow_spec,
        ],
        out_specs=[
            row_spec(width), pl.BlockSpec((1, states, slots, width), lambda i: (i, 0, 0, 0)), piece_spec,
        ],
        out_shape=[
            like((total_rows, width), F32), like((blocks, states, slots, width), F32), pieces_shape,
        ],
        scratch_shapes=[
            pltpu.VMEM((states, slots, width), F32), pltpu.VMEM((rows, width), F32), pltpu.VMEM((rows, width), F32),
            pltpu.VMEM((states, slots, width), F32), pltpu.VMEM((PAIR, 2 * states, slots, 128), F32),
            pltpu.VMEM((PAIR, 2 * states, slots, 128), F32), misc_shape,
        ],
        compiler_params=params(),
        cost_estimate=cost(36),
        name="mix",
    )(dtl, bc, inp, gate, packed, packed, packed)

    gis, ggate, gproj, gout, gmisc = pl.pallas_call(
        functools.partial(back_kernel, slots=slots, length=length),
        grid=grid,
        in_specs=[
            rev_piece_spec, rev_spec(rank), rev_spec(2 * states), rev_spec(width), rev_spec(width), rev_spec(width),
            pl.BlockSpec((1, states, slots, width), lambda i: (blocks - 1 - i, 0, 0, 0)), dtw_spec, misc_spec, ow_spec,
        ],
        out_specs=[
            rev_spec(width), rev_spec(width), rev_part_spec, whole((width, model)), whole((width, 256)),
        ],
        out_shape=[
            like((total_rows, width), F32), like((total_rows, width), BF16), parts_shape,
            like((width, model), BF16), like((width, 256), F32),
        ],
        scratch_shapes=[
            pltpu.VMEM((states, slots, width), F32), pltpu.VMEM((states, slots, width), F32),
            pltpu.VMEM((slots, width), F32), pltpu.VMEM((slots, width), F32), pltpu.VMEM((states, slots, width), F32),
        ]
        + [pltpu.VMEM((rows, width), F32)] * 5
        + [
            pltpu.VMEM((STEPS, states, slots, width), F32), pltpu.VMEM((STEPS, states, slots, width), F32),
            pltpu.VMEM((2 * states, rows, 128), F32), pltpu.VMEM((PAIR, 2 * states, slots, 128), F32),
            pltpu.VMEM((PAIR, 2 * states, slots, 128), F32), pltpu.VMEM((2 * states, rows), F32),
            pltpu.VMEM((states, slots, width), F32), pltpu.VMEM((rows, 2 * states), F32), misc_shape, misc_shape,
            pltpu.VMEM((width, model), F32),
        ],
        compiler_params=params(),
        cost_estimate=cost(95),
        name="back",
    )(g_branch, dtl, bc, inp, gate, y, ck, packed, packed, packed)

    gdtl, gbc = combine(gproj, BF16, 3)

    branch = collect(branch)
    branch, gdtl = lax.optimization_barrier((branch, gdtl))
    tile = own * slots
    vmem = pltpu.VMEM
    g_normed, gin, gout, gback, gtail, ggain = pl.pallas_call(
        functools.partial(finish_kernel, slots=slots, n_dp=n_dp, n_f=n_f),
        grid=grid,
        in_specs=[
            rev_spec(rank), rev_spec(2 * states), rev_spec(width), rev_spec(width), rev_spec(width), rev_spec(width),
            pl.BlockSpec((4 * slots, width), lambda i: (jnp.maximum((blocks - 1 - i) * (STEPS // 4) - 1, 0), 0)),
            rev_spec(model), whole((1, model)), win_spec, xw_spec, misc_spec, hbm, hbm,
        ],
        out_specs=[
            hbm, whole((d_rows, 2 * width * n_f)), whole((inner_rows, model)), whole((inner_rows, 256)),
            whole((inner_rows, 256)), whole((8, 128)),
        ],
        out_shape=[
            like((n_dp, tile, model), BF16), like((d_rows, 2 * width * n_f), F32), like((inner_rows, model), F32),
            like((inner_rows, 256), F32), like((inner_rows, 256), F32), like((8, 128), F32),
        ],
        scratch_shapes=[
            misc_shape, misc_shape, vmem((model, 2 * width), F32), vmem((width, 128), F32), vmem((width, 128), F32),
            vmem((1, model), F32), vmem((rows + 3 * slots, width), F32), vmem((rows + 3 * slots, width), F32),
            vmem((4, slots, width), F32), vmem((slots, width), F32),
            vmem((n_f, n_dp, tile, model), BF16), vmem((n_z, n_dp, tile, model), BF16),
            vmem((n_z + 1, n_dp, tile, model), BF16),
            vmem((n_dp, n_f, d_rows, 2 * width), BF16), vmem((n_dp, n_f, d_rows, 2 * width), BF16),
            vmem((n_f, d_rows, 2 * width), BF16), vmem((n_f, d_rows, 2 * width), BF16),
            vmem((n_dp, inner_rows, model), BF16), vmem((n_dp, inner_rows, 256), F32),
            vmem((n_dp, inner_rows, 256), F32), vmem((n_dp, inner_rows, 256), F32),
            vmem((n_dp, n_f, 8, 128), F32), vmem((n_dp, n_f, 8, 128), F32), vmem((n_f, 8, 128), F32),
            vmem((n_f, 8, 128), F32), dma((3,)),
        ]
        + [dma((n_z, n_dp))] * 6
        + [dma((n_dp,))] * 12
        + [dma((n_f,))] * 4,
        compiler_params=pltpu.CompilerParams(
            collective_id=4, has_side_effects=True, vmem_limit_bytes=FULL_VMEM, dimension_semantics=("arbitrary",)
        ),
        cost_estimate=cost(105),
        name="finish",
    )(
        gdtl, gbc, inp, gis, ggate, inner, inner, x, gain, win, packed, packed,
        gout.reshape(n_dp, inner_rows, model), gmisc.reshape(n_dp, inner_rows, 256),
    )

    hidden = tokens.astype(F32)
    upstream = cotangent.astype(F32)
    output = (hidden + jnp.where(own_mask[:, :, None], branch.astype(F32), 0.0)).astype(BF16)
    g_normed = g_normed.reshape(n_dp, own, slots, model).transpose(0, 2, 1, 3).reshape(seqs, own, model).astype(F32)
    factor = lax.rsqrt(jnp.mean(hidden * hidden, axis=-1, keepdims=True) + EPSILON)
    weighted = gain * g_normed
    input_grad = (
        upstream + factor * weighted - hidden * factor**3 * jnp.mean(hidden * weighted, axis=-1, keepdims=True)
    ).astype(BF16)
    conv_bias_grad = gtail[:, rank + CONV_BIAS]
    x_grad = gtail[:, : rank + 2 * states]
    return (
        output, input_grad, ggain[0, :d_rows], gin, gtail[:, rank + TAPS : rank + TAPS + 4], conv_bias_grad, x_grad,
        gback[:, :rank], gback[:, rank + DT_BIAS], gback[:, rank + DECAY : rank + DECAY + states],
        gback[:, rank + SKIP], gout,
    )


def solution(mesh):
    rows1, rows2, pos = P(BOTH), P(BOTH, None), P(None, BOTH, None)
    return jax.shard_map(
        functools.partial(body, n_dp=mesh.shape["dp"], n_f=mesh.shape["fsdp"]),
        mesh=mesh,
        in_specs=(pos, pos, P(), P(), rows1, rows2, rows2, rows1, rows2, rows2, rows1, rows2, rows1, rows2),
        out_specs=(pos, pos, rows1, rows2, rows2, rows1, rows2, rows2, rows1, rows2, rows1, rows2),
        check_vma=False,
    )
```

```python
import functools
import jax
import jax.numpy as jnp
from jax import lax
from jax.experimental import pallas as pl
from jax.experimental.pallas import tpu as pltpu
from jax.sharding import PartitionSpec as P

EPSILON = 1e-05
ROWS = 256
PAIR = 2
LAG = 4
HOP = jnp.bfloat16
LANES = 8
TOGETHER = 8
LOG2E = 1.4426950408889634
BOTH = ("dp", "fsdp")
F32 = jnp.float32
BF16 = jnp.bfloat16
VMEM_BYTES = 60 * 1024 * 1024
FULL_VMEM = 63 * 1024 * 1024
DECAY, TAPS, CONV_BIAS, DT_BIAS, SKIP = 32, 48, 52, 53, 54


def dot(a, b, dims=((1,), (0,))):
    return lax.dot_general(a, b, (dims, ((), ())), preferred_element_type=F32)


def sigmoid(v):
    return 1.0 / (1.0 + jnp.exp(-v))


def softplus(v):
    return jnp.maximum(v, 0.0) + jnp.log1p(jnp.exp(-jnp.abs(v)))


def rms_normed(x, gain):
    factor = lax.rsqrt(jnp.mean(x * x, axis=-1, keepdims=True) + EPSILON)
    return (x * factor * gain).astype(BF16)


def front_kernel(
    x_ref, gain_ref, win_ref, xw_ref, misc_ref, ow_ref, inner_ref, gate_ref, inp_ref, dtl_ref, bc_ref, owf_ref,
    pad_ref, misc_scr, ow_buf, ow_send, ow_recv, ow_local, *scratch, slots, length, n_dp, n_f
):
    d = lax.axis_index("dp")
    f = lax.axis_index("fsdp")

    def ow(k):
        return remote(ow_ref, owf_ref.at[d], ow_send.at[k], ow_recv.at[k], ((d + k) % n_dp, f))

    def ow_arrival(k):
        src = (d - k + n_dp) % n_dp
        return remote(ow_ref, owf_ref.at[src], ow_send.at[k], ow_recv.at[k], (src, f))

    ow_get = pltpu.make_async_copy(ow_ref, ow_buf, ow_local.at[0])
    ow_put = pltpu.make_async_copy(ow_buf, owf_ref.at[d], ow_local.at[1])
    enter, send, relay, close = combiner(scratch, dtl_ref, bc_ref, n_f)
    i = pl.program_id(0)
    last = pl.num_programs(0) - 1
    rows = x_ref.shape[0]
    width = inner_ref.shape[1]
    halo = 3 * slots
    parts = rows // length

    @pl.when(i == 0)
    def _():
        enter([((d + k) % n_dp, f) for k in range(1, n_dp)])
        for k in range(1, n_dp):
            ow(k).start()
        ow_get.start()

    @pl.when(i == 1)
    def _():
        ow_get.wait()
        ow_put.start()

    @pl.when(i > 0)
    def _():
        for a in range(parts):
            send((i - 1) * parts + a)

    normed = rms_normed(x_ref[...].astype(F32), gain_ref[...])
    both = dot(normed, win_ref[...])
    gate_ref[...] = both[:, width:]
    inner = both[:, :width]
    inner_ref[...] = inner

    @pl.when(pl.program_id(0) == 0)
    def _():
        pad_ref[0:halo, :] = jnp.zeros((halo, width), F32)
        misc_scr[...] = jnp.transpose(misc_ref[...].astype(F32))

    pad_ref[halo : halo + rows, :] = inner
    total = jnp.broadcast_to(misc_scr[CONV_BIAS : CONV_BIAS + 1, :], (rows, width))
    for tap in range(4):
        total = total + misc_scr[TAPS + tap : TAPS + tap + 1, :] * pad_ref[tap * slots : tap * slots + rows, :]
    inp = (total * sigmoid(total)).astype(BF16)
    inp_ref[...] = inp
    pack_rows(scratch[0], i * parts, dot(inp, xw_ref[...]), dot(inp, misc_ref[...])[:, :DECAY], length)
    pad_ref[0:halo, :] = pad_ref[rows : rows + halo, :]

    @pl.when(i > 0)
    def _():
        for a in range(parts):
            relay((i - 1) * parts + a)

    @pl.when(i == last)
    def _():
        for a in range(parts):
            send(i * parts + a)
        for a in range(parts):
            relay(i * parts + a)
        close()
        ow_put.wait()
        for k in range(1, n_dp):
            ow_arrival(k).wait_recv()
            ow(k).wait_send()


def spread_lanes(bc_ref, out_ref, k, slots, steps):
    for j in range(PAIR):
        t = jnp.minimum(k * PAIR + j, steps - 1)
        at = pl.ds(pl.multiple_of(t * slots, slots), slots)
        for n in range(out_ref.shape[1]):
            out_ref[j, n] = jnp.broadcast_to(bc_ref[at, n : n + 1], (slots, 128))


def widen(piece, width):
    return jnp.concatenate([piece] * (width // 128), axis=1)


def narrow(value):
    total = value[:, :128]
    for first in range(128, value.shape[1], 128):
        total = total + value[:, first : first + 128]
    return total


def mix_kernel(
    dtl_ref, bc_ref, inp_ref, gate_ref, dtw_ref, misc_ref, ow_ref,
    y_ref, ck_ref, br_ref, h_scr, delta_scr, u_scr, rate_scr, even_scr, odd_scr, misc_scr, *, slots
):
    rows, width = inp_ref.shape
    steps = rows // slots
    states = h_scr.shape[0]

    @pl.when(pl.program_id(0) == 0)
    def _():
        h_scr[...] = jnp.zeros_like(h_scr)
        misc_scr[...] = jnp.transpose(misc_ref[...].astype(F32))
        for n in range(states):
            rate_scr[n] = jnp.broadcast_to(-jnp.exp(misc_scr[DECAY + n : DECAY + n + 1, :]) * LOG2E, (slots, width))

    ck_ref[0] = h_scr[...]
    delta = softplus(dot(dtl_ref[...], dtw_ref[...], ((1,), (1,))) + misc_scr[DT_BIAS : DT_BIAS + 1, :])
    delta_scr[...] = delta
    u_scr[...] = delta * inp_ref[...].astype(F32)
    spread_lanes(bc_ref, even_scr, 0, slots, steps)

    def step(k, bcb_scr, next_scr):
        spread_lanes(bc_ref, next_scr, k + 1, slots, steps)
        ats, ds, us, ys = [], [], [], []
        for j in range(PAIR):
            at = pl.ds(pl.multiple_of((k * PAIR + j) * slots, slots), slots)
            ats.append(at)
            ds.append(delta_scr[at, :])
            us.append(u_scr[at, :])
            ys.append(None)
        for n in range(states):
            rate = rate_scr[n]
            h = h_scr[n]
            for j in range(PAIR):
                h = jnp.exp2(ds[j] * rate) * h + us[j] * widen(bcb_scr[j, n], width)
                term = h * widen(bcb_scr[j, states + n], width)
                ys[j] = term if n == 0 else ys[j] + term
            h_scr[n] = h
        for j in range(PAIR):
            y_ref[ats[j], :] = ys[j]

    def steps_twice(k, carry):
        step(2 * k, even_scr, odd_scr)
        step(2 * k + 1, odd_scr, even_scr)
        return carry

    lax.fori_loop(0, steps // PAIR // 2, steps_twice, 0)
    y = y_ref[...] + misc_scr[SKIP : SKIP + 1, :] * inp_ref[...].astype(F32)
    y_ref[...] = y
    gate = gate_ref[...]
    gated = (y * (gate * sigmoid(gate))).astype(BF16)
    br_ref[...] = dot(gated, ow_ref[...]).astype(br_ref.dtype).reshape(br_ref.shape)


def lane_sums(parts):
    lane = lax.broadcasted_iota(jnp.int32, parts[0].shape, 1)
    bit = 1
    while len(parts) > 1:
        low = (lane & bit) == 0
        merged = []
        for j in range(0, len(parts), 2):
            kept = jnp.where(low, parts[j], parts[j + 1])
            moved = jnp.where(low, parts[j + 1], parts[j])
            merged.append(kept + pltpu.roll(moved, bit, 1))
        parts = merged
        bit *= 2
    total = parts[0]
    while bit < total.shape[1]:
        total = total + pltpu.roll(total, bit, 1)
        bit *= 2
    return total


def back_kernel(
    gb_ref, dtl_ref, bc_ref, inp_ref, gate_ref, y_ref, ck_ref, dtw_ref, misc_ref, ow_ref, br_ref,
    gis_ref, ggate_ref, gdtl_ref, gbcs_ref, gout_ref, gmisc_ref, brr_ref,
    lam_scr, dacc_scr, sacc_scr, bacc_scr, rate_scr, delta_scr, u_scr, gy_scr, gu_scr, gd_scr, h_scr, a_scr, gbt_scr,
    even_scr, odd_scr, sums_scr, h_now, gbc_ref, misc_scr, back_scr, gout_scr,
    mine, theirs, passed, b_local, b_done, one_send, one_recv, up_send, up_recv, down_send, down_recv, *scratch,
    slots, length, n_dp, n_f
):
    enter, send, relay, close = combiner(scratch, gdtl_ref, gbcs_ref, n_f)
    d = lax.axis_index("dp")
    f = lax.axis_index("fsdp")
    n_z = n_f // 2
    z = f // 2
    core = f % 2
    other = 1 - core

    def one(to, j):
        return remote(
            br_ref.at[to * 2 + other, j], theirs.at[to, j], one_send.at[to, j], one_recv.at[to, j], (d, z * 2 + other)
        )

    def up(to, j):
        return remote(mine.at[to, j], passed.at[to + 1, j], up_send.at[to, j], up_recv.at[to, j], (d, f + 2))

    def down(to, j):
        return remote(mine.at[to, j], passed.at[to, j], down_send.at[to, j], down_recv.at[to, j], (d, f - 2))

    def load(to, j):
        return pltpu.make_async_copy(br_ref.at[to * 2 + core, j], mine.at[to, j], b_local.at[to, j])

    done = pltpu.make_async_copy(mine.at[z], brr_ref, b_done.at[0])

    def pair(to, j):
        one(to, j).wait_recv()
        load(to, j).wait()
        mine[to, j] = (mine[to, j].astype(F32) + theirs[to, j].astype(F32)).astype(mine.dtype)

    def take(to, j, slot):
        mine[to, j] = (mine[to, j].astype(F32) + passed[slot, j].astype(F32)).astype(mine.dtype)

    def hop(u):
        above = z + n_z - 1 - u
        below = u - (n_z - 1 - z)

        @pl.when((above > z) & (above < n_z))
        def _():
            def block(j, carry):
                pair(above, j)

                @pl.when(z > 0)
                def _():
                    up(above, j).wait_recv()
                    take(above, j, above + 1)

                up(above, j).start()
                return carry

            lax.fori_loop(0, n_dp, block, 0)

        @pl.when((below < z) & (below >= 0))
        def _():
            def block(j, carry):
                pair(below, j)

                @pl.when(z < n_z - 1)
                def _():
                    down(below, j).wait_recv()
                    take(below, j, below)

                down(below, j).start()
                return carry

            lax.fori_loop(0, n_dp, block, 0)

    def settle():
        def block(j, carry):
            pair(z, j)

            @pl.when(z > 0)
            def _():
                up(z, j).wait_recv()
                take(z, j, z + 1)

            @pl.when(z < n_z - 1)
            def _():
                down(z, j).wait_recv()
                take(z, j, z)

            return carry

        lax.fori_loop(0, n_dp, block, 0)
        done.start()

    rows, width = inp_ref.shape
    steps = rows // slots
    states = lam_scr.shape[0]
    rank = dtl_ref.shape[1]
    step_id = pl.program_id(0)
    final = pl.num_programs(0) - 1
    parts = rows // length

    @pl.when(step_id == 0)
    def _():
        enter()
        for to in range(n_z):
            for j in range(n_dp):
                one(to, j).start()
                load(to, j).start()

    for u in range(n_z - 1):

        @pl.when(step_id == 1 + 2 * u)
        def _():
            hop(u)

    @pl.when(step_id > 0)
    def _():
        for a in range(parts):
            send((final - step_id + 1) * parts + a)

    @pl.when(step_id == 0)
    def _():
        lam_scr[...] = jnp.zeros_like(lam_scr)
        dacc_scr[...] = jnp.zeros_like(dacc_scr)
        sacc_scr[...] = jnp.zeros_like(sacc_scr)
        bacc_scr[...] = jnp.zeros_like(bacc_scr)
        gout_scr[...] = jnp.zeros_like(gout_scr)
        gmisc_ref[...] = jnp.zeros_like(gmisc_ref)
        misc_scr[...] = jnp.transpose(misc_ref[...].astype(F32))
        for n in range(states):
            rate_scr[n] = jnp.broadcast_to(-jnp.exp(misc_scr[DECAY + n : DECAY + n + 1, :]) * LOG2E, (slots, width))

    gb = gb_ref[...].reshape(rows, gb_ref.shape[-1])
    gate = gate_ref[...]
    sig = sigmoid(gate)
    silu = gate * sig
    y = y_ref[...]
    inp = inp_ref[...].astype(F32)
    g_gated = dot(gb, ow_ref[...], ((1,), (1,)))
    g_y = g_gated * silu
    gy_scr[...] = g_y
    ggate_ref[...] = (g_gated * y * (sig * (1.0 + gate * (1.0 - sig)))).astype(BF16)
    gout_scr[...] += dot((y * silu).astype(BF16), gb, ((0,), (0,)))
    sacc_scr[...] += jnp.sum((g_y * inp).reshape(steps, slots, width), axis=0)
    pre = dot(dtl_ref[...], dtw_ref[...], ((1,), (1,))) + misc_scr[DT_BIAS : DT_BIAS + 1, :]
    delta = softplus(pre)
    delta_scr[...] = delta
    u_scr[...] = delta * inp

    last = steps // PAIR - 1
    spread_lanes(bc_ref, even_scr, 0, slots, steps)
    h_now[...] = ck_ref[0]

    def replay(k, bcb_scr, next_scr):
        spread_lanes(bc_ref, next_scr, k + 1, slots, steps)
        ds, us, gys = [], [], []
        for j in range(PAIR):
            at = pl.ds(pl.multiple_of((k * PAIR + j) * slots, slots), slots)
            ds.append(delta_scr[at, :])
            us.append(u_scr[at, :])
            gys.append(gy_scr[at, :])
        for n in range(states):
            rate = rate_scr[n]
            h = h_now[n]
            for j in range(PAIR):
                t = k * PAIR + j
                h_scr[t, n] = h
                decay = jnp.exp2(ds[j] * rate)
                a_scr[t, n] = decay
                h = decay * h + us[j] * widen(bcb_scr[j, n], width)
                gbt_scr[states + n, pl.ds(pl.multiple_of(t * slots, slots), slots), :] = narrow(h * gys[j])
            h_now[n] = h

    def replay_twice(k, carry):
        replay(2 * k, even_scr, odd_scr)
        replay(2 * k + 1, odd_scr, even_scr)
        return carry

    lax.fori_loop(0, steps // PAIR // 2, replay_twice, 0)
    spread_lanes(bc_ref, even_scr, last, slots, steps)

    def reverse(k, bcb_scr, next_scr):
        spread_lanes(bc_ref, next_scr, jnp.maximum(k - 1, 0), slots, steps)
        ats, ds, us, gys, gus, gds, ts = [], [], [], [], [], [], []
        for j in range(PAIR):
            t = k * PAIR + j
            at = pl.ds(pl.multiple_of(t * slots, slots), slots)
            ts.append(t)
            ats.append(at)
            ds.append(delta_scr[at, :])
            us.append(u_scr[at, :])
            gys.append(gy_scr[at, :])
            gus.append(None)
            gds.append(None)
        for n in range(states):
            rate = rate_scr[n]
            carried = lam_scr[n]
            total = dacc_scr[n]
            for j in reversed(range(PAIR)):
                t = ts[j]
                lam = carried + gys[j] * widen(bcb_scr[j, states + n], width)
                term = lam * widen(bcb_scr[j, n], width)
                gus[j] = term if n == 0 else gus[j] + term
                gbt_scr[n, ats[j], :] = narrow(lam * us[j])
                carried = a_scr[t, n] * lam
                q = carried * h_scr[t, n]
                term = q * rate
                gds[j] = term if n == 0 else gds[j] + term
                total = total + q * ds[j]
            lam_scr[n] = carried
            dacc_scr[n] = total
        for j in range(PAIR):
            gu_scr[ats[j], :] = gus[j]
            gd_scr[ats[j], :] = gds[j]

    def reverse_twice(i, carry):
        k = last - 2 * i
        reverse(k, even_scr, odd_scr)
        reverse(k - 1, odd_scr, even_scr)
        return carry

    lax.fori_loop(0, steps // PAIR // 2, reverse_twice, 0)

    def reduce_lanes(k, carry):
        for j in range(LANES):
            n = k * LANES + j
            sums_scr[pl.ds(n, 1), :] = jnp.sum(jnp.transpose(gbt_scr[n]), axis=0, keepdims=True)
        return carry

    lax.fori_loop(0, 2 * states // LANES, reduce_lanes, 0)
    gbc_ref[...] = jnp.transpose(sums_scr[...])
    gu = gu_scr[...]
    gis_ref[...] = gu * delta_scr[...] + misc_scr[SKIP : SKIP + 1, :] * gy_scr[...]
    g_pre = (gd_scr[...] * (1.0 / LOG2E) + gu * inp) * sigmoid(pre)
    bacc_scr[...] += jnp.sum(g_pre.reshape(steps, slots, width), axis=0)
    g_low = g_pre.astype(BF16)
    gmisc_ref[:, :rank] += dot(g_low, dtl_ref[...], ((0,), (0,)))
    pack_rows(scratch[0], (final - step_id) * parts, dot(g_low, dtw_ref[...]), gbc_ref[...], length)

    @pl.when(step_id > 0)
    def _():
        for a in range(parts):
            relay((final - step_id + 1) * parts + a)

    @pl.when(step_id == pl.num_programs(0) - 1)
    def _():
        back_scr[...] = jnp.zeros_like(back_scr)
        for n in range(states):
            rate = -jnp.exp(misc_scr[DECAY + n : DECAY + n + 1, :])
            back_scr[DECAY + n : DECAY + n + 1, :] = jnp.sum(dacc_scr[n], axis=0, keepdims=True) * rate
        back_scr[SKIP : SKIP + 1, :] = jnp.sum(sacc_scr[...], axis=0, keepdims=True)
        back_scr[DT_BIAS : DT_BIAS + 1, :] = jnp.sum(bacc_scr[...], axis=0, keepdims=True)
        for a in range(parts):
            send(a)
        gmisc_ref[:, rank:] = jnp.transpose(back_scr[...])
        gout_ref[...] = gout_scr[...].astype(gout_ref.dtype)
        for a in range(parts):
            relay(a)
        steps_run = pl.num_programs(0)
        lax.fori_loop(jnp.minimum(steps_run // 2, n_z - 1), n_z - 1, lambda u, c: (hop(u), c)[1], 0)
        settle()
        close()
        done.wait()
        for to in range(n_z):
            for j in range(n_dp):
                one(to, j).wait_send()

                @pl.when(z < to)
                def _():
                    up(to, j).wait_send()

                @pl.when(z > to)
                def _():
                    down(to, j).wait_send()


def remote(src, dst, send, recv, where):
    return pltpu.make_async_remote_copy(
        src_ref=src, dst_ref=dst, send_sem=send, recv_sem=recv, device_id=where, device_id_type=pl.DeviceIdType.MESH
    )


def gather_kernel(
    tok_ref, cot_ref, win_ref, gain_ref, pk_ref, x_ref, c_ref, w_ref, g_ref, p_ref,
    tok_buf, cot_buf, win_buf, gain_buf, pk_buf, local_sem,
    tdp_send, tdp_recv, cdp_send, cdp_recv, up_send, up_recv, down_send, down_recv, core_send, core_recv,
    w1_send, w1_recv, w2_send, w2_recv, g1_send, g1_recv, g2_send, g2_recv, p_send, p_recv, *, n_dp, n_f
):
    d = lax.axis_index("dp")
    f = lax.axis_index("fsdp")
    n_z = n_f // 2
    z = f // 2
    core = f % 2
    partner = z * 2 + (1 - core)

    barrier = pltpu.get_barrier_semaphore()
    for k in range(1, n_f):
        pl.semaphore_signal(barrier, inc=1, device_id=(d, (f + k) % n_f), device_id_type=pl.DeviceIdType.MESH)
    for k in range(1, n_dp):
        pl.semaphore_signal(barrier, inc=1, device_id=((d + k) % n_dp, f), device_id_type=pl.DeviceIdType.MESH)
    pl.semaphore_wait(barrier, n_f + n_dp - 2)

    loads = (
        pltpu.make_async_copy(tok_ref.at[d], tok_buf, local_sem.at[0]),
        pltpu.make_async_copy(win_ref.at[f], win_buf, local_sem.at[1]),
        pltpu.make_async_copy(gain_ref, gain_buf, local_sem.at[2]),
        pltpu.make_async_copy(pk_ref, pk_buf, local_sem.at[3]),
        pltpu.make_async_copy(cot_ref.at[d], cot_buf, local_sem.at[8]),
    )
    stores = (
        pltpu.make_async_copy(tok_buf, x_ref.at[d, f], local_sem.at[4]),
        pltpu.make_async_copy(win_buf, w_ref.at[d, f], local_sem.at[5]),
        pltpu.make_async_copy(gain_buf, g_ref.at[d, f], local_sem.at[6]),
        pltpu.make_async_copy(pk_buf, p_ref.at[d], local_sem.at[7]),
        pltpu.make_async_copy(cot_buf, c_ref.at[d], local_sem.at[9]),
    )
    for load in loads:
        load.start()

    def tok_dp(k):
        to = (d + k) % n_dp
        return remote(tok_ref.at[to], x_ref.at[d, f], tdp_send.at[k], tdp_recv.at[k], (to, f))

    def tok_dp_arrival(k):
        src = (d - k + n_dp) % n_dp
        return remote(tok_ref.at[d], x_ref.at[src, f], tdp_send.at[k], tdp_recv.at[k], (src, f))

    def cot_dp(k):
        to = (d + k) % n_dp
        return remote(cot_ref.at[to], c_ref.at[d], cdp_send.at[k], cdp_recv.at[k], (to, f))

    def cot_dp_arrival(k):
        src = (d - k + n_dp) % n_dp
        return remote(cot_ref.at[d], c_ref.at[src], cdp_send.at[k], cdp_recv.at[k], (src, f))

    def w1(k):
        to = (f + k) % n_f
        return remote(win_ref.at[to], w_ref.at[d, f], w1_send.at[k], w1_recv.at[k], (d, to))

    def w1_arrival(k):
        src = (f - k + n_f) % n_f
        return remote(win_ref.at[f], w_ref.at[d, src], w1_send.at[k], w1_recv.at[k], (d, src))

    def g1(k):
        to = (f + k) % n_f
        return remote(gain_ref, g_ref.at[d, f], g1_send.at[k], g1_recv.at[k], (d, to))

    def g1_arrival(k):
        src = (f - k + n_f) % n_f
        return remote(gain_ref, g_ref.at[d, src], g1_send.at[k], g1_recv.at[k], (d, src))

    def w2(k):
        to = (d + k) % n_dp
        return remote(w_ref.at[d], w_ref.at[d], w2_send.at[k], w2_recv.at[k], (to, f))

    def w2_arrival(k):
        src = (d - k + n_dp) % n_dp
        return remote(w_ref.at[src], w_ref.at[src], w2_send.at[k], w2_recv.at[k], (src, f))

    def g2(k):
        to = (d + k) % n_dp
        return remote(g_ref.at[d], g_ref.at[d], g2_send.at[k], g2_recv.at[k], (to, f))

    def g2_arrival(k):
        src = (d - k + n_dp) % n_dp
        return remote(g_ref.at[src], g_ref.at[src], g2_send.at[k], g2_recv.at[k], (src, f))

    def pk(k):
        to = (d + k) % n_dp
        return remote(pk_ref, p_ref.at[d], p_send.at[k], p_recv.at[k], (to, f))

    def pk_arrival(k):
        src = (d - k + n_dp) % n_dp
        return remote(pk_ref, p_ref.at[src], p_send.at[k], p_recv.at[k], (src, f))

    def block(j, origin, side):
        at = (d - j + n_dp) % n_dp
        return x_ref.at[at, origin * 2 + side]

    def up(j, origin, src=None):
        ref = block(j, origin, core)
        return remote(ref if src is None else src, ref, up_send.at[origin, j], up_recv.at[origin, j], (d, f + 2))

    def down(j, origin, src=None):
        ref = block(j, origin, core)
        return remote(ref if src is None else src, ref, down_send.at[origin, j], down_recv.at[origin, j], (d, f - 2))

    def across(j, origin, src=None):
        ref = block(j, origin, core)
        return remote(
            ref if src is None else src, ref, core_send.at[origin, j], core_recv.at[origin, j], (d, partner)
        )

    def across_arrival(j, origin):
        ref = block(j, origin, 1 - core)
        return remote(ref, ref, core_send.at[origin, j], core_recv.at[origin, j], (d, partner))

    def launch(j, src=None):
        @pl.when(z < n_z - 1)
        def _():
            up(j, z, src).start()

        @pl.when(z > 0)
        def _():
            down(j, z, src).start()

        across(j, z, src).start()

    for k in range(1, n_f):
        w1(k).start()
    for k in range(1, n_dp):
        tok_dp(k).start()
    launch(0, tok_ref.at[d])
    for k in range(1, n_f):
        g1(k).start()
    for k in range(1, n_dp):
        pk(k).start()
    for k in range(1, n_dp):
        cot_dp(k).start()
    for load, store in zip(loads, stores):
        load.wait()
        store.start()
    for k in range(1, n_dp):
        tok_dp_arrival(k).wait_recv()
        launch(k)
    for store in stores:
        store.wait()
    for k in range(1, n_f):
        w1_arrival(k).wait_recv()
        g1_arrival(k).wait_recv()
    for k in range(1, n_dp):
        w2(k).start()
        g2(k).start()
    for far in range(1, n_z):
        for j in range(n_dp):

            @pl.when(z >= far)
            def _():
                origin = z - far
                up(j, origin).wait_recv()

                @pl.when(z < n_z - 1)
                def _():
                    up(j, origin).start()

                across(j, origin).start()

            @pl.when(z + far < n_z)
            def _():
                origin = z + far
                down(j, origin).wait_recv()

                @pl.when(z > 0)
                def _():
                    down(j, origin).start()

                across(j, origin).start()

    for origin in range(n_z):
        for j in range(n_dp):
            across_arrival(j, origin).wait_recv()
            across(j, origin).wait_send()
    for origin in range(n_z):
        for j in range(n_dp):

            @pl.when((origin <= z) & (z < n_z - 1))
            def _():
                up(j, origin).wait_send()

            @pl.when((origin >= z) & (z > 0))
            def _():
                down(j, origin).wait_send()

    for k in range(1, n_dp):
        pk_arrival(k).wait_recv()
        cot_dp_arrival(k).wait_recv()
        cot_dp(k).wait_send()
        w2_arrival(k).wait_recv()
        g2_arrival(k).wait_recv()
        tok_dp(k).wait_send()
        w2(k).wait_send()
        g2(k).wait_send()
        pk(k).wait_send()
    for k in range(1, n_f):
        w1(k).wait_send()
        g1(k).wait_send()


def pack_rows(out_ref, base, main, rest, chunk):
    part = chunk // 4
    for q in range(main.shape[0] // chunk):
        out_ref[base + q, 0:chunk, :] = main[q * chunk : (q + 1) * chunk, :]
        for j in range(4):
            first = q * chunk + j * part
            out_ref[base + q, chunk : chunk + part, j * 32 : (j + 1) * 32] = rest[first : first + part, :]


def combiner(scratch, main_ref, rest_ref, n_f):
    (
        part, own, one, sums, two, tops, rests, one_send, one_recv, two_send, two_recv, top_send, top_recv,
        rest_send, rest_recv, ctop_send, ctop_recv, crest_send, crest_recv,
    ) = scratch
    d = lax.axis_index("dp")
    f = lax.axis_index("fsdp")
    n_z = n_f // 2
    z = f // 2
    core = f % 2
    other = 1 - core
    partner = z * 2 + other
    chunk = tops.shape[2]

    def first(q):
        return remote(part.at[q], one.at[q // 2], one_send.at[q // 2], one_recv.at[q // 2], (d, partner))

    def second(to, k):
        return remote(sums.at[to], two.at[k], two_send.at[k], two_recv.at[k], (d, to * 2 + core))

    def third(k):
        to = ((z + k) % n_z * 2 + core,)
        return (
            remote(tops.at[z, core], tops.at[z, core], top_send.at[k], top_recv.at[k], (d,) + to),
            remote(rests.at[z, core], rests.at[z, core], rest_send.at[k], rest_recv.at[k], (d,) + to),
        )

    def third_arrival(k):
        src = (z - k + n_z) % n_z
        to = (src * 2 + core,)
        return (
            remote(tops.at[src, core], tops.at[src, core], top_send.at[k], top_recv.at[k], (d,) + to),
            remote(rests.at[src, core], rests.at[src, core], rest_send.at[k], rest_recv.at[k], (d,) + to),
        )

    def fourth(k, side):
        src = (z - k + n_z) % n_z
        return (
            remote(tops.at[src, side], tops.at[src, side], ctop_send.at[k], ctop_recv.at[k], (d, partner)),
            remote(rests.at[src, side], rests.at[src, side], crest_send.at[k], crest_recv.at[k], (d, partner)),
        )

    def enter(peers=()):
        barrier = pltpu.get_barrier_semaphore()
        for peer in peers:
            pl.semaphore_signal(barrier, inc=1, device_id=peer, device_id_type=pl.DeviceIdType.MESH)
        pl.semaphore_signal(barrier, inc=1, device_id=(d, partner), device_id_type=pl.DeviceIdType.MESH)
        for k in range(1, n_z):
            pl.semaphore_signal(
                barrier, inc=1, device_id=(d, (z + k) % n_z * 2 + core), device_id_type=pl.DeviceIdType.MESH
            )
        pl.semaphore_wait(barrier, n_z + len(peers))

    def send(q):
        @pl.when(q % 2 == other)
        def _():
            first(q).start()

    def relay(q):
        @pl.when(q % 2 == core)
        def _():
            to = q // 2
            first(q).wait_recv()
            total = part[q] + one[to]

            @pl.when(to == z)
            def _():
                own[...] = total

            @pl.when(to != z)
            def _():
                sums[to] = total.astype(sums.dtype)
                second(to, (to - z + n_z) % n_z).start()

    def close():
        total = own[...]
        for k in range(1, n_z):
            second(z, k).wait_recv()
            total = total + two[k].astype(F32)
        tops[z, core] = total[0:chunk, :].astype(tops.dtype)
        rests[z, core] = total[chunk:, :].astype(rests.dtype)
        for k in range(1, n_z):
            for copy in third(k):
                copy.start()
        for copy in fourth(0, core):
            copy.start()
        for k in range(1, n_z):
            for copy in third_arrival(k):
                copy.wait_recv()
            for copy in fourth(k, core):
                copy.start()
        for k in range(n_z):
            for copy in fourth(k, other):
                copy.wait_recv()
        quarter = chunk // 4
        for a in range(n_z):
            for b in range(2):
                at = (a * 2 + b) * chunk
                main_ref[at : at + chunk, :] = tops[a, b]
                rest = rests[a, b]
                for j in range(4):
                    rest_ref[at + j * quarter : at + (j + 1) * quarter, :] = rest[:, j * 32 : (j + 1) * 32]
        for k in range(n_z):
            first(k * 2 + other).wait_send()
            for copy in fourth(k, core):
                copy.wait_send()
            if k:
                second((z + k) % n_z, k).wait_send()
                for copy in third(k):
                    copy.wait_send()

    return enter, send, relay, close


def combine_scratch(n_f, length, rest_type):
    n_z = n_f // 2
    packed_rows = length + length // 4
    return [
        pltpu.VMEM((n_f, packed_rows, 128), F32), pltpu.VMEM((packed_rows, 128), F32),
        pltpu.VMEM((n_z, packed_rows, 128), F32), pltpu.VMEM((n_z, packed_rows, 128), HOP),
        pltpu.VMEM((n_z, packed_rows, 128), HOP), pltpu.VMEM((n_z, 2, length, 128), BF16),
        pltpu.VMEM((n_z, 2, length // 4, 128), rest_type),
    ] + [pltpu.SemaphoreType.DMA((n_z,))] * 12


def finish_kernel(
    gdtl_ref, gbc_ref, inp_ref, gis_ref, ggate_ref, inner_ref, before_ref, x_ref, gain_ref, win_ref, xw_ref, misc_ref,
    gout_ref, gback_ref, br_ref, out_ref, brout_ref, gin_out, gout_out, gback_out, gtail_out, gg_out,
    misc_scr, tail_scr, gin_scr, gsel_scr, grest_scr, ggain_scr, pad_scr, gpad_scr, wacc_scr, cacc_scr,
    mine, theirs, passed, gin_low, gin_got, gin_sum, gin_all, gout_got, gback_got, gtail_low, gtail_got,
    gg_low, gg_got, gg_sum, gg_all, br_buf, local_sem,
    one_send, one_recv, up_send, up_recv, down_send, down_recv, dp_send, dp_recv,
    r_send, r_recv, w_send, w_recv, o_send, o_recv, b_send, b_recv, t_send, t_recv, g_send, g_recv,
    w2_send, w2_recv, g2_send, g2_recv, *, slots, n_dp, n_f
):
    d = lax.axis_index("dp")
    f = lax.axis_index("fsdp")
    n_z = n_f // 2
    z = f // 2
    core = f % 2
    other = 1 - core
    partner = z * 2 + other
    rows, width = inp_ref.shape
    steps = rows // slots
    halo = 3 * slots
    i = pl.program_id(0)
    blocks = mine.shape[0] * mine.shape[1] * mine.shape[2] // rows
    last = blocks - 1
    tile = mine.shape[2]
    held = rows // tile
    per = n_f // held
    pairs = held // 2
    rank = gdtl_ref.shape[1]
    d_rows, inner_rows = gin_out.shape[0], gout_out.shape[0]

    def place(q):
        return (last - q) // per, (last - q) % per * pairs

    def one(to, j):
        return remote(
            mine.at[to * 2 + other, j], theirs.at[to, j], one_send.at[to, j], one_recv.at[to, j], (d, partner)
        )

    def up(to, j):
        return remote(
            mine.at[to * 2 + core, j], passed.at[to + 1, j], up_send.at[to, j], up_recv.at[to, j], (d, f + 2)
        )

    def down(to, j):
        return remote(
            mine.at[to * 2 + core, j], passed.at[to, j], down_send.at[to, j], down_recv.at[to, j], (d, f - 2)
        )

    def dp(k):
        to = (d + k) % n_dp
        return remote(mine.at[f, to], out_ref.at[d], dp_send.at[k], dp_recv.at[k], (to, f))

    def dp_arrival(k):
        src = (d - k + n_dp) % n_dp
        return remote(mine.at[f, src], out_ref.at[src], dp_send.at[k], dp_recv.at[k], (src, f))

    def over_dp(src, dst, send, recv):
        return [
            remote(src.at[(d + k) % n_dp], dst.at[k], send.at[k], recv.at[k], ((d + k) % n_dp, f))
            for k in range(1, n_dp)
        ]

    def over_f(src, dst, send, recv, k):
        to = (f + k) % n_f
        return remote(src.at[to], dst.at[f], send.at[k], recv.at[k], (d, to))

    def over_f_arrival(src, dst, send, recv, k):
        to = (f - k + n_f) % n_f
        return remote(src.at[to], dst.at[to], send.at[k], recv.at[k], (d, to))

    def branch(k):
        to = (d + k) % n_dp
        return remote(br_ref.at[to], brout_ref.at[d], r_send.at[k], r_recv.at[k], (to, f))

    def branch_arrival(k):
        src = (d - k + n_dp) % n_dp
        return remote(br_ref.at[src], brout_ref.at[src], r_send.at[k], r_recv.at[k], (src, f))

    get_branch = pltpu.make_async_copy(br_ref.at[d], br_buf, local_sem.at[3])
    put_branch = pltpu.make_async_copy(br_buf, brout_ref.at[d], local_sem.at[4])
    outs = lambda: over_dp(gout_ref, gout_got, o_send, o_recv)
    backs = lambda: over_dp(gback_ref, gback_got, b_send, b_recv)
    ins = lambda: over_dp(gin_low, gin_got, w_send, w_recv)
    tails = lambda: over_dp(gtail_low, gtail_got, t_send, t_recv)
    gains = lambda: over_dp(gg_low, gg_got, g_send, g_recv)
    own_out = pltpu.make_async_copy(gout_ref.at[d], gout_got.at[0], local_sem.at[0])
    own_back = pltpu.make_async_copy(gback_ref.at[d], gback_got.at[0], local_sem.at[1])
    put = pltpu.make_async_copy(mine.at[f, d], out_ref.at[d], local_sem.at[2])

    def send_halves(q):
        j, first = place(q)
        for a in range(pairs):
            one(first + a, j).start()

    def pair(to, j):
        one(to, j).wait_recv()
        return mine[to * 2 + core, j].astype(F32) + theirs[to, j].astype(F32)

    def hops(step):
        q_up = step - 1 - LAG * z
        q_down = step - 1 - LAG * (n_z - 1 - z)
        q_end = step - 1 - LAG * jnp.maximum(z, n_z - 1 - z)

        @pl.when((q_up >= 0) & (q_up < blocks))
        def _():
            j, first = place(q_up)
            for a in range(pairs):
                to = first + a

                @pl.when(to > z)
                def _():
                    mine[to * 2 + core, j] = pair(to, j).astype(mine.dtype)

                    @pl.when(z > 0)
                    def _():
                        up(to, j).wait_recv()
                        mine[to * 2 + core, j] = (
                            mine[to * 2 + core, j].astype(F32) + passed[to + 1, j].astype(F32)
                        ).astype(mine.dtype)

            for a in range(pairs):

                @pl.when(first + a > z)
                def _():
                    up(first + a, j).start()

        @pl.when((q_down >= 0) & (q_down < blocks))
        def _():
            j, first = place(q_down)
            for a in range(pairs):
                to = first + a

                @pl.when(to < z)
                def _():
                    mine[to * 2 + core, j] = pair(to, j).astype(mine.dtype)

                    @pl.when(z < n_z - 1)
                    def _():
                        down(to, j).wait_recv()
                        mine[to * 2 + core, j] = (
                            mine[to * 2 + core, j].astype(F32) + passed[to, j].astype(F32)
                        ).astype(mine.dtype)

            for a in range(pairs):

                @pl.when(first + a < z)
                def _():
                    down(first + a, j).start()

        @pl.when((q_end >= 0) & (q_end < blocks))
        def _():
            j, first = place(q_end)

            @pl.when((z >= first) & (z < first + pairs))
            def _():
                mine[f, j] = pair(z, j).astype(mine.dtype)

                @pl.when(z > 0)
                def _():
                    up(z, j).wait_recv()
                    mine[f, j] = (mine[f, j].astype(F32) + passed[z + 1, j].astype(F32)).astype(mine.dtype)

                @pl.when(z < n_z - 1)
                def _():
                    down(z, j).wait_recv()
                    mine[f, j] = (mine[f, j].astype(F32) + passed[z, j].astype(F32)).astype(mine.dtype)

                for k in range(n_dp):

                    @pl.when(j == (d + k) % n_dp)
                    def _():
                        if k:
                            dp(k).start()
                        else:
                            put.start()

    @pl.when(i == 0)
    def _():
        barrier = pltpu.get_barrier_semaphore()
        for k in range(1, n_f):
            pl.semaphore_signal(barrier, inc=1, device_id=(d, (f + k) % n_f), device_id_type=pl.DeviceIdType.MESH)
        for k in range(1, n_dp):
            pl.semaphore_signal(barrier, inc=1, device_id=((d + k) % n_dp, f), device_id_type=pl.DeviceIdType.MESH)
        pl.semaphore_wait(barrier, n_f + n_dp - 2)
        for copy in outs() + backs():
            copy.start()
        for k in range(1, n_dp):
            branch(k).start()
        get_branch.start()
        own_out.start()
        own_back.start()
        gpad_scr[rows : rows + halo, :] = jnp.zeros((halo, width), F32)
        wacc_scr[...] = jnp.zeros_like(wacc_scr)
        cacc_scr[...] = jnp.zeros_like(cacc_scr)
        gin_scr[...] = jnp.zeros_like(gin_scr)
        gsel_scr[...] = jnp.zeros_like(gsel_scr)
        grest_scr[...] = jnp.zeros_like(grest_scr)
        ggain_scr[...] = jnp.zeros_like(ggain_scr)
        misc_scr[...] = jnp.transpose(misc_ref[...].astype(F32))

    @pl.when(i > 0)
    def _():
        send_halves(i - 1)

    gdtl = gdtl_ref[...]
    gbc = gbc_ref[...]
    inp = inp_ref[...]
    gsel_scr[...] += dot(inp, gdtl, ((0,), (0,)))
    grest_scr[:, :DECAY] += dot(inp, gbc, ((0,), (0,)))
    g_inputs = (
        gis_ref[...]
        + dot(gdtl, xw_ref[...], ((1,), (1,)))
        + dot(gbc, misc_ref[:, :DECAY], ((1,), (1,)))
    )
    pad_scr[0:halo, :] = before_ref[slots : slots + halo, :] * (i < last).astype(F32)
    pad_scr[halo : halo + rows, :] = inner_ref[...]
    total = jnp.broadcast_to(misc_scr[CONV_BIAS : CONV_BIAS + 1, :], (rows, width))
    for tap in range(4):
        total = total + misc_scr[TAPS + tap : TAPS + tap + 1, :] * pad_scr[tap * slots : tap * slots + rows, :]
    sig = sigmoid(total)
    g_conv = g_inputs * (sig * (1.0 + total * (1.0 - sig)))
    gpad_scr[0:rows, :] = g_conv
    g_inner = jnp.zeros((rows, width), F32)
    for tap in range(4):
        back = (3 - tap) * slots
        g_inner = g_inner + misc_scr[TAPS + tap : TAPS + tap + 1, :] * gpad_scr[back : back + rows, :]
        wacc_scr[tap] += jnp.sum(
            (g_conv * pad_scr[tap * slots : tap * slots + rows, :]).reshape(steps, slots, width), axis=0
        )
    cacc_scr[...] += jnp.sum(g_conv.reshape(steps, slots, width), axis=0)
    gpad_scr[rows : rows + halo, :] = gpad_scr[0:halo, :]
    g_both = jnp.concatenate([g_inner.astype(BF16), ggate_ref[...]], axis=1)
    x = x_ref[...].astype(F32)
    scaled = x * lax.rsqrt(jnp.mean(x * x, axis=-1, keepdims=True) + EPSILON)
    gin_scr[...] += dot((scaled * gain_ref[...]).astype(BF16), g_both, ((0,), (0,)))
    g_normed = dot(g_both, win_ref[...], ((1,), (1,)))
    ggain_scr[...] += jnp.sum(g_normed * scaled, axis=0, keepdims=True)
    block, first = place(i)
    for a in range(held):
        mine[first * 2 + a, block] = g_normed[a * tile : (a + 1) * tile, :].astype(mine.dtype)
    hops(i)

    @pl.when(i == last)
    def _():
        for a in range(n_dp):
            for b in range(n_f):
                at = (a * n_f + b) * d_rows
                gin_low[a, b] = gin_scr[at : at + d_rows, :].astype(gin_low.dtype)
                gg_low[a, b] = jnp.zeros((8, 128), F32)
                gg_low[a, b, 0:1, 0:d_rows] = ggain_scr[:, at : at + d_rows]
        tail_scr[...] = jnp.zeros_like(tail_scr)
        for tap in range(4):
            tail_scr[TAPS + tap : TAPS + tap + 1, :] = jnp.sum(wacc_scr[tap], axis=0, keepdims=True)
        tail_scr[CONV_BIAS : CONV_BIAS + 1, :] = jnp.sum(cacc_scr[...], axis=0, keepdims=True)
        grest_scr[:, DECAY:] = jnp.transpose(tail_scr[...])[:, DECAY:]
        for a in range(n_dp):
            at = a * inner_rows
            gtail_low[a, :, :rank] = gsel_scr[at : at + inner_rows, :]
            gtail_low[a, :, rank:] = grest_scr[at : at + inner_rows, :]
        send_halves(last)
        for copy in ins() + tails() + gains():
            copy.start()
        hops(blocks)
        get_branch.wait()
        put_branch.start()
        own_out.wait()
        own_back.wait()
        for copy in outs() + backs():
            copy.wait_recv()
        total = gout_got[0].astype(F32)
        for k in range(1, n_dp):
            total = total + gout_got[k].astype(F32)
        gout_out[...] = total
        total = gback_got[0]
        for k in range(1, n_dp):
            total = total + gback_got[k]
        gback_out[...] = total

        def drain(step, carry):
            hops(step)
            return carry

        lax.fori_loop(blocks + 1, blocks + 1 + LAG * (n_z - 1), drain, 0)

        for copy in ins() + tails() + gains():
            copy.wait_recv()

        def add(q, carry):
            total = gin_low[d, q].astype(F32)
            for k in range(1, n_dp):
                total = total + gin_got[k, q].astype(F32)
            gin_sum[q] = total.astype(gin_sum.dtype)
            total = gg_low[d, q]
            for k in range(1, n_dp):
                total = total + gg_got[k, q]
            gg_sum[q] = total
            return carry

        lax.fori_loop(0, n_f, add, 0)
        for k in range(1, n_f):
            over_f(gin_sum, gin_all, w2_send, w2_recv, k).start()
            over_f(gg_sum, gg_all, g2_send, g2_recv, k).start()
        gin_all[f] = gin_sum[f]
        gg_all[f] = gg_sum[f]
        total = gtail_low[d]
        for k in range(1, n_dp):
            total = total + gtail_got[k]
        gtail_out[...] = total
        for k in range(1, n_f):
            over_f_arrival(gin_sum, gin_all, w2_send, w2_recv, k).wait_recv()
            over_f_arrival(gg_sum, gg_all, g2_send, g2_recv, k).wait_recv()
        total = gg_all[0]
        for b in range(1, n_f):
            total = total + gg_all[b]
        gg_out[...] = total
        for b in range(n_f):
            for h in range(2):
                for a in range(n_dp):
                    to = (h * n_dp + a) * n_f * inner_rows + b * inner_rows
                    at = (h * n_dp + a) * inner_rows
                    gin_out[:, to : to + inner_rows] = gin_all[b, :, at : at + inner_rows].astype(F32)
        for k in range(1, n_dp):
            dp_arrival(k).wait_recv()
            dp(k).wait_send()
        put.wait()
        put_branch.wait()
        for k in range(1, n_dp):
            branch_arrival(k).wait_recv()
            branch(k).wait_send()
        for copy in outs() + backs() + ins() + tails() + gains():
            copy.wait_send()
        for k in range(1, n_f):
            over_f(gin_sum, gin_all, w2_send, w2_recv, k).wait_send()
            over_f(gg_sum, gg_all, g2_send, g2_recv, k).wait_send()
        for to in range(n_z):
            for j in range(n_dp):
                one(to, j).wait_send()

                @pl.when(z < to)
                def _():
                    up(to, j).wait_send()

                @pl.when(z > to)
                def _():
                    down(to, j).wait_send()


def whole(shape):
    return pl.BlockSpec(shape, lambda i: (0,) * len(shape))


def cost(micros):
    return pl.CostEstimate(flops=int(micros * 1.15e9), bytes_accessed=1 << 20, transcendentals=0)


def params(number=None):
    if number is None:
        return pltpu.CompilerParams(vmem_limit_bytes=VMEM_BYTES, dimension_semantics=("arbitrary",))
    return pltpu.CompilerParams(
        vmem_limit_bytes=FULL_VMEM, dimension_semantics=("arbitrary",), collective_id=number, has_side_effects=True
    )


def body(
    tokens, cotangent, lengths, deal_order, norm_gain, in_weight, conv_weight, conv_bias,
    x_weight, dt_weight, dt_bias, decay_log, skip_gain, out_weight, *, n_dp, n_f
):
    seqs, own, model = tokens.shape
    slots = seqs // n_dp
    inner_rows, states = decay_log.shape
    rank = dt_weight.shape[1]
    width = inner_rows * n_dp
    length = own * n_dp * n_f
    d_rows = in_weight.shape[0]
    total_rows = length * slots
    group = lax.axis_index("dp")
    member = lax.axis_index("fsdp")

    low = lambda v: v.astype(BF16)
    slot_ids = jnp.arange(seqs, dtype=jnp.int32)
    seq_len = jnp.sum(jnp.where(deal_order[:, None] == slot_ids[None, :], lengths[:, None], 0), axis=0)
    own_pos = (group * n_f + member) * own + jnp.arange(own, dtype=jnp.int32)
    own_mask = own_pos[None, :] < seq_len[:, None]

    def by_group(v):
        return v.reshape(n_dp, slots, own, model).transpose(0, 2, 1, 3).reshape(n_dp, own * slots, model)

    def by_seq(v):
        return v.reshape(n_dp, own, slots, model).transpose(0, 2, 1, 3).reshape(seqs, own, model).astype(F32)

    masked = by_group(jnp.where(own_mask[:, :, None], cotangent, jnp.zeros_like(cotangent)))

    tok = by_group(tokens)
    win = low(in_weight).reshape(d_rows, 2, n_dp, n_f, inner_rows).transpose(3, 0, 1, 2, 4)
    win = win.reshape(n_f, d_rows, 2 * width)
    gain_tile = jnp.zeros((8, 128), F32).at[0, :d_rows].set(low(norm_gain).astype(F32))
    misc = jnp.concatenate(
        [x_weight[:, rank:], decay_log, conv_weight, conv_bias[:, None], dt_bias[:, None], skip_gain[:, None]], axis=1
    )
    misc = jnp.pad(misc, ((0, 0), (0, 128 - misc.shape[1])))
    packed = low(jnp.concatenate([x_weight[:, :rank], misc, dt_weight], axis=1))
    ow = low(out_weight)
    n_z = n_f // 2
    dma = pltpu.SemaphoreType.DMA
    hbm = pl.BlockSpec(memory_space=pl.ANY)
    x, g_branch, win, gain, packed = pl.pallas_call(
        functools.partial(gather_kernel, n_dp=n_dp, n_f=n_f),
        in_specs=[hbm] * 5,
        out_specs=[hbm] * 5,
        out_shape=[
            jax.ShapeDtypeStruct((n_dp, n_f) + tok.shape[1:], BF16),
            jax.ShapeDtypeStruct(tok.shape, BF16),
            jax.ShapeDtypeStruct((n_dp, n_f) + win.shape[1:], BF16),
            jax.ShapeDtypeStruct((n_dp, n_f, 8, 128), F32),
            jax.ShapeDtypeStruct((n_dp,) + packed.shape, BF16),
        ],
        scratch_shapes=[
            pltpu.VMEM(tok.shape[1:], BF16), pltpu.VMEM(tok.shape[1:], BF16), pltpu.VMEM(win.shape[1:], BF16),
            pltpu.VMEM((8, 128), F32), pltpu.VMEM(packed.shape, BF16), dma((10,)),
            dma((n_dp,)), dma((n_dp,)), dma((n_dp,)), dma((n_dp,)),
        ]
        + [dma((n_z, n_dp))] * 6
        + [dma((n_f,)), dma((n_f,)), dma((n_dp,)), dma((n_dp,)), dma((n_f,)), dma((n_f,))]
        + [dma((n_dp,))] * 4,
        compiler_params=pltpu.CompilerParams(collective_id=1, has_side_effects=True),
        cost_estimate=cost(90),
        name="gather",
    )(tok, masked, win, gain_tile, packed)
    g_branch = lax.all_gather(g_branch, "fsdp", axis=0, tiled=False)
    x = x.reshape(total_rows, model)
    win = win.reshape(model, 2 * width)
    gain = gain[:, :, 0, :d_rows].reshape(1, model)
    packed = packed.reshape(width, -1)
    span = ROWS // slots
    rows = span * slots
    blocks = length // span
    grid = (blocks,)
    row_spec = lambda cols: pl.BlockSpec((rows, cols), lambda i: (i, 0))
    rev_spec = lambda cols: pl.BlockSpec((rows, cols), lambda i: (blocks - 1 - i, 0))
    once = dict(pipeline_mode=pl.Buffered(1))
    ow_spec = pl.BlockSpec((width, model), lambda i: (0, 0), **once)
    xw_spec = pl.BlockSpec((width, 128), lambda i: (0, 0), **once)
    misc_spec = pl.BlockSpec((width, 128), lambda i: (0, 1), **once)
    dtw_spec = pl.BlockSpec((width, 128), lambda i: (0, 2), **once)
    win_spec = pl.BlockSpec((model, 2 * width), lambda i: (0, 0), **once)
    misc_shape = pltpu.VMEM((128, width), F32)
    like = jax.ShapeDtypeStruct
    held = span // own
    per = n_f // held
    piece = (held, 1, own * slots, model)
    piece_spec = pl.BlockSpec(piece, lambda i: (i % per, i // per, 0, 0))
    rev_piece_spec = pl.BlockSpec(piece, lambda i: ((blocks - 1 - i) % per, (blocks - 1 - i) // per, 0, 0))
    pieces_shape = like((n_f, n_dp, own * slots, model), BF16)
    inner, gate, inp, dtl, bc, ow = pl.pallas_call(
        functools.partial(front_kernel, slots=slots, length=length, n_dp=n_dp, n_f=n_f),
        grid=grid,
        in_specs=[
            row_spec(model), whole((1, model)), win_spec, xw_spec, misc_spec, hbm,
        ],
        out_specs=[
            row_spec(width), row_spec(width), row_spec(width), whole((total_rows, rank)), whole((total_rows, 2 * states)),
            hbm,
        ],
        out_shape=[
            like((total_rows, width), F32), like((total_rows, width), F32), like((total_rows, width), BF16),
            like((total_rows, rank), BF16), like((total_rows, 2 * states), F32), like((n_dp,) + ow.shape, BF16),
        ],
        scratch_shapes=[
            pltpu.VMEM((rows + 3 * slots, width), F32), misc_shape, pltpu.VMEM(ow.shape, BF16),
            dma((n_dp,)), dma((n_dp,)), dma((2,)),
        ]
        + combine_scratch(n_f, length, F32),
        compiler_params=params(2),
        cost_estimate=cost(42),
        name="front",
    )(x, gain, win, packed, packed, ow)
    ow = ow.reshape(width, model)


    y, ck, branch = pl.pallas_call(
        functools.partial(mix_kernel, slots=slots),
        grid=grid,
        in_specs=[
            row_spec(rank), row_spec(2 * states), row_spec(width), row_spec(width), dtw_spec, misc_spec, ow_spec,
        ],
        out_specs=[
            row_spec(width), pl.BlockSpec((1, states, slots, width), lambda i: (i, 0, 0, 0)), piece_spec,
        ],
        out_shape=[
            like((total_rows, width), F32), like((blocks, states, slots, width), F32), pieces_shape,
        ],
        scratch_shapes=[
            pltpu.VMEM((states, slots, width), F32), pltpu.VMEM((rows, width), F32), pltpu.VMEM((rows, width), F32),
            pltpu.VMEM((states, slots, width), F32), pltpu.VMEM((PAIR, 2 * states, slots, 128), F32),
            pltpu.VMEM((PAIR, 2 * states, slots, 128), F32), misc_shape,
        ],
        compiler_params=params(),
        cost_estimate=cost(36),
        name="mix",
    )(dtl, bc, inp, gate, packed, packed, ow)

    gis, ggate, gdtl, gbc, gout, gmisc, branch = pl.pallas_call(
        functools.partial(back_kernel, slots=slots, length=length, n_dp=n_dp, n_f=n_f),
        grid=grid,
        in_specs=[
            rev_piece_spec, rev_spec(rank), rev_spec(2 * states), rev_spec(width), rev_spec(width), rev_spec(width),
            pl.BlockSpec((1, states, slots, width), lambda i: (blocks - 1 - i, 0, 0, 0)), dtw_spec, misc_spec, ow_spec,
            hbm,
        ],
        out_specs=[
            rev_spec(width), rev_spec(width), whole((total_rows, rank)), whole((total_rows, 2 * states)),
            whole((width, model)), whole((width, 256)), hbm,
        ],
        out_shape=[
            like((total_rows, width), F32), like((total_rows, width), BF16), like((total_rows, rank), BF16),
            like((total_rows, 2 * states), BF16), like((width, model), BF16), like((width, 256), F32),
            like((n_dp, own * slots, model), BF16),
        ],
        scratch_shapes=[
            pltpu.VMEM((states, slots, width), F32), pltpu.VMEM((states, slots, width), F32),
            pltpu.VMEM((slots, width), F32), pltpu.VMEM((slots, width), F32), pltpu.VMEM((states, slots, width), F32),
        ]
        + [pltpu.VMEM((rows, width), F32)] * 5
        + [
            pltpu.VMEM((span, states, slots, width), F32), pltpu.VMEM((span, states, slots, width), F32),
            pltpu.VMEM((2 * states, rows, 128), F32), pltpu.VMEM((PAIR, 2 * states, slots, 128), F32),
            pltpu.VMEM((PAIR, 2 * states, slots, 128), F32), pltpu.VMEM((2 * states, rows), F32),
            pltpu.VMEM((states, slots, width), F32), pltpu.VMEM((rows, 2 * states), F32), misc_shape, misc_shape,
            pltpu.VMEM((width, model), F32), pltpu.VMEM((n_z, n_dp, own * slots, model), BF16),
            pltpu.VMEM((n_z, n_dp, own * slots, model), BF16), pltpu.VMEM((n_z + 1, n_dp, own * slots, model), BF16),
            dma((n_z, n_dp)), dma((1,)),
        ]
        + [dma((n_z, n_dp))] * 6
        + combine_scratch(n_f, length, BF16),
        compiler_params=params(3),
        cost_estimate=cost(100),
        name="back",
    )(g_branch, dtl, bc, inp, gate, y, ck, packed, packed, ow, branch)


    tile = own * slots
    vmem = pltpu.VMEM
    g_normed, branch, gin, gout, gback, gtail, ggain = pl.pallas_call(
        functools.partial(finish_kernel, slots=slots, n_dp=n_dp, n_f=n_f),
        grid=grid,
        in_specs=[
            rev_spec(rank), rev_spec(2 * states), rev_spec(width), rev_spec(width), rev_spec(width), rev_spec(width),
            pl.BlockSpec((4 * slots, width), lambda i: (jnp.maximum((blocks - 1 - i) * (span // 4) - 1, 0), 0)),
            rev_spec(model), whole((1, model)), win_spec, xw_spec, misc_spec, hbm, hbm, hbm,
        ],
        out_specs=[
            hbm, hbm, whole((d_rows, 2 * width * n_f)), whole((inner_rows, model)), whole((inner_rows, 256)),
            whole((inner_rows, 256)), whole((8, 128)),
        ],
        out_shape=[
            like((n_dp, tile, model), BF16), like((n_dp, tile, model), BF16), like((d_rows, 2 * width * n_f), F32), like((inner_rows, model), F32),
            like((inner_rows, 256), F32), like((inner_rows, 256), F32), like((8, 128), F32),
        ],
        scratch_shapes=[
            misc_shape, misc_shape, vmem((model, 2 * width), F32), vmem((width, 128), F32), vmem((width, 128), F32),
            vmem((1, model), F32), vmem((rows + 3 * slots, width), F32), vmem((rows + 3 * slots, width), F32),
            vmem((4, slots, width), F32), vmem((slots, width), F32),
            vmem((n_f, n_dp, tile, model), BF16), vmem((n_z, n_dp, tile, model), BF16),
            vmem((n_z + 1, n_dp, tile, model), BF16),
            vmem((n_dp, n_f, d_rows, 2 * width), BF16), vmem((n_dp, n_f, d_rows, 2 * width), BF16),
            vmem((n_f, d_rows, 2 * width), BF16), vmem((n_f, d_rows, 2 * width), BF16),
            vmem((n_dp, inner_rows, model), BF16), vmem((n_dp, inner_rows, 256), F32),
            vmem((n_dp, inner_rows, 256), F32), vmem((n_dp, inner_rows, 256), F32),
            vmem((n_dp, n_f, 8, 128), F32), vmem((n_dp, n_f, 8, 128), F32), vmem((n_f, 8, 128), F32),
            vmem((n_f, 8, 128), F32), vmem((tile, model), BF16), dma((5,)),
        ]
        + [dma((n_z, n_dp))] * 6
        + [dma((n_dp,))] * 14
        + [dma((n_f,))] * 4,
        compiler_params=params(4),
        cost_estimate=cost(105),
        name="finish",
    )(
        gdtl, gbc, inp, gis, ggate, inner, inner, x, gain, win, packed, packed,
        gout.reshape(n_dp, inner_rows, model), gmisc.reshape(n_dp, inner_rows, 256), branch,
    )

    hidden = tokens.astype(F32)
    upstream = cotangent.astype(F32)
    output = (hidden + jnp.where(own_mask[:, :, None], by_seq(branch), 0.0)).astype(BF16)
    g_normed = by_seq(g_normed)
    factor = lax.rsqrt(jnp.mean(hidden * hidden, axis=-1, keepdims=True) + EPSILON)
    weighted = gain * g_normed
    input_grad = (
        upstream + factor * weighted - hidden * factor**3 * jnp.mean(hidden * weighted, axis=-1, keepdims=True)
    ).astype(BF16)
    conv_bias_grad = gtail[:, rank + CONV_BIAS]
    x_grad = gtail[:, : rank + 2 * states]
    return (
        output, input_grad, ggain[0, :d_rows], gin, gtail[:, rank + TAPS : rank + TAPS + 4], conv_bias_grad, x_grad,
        gback[:, :rank], gback[:, rank + DT_BIAS], gback[:, rank + DECAY : rank + DECAY + states],
        gback[:, rank + SKIP], gout,
    )


def solution(mesh):
    rows1, rows2, pos = P(BOTH), P(BOTH, None), P(None, BOTH, None)
    return jax.shard_map(
        functools.partial(body, n_dp=mesh.shape["dp"], n_f=mesh.shape["fsdp"]),
        mesh=mesh,
        in_specs=(pos, pos, P(), P(), rows1, rows2, rows2, rows1, rows2, rows2, rows1, rows2, rows1, rows2),
        out_specs=(pos, pos, rows1, rows2, rows2, rows1, rows2, rows2, rows1, rows2, rows1, rows2),
        check_vma=False,
    )
```

```python
import functools
import jax
import jax.numpy as jnp
from jax import lax
from jax.experimental import pallas as pl
from jax.experimental.pallas import tpu as pltpu
from jax.sharding import PartitionSpec as P

EPSILON = 1e-05
ROWS = 256
PAIR = 2
LAG = 4
MID = 3
HOP = jnp.bfloat16
LANES = 8
TOGETHER = 8
LOG2E = 1.4426950408889634
BOTH = ("dp", "fsdp")
F32 = jnp.float32
BF16 = jnp.bfloat16
VMEM_BYTES = 60 * 1024 * 1024
FULL_VMEM = 63 * 1024 * 1024
DECAY, TAPS, CONV_BIAS, DT_BIAS, SKIP = 32, 48, 52, 53, 54


def dot(a, b, dims=((1,), (0,))):
    return lax.dot_general(a, b, (dims, ((), ())), preferred_element_type=F32)


def sigmoid(v):
    return 1.0 / (1.0 + jnp.exp(-v))


def softplus(v):
    return jnp.maximum(v, 0.0) + jnp.log1p(jnp.exp(-jnp.abs(v)))


def rms_normed(x, gain):
    factor = lax.rsqrt(jnp.mean(x * x, axis=-1, keepdims=True) + EPSILON)
    return (x * factor * gain).astype(BF16)


def front_kernel(
    x_ref, gain_ref, win_ref, xw_ref, misc_ref, ow_ref, cin_ref, inner_ref, gate_ref, inp_ref, dtl_ref, bc_ref, owf_ref, c_ref,
    pad_ref, misc_scr, ow_raw, ow_buf, ow_send, ow_recv, ow_local, c_buf, c_local,
    cu_send, cu_recv, cd_send, cd_recv, ca_send, ca_recv, *scratch, slots, length, n_dp, n_f
):
    d = lax.axis_index("dp")
    f = lax.axis_index("fsdp")

    def ow(k):
        return remote(ow_buf, owf_ref.at[d], ow_send.at[k], ow_recv.at[k], ((d + k) % n_dp, f))

    def ow_arrival(k):
        src = (d - k + n_dp) % n_dp
        return remote(ow_buf, owf_ref.at[src], ow_send.at[k], ow_recv.at[k], (src, f))

    n_z = n_f // 2
    z = f // 2
    partner = z * 2 + 1 - f % 2

    def c_up(j, src):
        return remote(cin_ref.at[j], c_ref.at[src, j], cu_send.at[j], cu_recv.at[j], (d, f + 2))

    def c_down(j, src):
        return remote(cin_ref.at[j], c_ref.at[src, j], cd_send.at[j], cd_recv.at[j], (d, f - 2))

    def c_across(j, src):
        return remote(cin_ref.at[j], c_ref.at[src, j], ca_send.at[j], ca_recv.at[j], (d, partner))

    c_get = pltpu.make_async_copy(cin_ref, c_buf, c_local.at[0])
    c_put = pltpu.make_async_copy(c_buf, c_ref.at[f], c_local.at[1])
    ow_get = pltpu.make_async_copy(ow_ref, ow_raw, ow_local.at[0])
    ow_put = pltpu.make_async_copy(ow_buf, owf_ref.at[d], ow_local.at[1])
    enter, send, relay, close = combiner(scratch, dtl_ref, bc_ref, n_f)
    i = pl.program_id(0)
    last = pl.num_programs(0) - 1
    rows = x_ref.shape[0]
    width = inner_ref.shape[1]
    halo = 3 * slots
    parts = rows // length

    @pl.when(i == 0)
    def _():
        enter([((d + k) % n_dp, f) for k in range(1, n_dp)])
        ow_get.start()
        c_get.start()
        for j in range(n_dp):

            @pl.when(z < n_z - 1)
            def _():
                c_up(j, f).start()

            @pl.when(z > 0)
            def _():
                c_down(j, f).start()

            c_across(j, f).start()

    @pl.when(i == 1)
    def _():
        ow_get.wait()
        ow_buf[...] = ow_raw[...].astype(BF16)
        c_get.wait()
        c_put.start()

    @pl.when(i == 2)
    def _():
        ow_put.start()
        for k in range(1, n_dp):
            ow(k).start()

    @pl.when(i > 0)
    def _():
        for a in range(parts):
            send((i - 1) * parts + a)

    normed = rms_normed(x_ref[...].astype(F32), gain_ref[...])
    both = dot(normed, win_ref[...])
    gate_ref[...] = both[:, width:]
    inner = both[:, :width]
    inner_ref[...] = inner

    @pl.when(pl.program_id(0) == 0)
    def _():
        pad_ref[0:halo, :] = jnp.zeros((halo, width), F32)
        misc_scr[...] = jnp.transpose(misc_ref[...].astype(F32))

    pad_ref[halo : halo + rows, :] = inner
    total = jnp.broadcast_to(misc_scr[CONV_BIAS : CONV_BIAS + 1, :], (rows, width))
    for tap in range(4):
        total = total + misc_scr[TAPS + tap : TAPS + tap + 1, :] * pad_ref[tap * slots : tap * slots + rows, :]
    inp = (total * sigmoid(total)).astype(BF16)
    inp_ref[...] = inp
    pack_rows(scratch[0], i * parts, dot(inp, xw_ref[...]), dot(inp, misc_ref[...])[:, :DECAY], length)
    pad_ref[0:halo, :] = pad_ref[rows : rows + halo, :]

    @pl.when(i > 0)
    def _():
        for a in range(parts):
            relay((i - 1) * parts + a)

    @pl.when(i == last)
    def _():
        for a in range(parts):
            send(i * parts + a)
        for a in range(parts):
            relay(i * parts + a)
        close()
        c_put.wait()
        for j in range(n_dp):

            @pl.when(z > 0)
            def _():
                c_up(j, f - 2).wait_recv()
                c_down(j, f).wait_send()

            @pl.when(z < n_z - 1)
            def _():
                c_down(j, f + 2).wait_recv()
                c_up(j, f).wait_send()

            c_across(j, partner).wait_recv()
            c_across(j, f).wait_send()

        ow_put.wait()
        for k in range(1, n_dp):
            ow_arrival(k).wait_recv()
            ow(k).wait_send()


def spread_lanes(bc_ref, out_ref, k, slots, steps):
    for j in range(PAIR):
        t = jnp.minimum(k * PAIR + j, steps - 1)
        at = pl.ds(pl.multiple_of(t * slots, slots), slots)
        for n in range(out_ref.shape[1]):
            out_ref[j, n] = jnp.broadcast_to(bc_ref[at, n : n + 1], (slots, 128))


def widen(piece, width):
    return jnp.concatenate([piece] * (width // 128), axis=1)


def narrow(value):
    total = value[:, :128]
    for first in range(128, value.shape[1], 128):
        total = total + value[:, first : first + 128]
    return total


def mix_kernel(
    dtl_ref, bc_ref, inp_ref, gate_ref, dtw_ref, misc_ref, ow_ref, near_ref,
    y_ref, ck_ref, br_ref, c_ref, h_scr, delta_scr, u_scr, rate_scr, even_scr, odd_scr, misc_scr,
    up_send, up_recv, down_send, down_recv, core_send, core_recv, *, slots, n_dp, n_f
):
    d = lax.axis_index("dp")
    f = lax.axis_index("fsdp")
    n_z = n_f // 2
    z = f // 2
    core = f % 2
    partner = z * 2 + 1 - core
    i = pl.program_id(0)
    last = pl.num_programs(0) - 1

    def up(j, o):
        ref = c_ref.at[o * 2 + core, j]
        return remote(ref, ref, up_send.at[o, j], up_recv.at[o, j], (d, f + 2))

    def down(j, o):
        ref = c_ref.at[o * 2 + core, j]
        return remote(ref, ref, down_send.at[o, j], down_recv.at[o, j], (d, f - 2))

    def across(j, o, side):
        ref = c_ref.at[o * 2 + side, j]
        return remote(ref, ref, core_send.at[o, j], core_recv.at[o, j], (d, partner))

    def far(k, js):
        for j in js:

            @pl.when(z >= k)
            def _():
                if k > 1:
                    up(j, z - k).wait_recv()

                @pl.when(z < n_z - 1)
                def _():
                    up(j, z - k).start()

                across(j, z - k, core).start()

            @pl.when(z + k < n_z)
            def _():
                if k > 1:
                    down(j, z + k).wait_recv()

                @pl.when(z > 0)
                def _():
                    down(j, z + k).start()

                across(j, z + k, core).start()

    @pl.when(i == 0)
    def _():
        barrier = pltpu.get_barrier_semaphore()
        pl.semaphore_signal(barrier, inc=1, device_id=(d, partner), device_id_type=pl.DeviceIdType.MESH)
        for k in range(1, n_z):
            pl.semaphore_signal(
                barrier, inc=1, device_id=(d, (z + k) % n_z * 2 + core), device_id_type=pl.DeviceIdType.MESH
            )
        pl.semaphore_wait(barrier, n_z)
        far(1, range(n_dp))

    @pl.when(i == 3)
    def _():
        far(2, range(n_dp // 2))

    @pl.when(i == 5)
    def _():
        far(2, range(n_dp // 2, n_dp))

    rows, width = inp_ref.shape
    steps = rows // slots
    states = h_scr.shape[0]

    @pl.when(pl.program_id(0) == 0)
    def _():
        h_scr[...] = jnp.zeros_like(h_scr)
        misc_scr[...] = jnp.transpose(misc_ref[...].astype(F32))
        for n in range(states):
            rate_scr[n] = jnp.broadcast_to(-jnp.exp(misc_scr[DECAY + n : DECAY + n + 1, :]) * LOG2E, (slots, width))

    ck_ref[0] = h_scr[...]
    delta = softplus(dot(dtl_ref[...], dtw_ref[...], ((1,), (1,))) + misc_scr[DT_BIAS : DT_BIAS + 1, :])
    delta_scr[...] = delta
    u_scr[...] = delta * inp_ref[...].astype(F32)
    spread_lanes(bc_ref, even_scr, 0, slots, steps)

    def step(k, bcb_scr, next_scr):
        spread_lanes(bc_ref, next_scr, k + 1, slots, steps)
        ats, ds, us, ys = [], [], [], []
        for j in range(PAIR):
            at = pl.ds(pl.multiple_of((k * PAIR + j) * slots, slots), slots)
            ats.append(at)
            ds.append(delta_scr[at, :])
            us.append(u_scr[at, :])
            ys.append(None)
        for n in range(states):
            rate = rate_scr[n]
            h = h_scr[n]
            for j in range(PAIR):
                h = jnp.exp2(ds[j] * rate) * h + us[j] * widen(bcb_scr[j, n], width)
                term = h * widen(bcb_scr[j, states + n], width)
                ys[j] = term if n == 0 else ys[j] + term
            h_scr[n] = h
        for j in range(PAIR):
            y_ref[ats[j], :] = ys[j]

    def steps_twice(k, carry):
        step(2 * k, even_scr, odd_scr)
        step(2 * k + 1, odd_scr, even_scr)
        return carry

    lax.fori_loop(0, steps // PAIR // 2, steps_twice, 0)
    y = y_ref[...] + misc_scr[SKIP : SKIP + 1, :] * inp_ref[...].astype(F32)
    y_ref[...] = y
    gate = gate_ref[...]
    gated = (y * (gate * sigmoid(gate))).astype(BF16)
    br_ref[...] = dot(gated, ow_ref[...]).astype(br_ref.dtype).reshape(br_ref.shape)

    @pl.when(i == last)
    def _():
        for k in range(3, n_z):
            far(k, range(n_dp))
        for o in range(n_z):
            for j in range(n_dp):

                @pl.when(o != z)
                def _():
                    across(j, o, 1 - core).wait_recv()
                    across(j, o, core).wait_send()

                @pl.when((o < z) & (z < n_z - 1))
                def _():
                    up(j, o).wait_send()

                @pl.when((o > z) & (z > 0))
                def _():
                    down(j, o).wait_send()


def lane_sums(parts):
    lane = lax.broadcasted_iota(jnp.int32, parts[0].shape, 1)
    bit = 1
    while len(parts) > 1:
        low = (lane & bit) == 0
        merged = []
        for j in range(0, len(parts), 2):
            kept = jnp.where(low, parts[j], parts[j + 1])
            moved = jnp.where(low, parts[j + 1], parts[j])
            merged.append(kept + pltpu.roll(moved, bit, 1))
        parts = merged
        bit *= 2
    total = parts[0]
    while bit < total.shape[1]:
        total = total + pltpu.roll(total, bit, 1)
        bit *= 2
    return total


def back_kernel(
    gb_ref, dtl_ref, bc_ref, inp_ref, gate_ref, y_ref, ck_ref, dtw_ref, misc_ref, ow_ref, br_ref,
    gis_ref, ggate_ref, gdtl_ref, gbcs_ref, gout_ref, gmisc_ref, brr_ref,
    lam_scr, dacc_scr, sacc_scr, bacc_scr, rate_scr, delta_scr, u_scr, gy_scr, gu_scr, gd_scr, h_scr, a_scr, gbt_scr,
    even_scr, odd_scr, sums_scr, h_now, gbc_ref, misc_scr, back_scr, gout_scr,
    mine, theirs, passed, b_local, b_done, one_send, one_recv, up_send, up_recv, down_send, down_recv, *scratch,
    slots, length, n_dp, n_f
):
    enter, send, relay, close = combiner(scratch, gdtl_ref, gbcs_ref, n_f)
    d = lax.axis_index("dp")
    f = lax.axis_index("fsdp")
    n_z = n_f // 2
    z = f // 2
    core = f % 2
    other = 1 - core

    def one(to, j):
        return remote(
            br_ref.at[to * 2 + other, j], theirs.at[to, j], one_send.at[to, j], one_recv.at[to, j], (d, z * 2 + other)
        )

    def up(to, j):
        return remote(mine.at[to, j], passed.at[to + 1, j], up_send.at[to, j], up_recv.at[to, j], (d, f + 2))

    def down(to, j):
        return remote(mine.at[to, j], passed.at[to, j], down_send.at[to, j], down_recv.at[to, j], (d, f - 2))

    def load(to, j):
        return pltpu.make_async_copy(br_ref.at[to * 2 + core, j], mine.at[to, j], b_local.at[to, j])

    done = pltpu.make_async_copy(mine.at[z], brr_ref, b_done.at[0])

    def pair(to, j):
        one(to, j).wait_recv()
        load(to, j).wait()
        mine[to, j] = (mine[to, j].astype(F32) + theirs[to, j].astype(F32)).astype(mine.dtype)

    def take(to, j, slot):
        mine[to, j] = (mine[to, j].astype(F32) + passed[slot, j].astype(F32)).astype(mine.dtype)

    def hop(u):
        above = z + n_z - 1 - u
        below = u - (n_z - 1 - z)

        @pl.when((above > z) & (above < n_z))
        def _():
            def block(j, carry):
                pair(above, j)

                @pl.when(z > 0)
                def _():
                    up(above, j).wait_recv()
                    take(above, j, above + 1)

                up(above, j).start()
                return carry

            lax.fori_loop(0, n_dp, block, 0)

        @pl.when((below < z) & (below >= 0))
        def _():
            def block(j, carry):
                pair(below, j)

                @pl.when(z < n_z - 1)
                def _():
                    down(below, j).wait_recv()
                    take(below, j, below)

                down(below, j).start()
                return carry

            lax.fori_loop(0, n_dp, block, 0)

    def settle():
        def block(j, carry):
            pair(z, j)

            @pl.when(z > 0)
            def _():
                up(z, j).wait_recv()
                take(z, j, z + 1)

            @pl.when(z < n_z - 1)
            def _():
                down(z, j).wait_recv()
                take(z, j, z)

            return carry

        lax.fori_loop(0, n_dp, block, 0)
        done.start()

    rows, width = inp_ref.shape
    steps = rows // slots
    states = lam_scr.shape[0]
    rank = dtl_ref.shape[1]
    step_id = pl.program_id(0)
    final = pl.num_programs(0) - 1
    parts = rows // length

    @pl.when(step_id == 0)
    def _():
        enter()
        for to in range(n_z):
            for j in range(n_dp):
                one(to, j).start()
                load(to, j).start()

    for u in range(n_z - 1):

        @pl.when(step_id == 1 + 2 * u)
        def _():
            hop(u)

    @pl.when(step_id > 0)
    def _():
        for a in range(parts):
            send((final - step_id + 1) * parts + a)

    @pl.when(step_id == 0)
    def _():
        lam_scr[...] = jnp.zeros_like(lam_scr)
        dacc_scr[...] = jnp.zeros_like(dacc_scr)
        sacc_scr[...] = jnp.zeros_like(sacc_scr)
        bacc_scr[...] = jnp.zeros_like(bacc_scr)
        gout_scr[...] = jnp.zeros_like(gout_scr)
        gmisc_ref[...] = jnp.zeros_like(gmisc_ref)
        misc_scr[...] = jnp.transpose(misc_ref[...].astype(F32))
        for n in range(states):
            rate_scr[n] = jnp.broadcast_to(-jnp.exp(misc_scr[DECAY + n : DECAY + n + 1, :]) * LOG2E, (slots, width))

    gb = gb_ref[...].reshape(rows, gb_ref.shape[-1])
    gate = gate_ref[...]
    sig = sigmoid(gate)
    silu = gate * sig
    y = y_ref[...]
    inp = inp_ref[...].astype(F32)
    g_gated = dot(gb, ow_ref[...], ((1,), (1,)))
    g_y = g_gated * silu
    gy_scr[...] = g_y
    ggate_ref[...] = (g_gated * y * (sig * (1.0 + gate * (1.0 - sig)))).astype(BF16)
    gout_scr[...] += dot((y * silu).astype(BF16), gb, ((0,), (0,)))
    sacc_scr[...] += jnp.sum((g_y * inp).reshape(steps, slots, width), axis=0)
    pre = dot(dtl_ref[...], dtw_ref[...], ((1,), (1,))) + misc_scr[DT_BIAS : DT_BIAS + 1, :]
    delta = softplus(pre)
    delta_scr[...] = delta
    u_scr[...] = delta * inp

    last = steps // PAIR - 1
    spread_lanes(bc_ref, even_scr, 0, slots, steps)
    h_now[...] = ck_ref[0]

    def replay(k, bcb_scr, next_scr):
        spread_lanes(bc_ref, next_scr, k + 1, slots, steps)
        ds, us, gys = [], [], []
        for j in range(PAIR):
            at = pl.ds(pl.multiple_of((k * PAIR + j) * slots, slots), slots)
            ds.append(delta_scr[at, :])
            us.append(u_scr[at, :])
            gys.append(gy_scr[at, :])
        for n in range(states):
            rate = rate_scr[n]
            h = h_now[n]
            for j in range(PAIR):
                t = k * PAIR + j
                h_scr[t, n] = h
                decay = jnp.exp2(ds[j] * rate)
                a_scr[t, n] = decay
                h = decay * h + us[j] * widen(bcb_scr[j, n], width)
                gbt_scr[states + n, pl.ds(pl.multiple_of(t * slots, slots), slots), :] = narrow(h * gys[j])
            h_now[n] = h

    def replay_twice(k, carry):
        replay(2 * k, even_scr, odd_scr)
        replay(2 * k + 1, odd_scr, even_scr)
        return carry

    lax.fori_loop(0, steps // PAIR // 2, replay_twice, 0)
    spread_lanes(bc_ref, even_scr, last, slots, steps)

    def reverse(k, bcb_scr, next_scr):
        spread_lanes(bc_ref, next_scr, jnp.maximum(k - 1, 0), slots, steps)
        ats, ds, us, gys, gus, gds, ts = [], [], [], [], [], [], []
        for j in range(PAIR):
            t = k * PAIR + j
            at = pl.ds(pl.multiple_of(t * slots, slots), slots)
            ts.append(t)
            ats.append(at)
            ds.append(delta_scr[at, :])
            us.append(u_scr[at, :])
            gys.append(gy_scr[at, :])
            gus.append(None)
            gds.append(None)
        for n in range(states):
            rate = rate_scr[n]
            carried = lam_scr[n]
            total = dacc_scr[n]
            for j in reversed(range(PAIR)):
                t = ts[j]
                lam = carried + gys[j] * widen(bcb_scr[j, states + n], width)
                term = lam * widen(bcb_scr[j, n], width)
                gus[j] = term if n == 0 else gus[j] + term
                gbt_scr[n, ats[j], :] = narrow(lam * us[j])
                carried = a_scr[t, n] * lam
                q = carried * h_scr[t, n]
                term = q * rate
                gds[j] = term if n == 0 else gds[j] + term
                total = total + q * ds[j]
            lam_scr[n] = carried
            dacc_scr[n] = total
        for j in range(PAIR):
            gu_scr[ats[j], :] = gus[j]
            gd_scr[ats[j], :] = gds[j]

    def reverse_twice(i, carry):
        k = last - 2 * i
        reverse(k, even_scr, odd_scr)
        reverse(k - 1, odd_scr, even_scr)
        return carry

    lax.fori_loop(0, steps // PAIR // 2, reverse_twice, 0)

    def reduce_lanes(k, carry):
        for j in range(LANES):
            n = k * LANES + j
            sums_scr[pl.ds(n, 1), :] = jnp.sum(jnp.transpose(gbt_scr[n]), axis=0, keepdims=True)
        return carry

    lax.fori_loop(0, 2 * states // LANES, reduce_lanes, 0)
    gbc_ref[...] = jnp.transpose(sums_scr[...])
    gu = gu_scr[...]
    gis_ref[...] = gu * delta_scr[...] + misc_scr[SKIP : SKIP + 1, :] * gy_scr[...]
    g_pre = (gd_scr[...] * (1.0 / LOG2E) + gu * inp) * sigmoid(pre)
    bacc_scr[...] += jnp.sum(g_pre.reshape(steps, slots, width), axis=0)
    g_low = g_pre.astype(BF16)
    gmisc_ref[:, :rank] += dot(g_low, dtl_ref[...], ((0,), (0,)))
    pack_rows(scratch[0], (final - step_id) * parts, dot(g_low, dtw_ref[...]), gbc_ref[...], length)

    @pl.when(step_id > 0)
    def _():
        for a in range(parts):
            relay((final - step_id + 1) * parts + a)

    @pl.when(step_id == pl.num_programs(0) - 1)
    def _():
        back_scr[...] = jnp.zeros_like(back_scr)
        for n in range(states):
            rate = -jnp.exp(misc_scr[DECAY + n : DECAY + n + 1, :])
            back_scr[DECAY + n : DECAY + n + 1, :] = jnp.sum(dacc_scr[n], axis=0, keepdims=True) * rate
        back_scr[SKIP : SKIP + 1, :] = jnp.sum(sacc_scr[...], axis=0, keepdims=True)
        back_scr[DT_BIAS : DT_BIAS + 1, :] = jnp.sum(bacc_scr[...], axis=0, keepdims=True)
        for a in range(parts):
            send(a)
        gmisc_ref[:, rank:] = jnp.transpose(back_scr[...])
        gout_ref[...] = gout_scr[...].astype(gout_ref.dtype)
        for a in range(parts):
            relay(a)
        steps_run = pl.num_programs(0)
        lax.fori_loop(jnp.minimum(steps_run // 2, n_z - 1), n_z - 1, lambda u, c: (hop(u), c)[1], 0)
        settle()
        close()
        done.wait()
        for to in range(n_z):
            for j in range(n_dp):
                one(to, j).wait_send()

                @pl.when(z < to)
                def _():
                    up(to, j).wait_send()

                @pl.when(z > to)
                def _():
                    down(to, j).wait_send()


def remote(src, dst, send, recv, where):
    return pltpu.make_async_remote_copy(
        src_ref=src, dst_ref=dst, send_sem=send, recv_sem=recv, device_id=where, device_id_type=pl.DeviceIdType.MESH
    )


def gather_kernel(
    tok_ref, cot_ref, win_ref, gain_ref, pk_ref, x_ref, c_ref, w_ref, g_ref, p_ref,
    tok_buf, cot_buf, win_buf, gain_buf, pk_buf, local_sem,
    tdp_send, tdp_recv, cdp_send, cdp_recv, up_send, up_recv, down_send, down_recv, core_send, core_recv,
    w1_send, w1_recv, w2_send, w2_recv, g1_send, g1_recv, g2_send, g2_recv, p_send, p_recv, *, n_dp, n_f
):
    d = lax.axis_index("dp")
    f = lax.axis_index("fsdp")
    n_z = n_f // 2
    z = f // 2
    core = f % 2
    partner = z * 2 + (1 - core)

    barrier = pltpu.get_barrier_semaphore()
    for k in range(1, n_f):
        pl.semaphore_signal(barrier, inc=1, device_id=(d, (f + k) % n_f), device_id_type=pl.DeviceIdType.MESH)
    for k in range(1, n_dp):
        pl.semaphore_signal(barrier, inc=1, device_id=((d + k) % n_dp, f), device_id_type=pl.DeviceIdType.MESH)
    pl.semaphore_wait(barrier, n_f + n_dp - 2)

    loads = (
        pltpu.make_async_copy(tok_ref.at[d], tok_buf, local_sem.at[0]),
        pltpu.make_async_copy(win_ref.at[f], win_buf, local_sem.at[1]),
        pltpu.make_async_copy(gain_ref, gain_buf, local_sem.at[2]),
        pltpu.make_async_copy(pk_ref, pk_buf, local_sem.at[3]),
        pltpu.make_async_copy(cot_ref.at[d], cot_buf, local_sem.at[8]),
    )
    stores = (
        pltpu.make_async_copy(tok_buf, x_ref.at[d, f], local_sem.at[4]),
        pltpu.make_async_copy(win_buf, w_ref.at[d, f], local_sem.at[5]),
        pltpu.make_async_copy(gain_buf, g_ref.at[d, f], local_sem.at[6]),
        pltpu.make_async_copy(pk_buf, p_ref.at[d], local_sem.at[7]),
        pltpu.make_async_copy(cot_buf, c_ref.at[d], local_sem.at[9]),
    )
    for load in loads:
        load.start()

    def tok_dp(k):
        to = (d + k) % n_dp
        return remote(tok_ref.at[to], x_ref.at[d, f], tdp_send.at[k], tdp_recv.at[k], (to, f))

    def tok_dp_arrival(k):
        src = (d - k + n_dp) % n_dp
        return remote(tok_ref.at[d], x_ref.at[src, f], tdp_send.at[k], tdp_recv.at[k], (src, f))

    def cot_dp(k):
        to = (d + k) % n_dp
        return remote(cot_ref.at[to], c_ref.at[d], cdp_send.at[k], cdp_recv.at[k], (to, f))

    def cot_dp_arrival(k):
        src = (d - k + n_dp) % n_dp
        return remote(cot_ref.at[d], c_ref.at[src], cdp_send.at[k], cdp_recv.at[k], (src, f))

    def w1(k):
        to = (f + k) % n_f
        return remote(win_ref.at[to], w_ref.at[d, f], w1_send.at[k], w1_recv.at[k], (d, to))

    def w1_arrival(k):
        src = (f - k + n_f) % n_f
        return remote(win_ref.at[f], w_ref.at[d, src], w1_send.at[k], w1_recv.at[k], (d, src))

    def g1(k):
        to = (f + k) % n_f
        return remote(gain_ref, g_ref.at[d, f], g1_send.at[k], g1_recv.at[k], (d, to))

    def g1_arrival(k):
        src = (f - k + n_f) % n_f
        return remote(gain_ref, g_ref.at[d, src], g1_send.at[k], g1_recv.at[k], (d, src))

    def w2(k):
        to = (d + k) % n_dp
        return remote(w_ref.at[d], w_ref.at[d], w2_send.at[k], w2_recv.at[k], (to, f))

    def w2_arrival(k):
        src = (d - k + n_dp) % n_dp
        return remote(w_ref.at[src], w_ref.at[src], w2_send.at[k], w2_recv.at[k], (src, f))

    def g2(k):
        to = (d + k) % n_dp
        return remote(g_ref.at[d], g_ref.at[d], g2_send.at[k], g2_recv.at[k], (to, f))

    def g2_arrival(k):
        src = (d - k + n_dp) % n_dp
        return remote(g_ref.at[src], g_ref.at[src], g2_send.at[k], g2_recv.at[k], (src, f))

    def pk(k):
        to = (d + k) % n_dp
        return remote(pk_ref, p_ref.at[d], p_send.at[k], p_recv.at[k], (to, f))

    def pk_arrival(k):
        src = (d - k + n_dp) % n_dp
        return remote(pk_ref, p_ref.at[src], p_send.at[k], p_recv.at[k], (src, f))

    def block(j, origin, side):
        at = (d - j + n_dp) % n_dp
        return x_ref.at[at, origin * 2 + side]

    def up(j, origin, src=None):
        ref = block(j, origin, core)
        return remote(ref if src is None else src, ref, up_send.at[origin, j], up_recv.at[origin, j], (d, f + 2))

    def down(j, origin, src=None):
        ref = block(j, origin, core)
        return remote(ref if src is None else src, ref, down_send.at[origin, j], down_recv.at[origin, j], (d, f - 2))

    def across(j, origin, src=None):
        ref = block(j, origin, core)
        return remote(
            ref if src is None else src, ref, core_send.at[origin, j], core_recv.at[origin, j], (d, partner)
        )

    def across_arrival(j, origin):
        ref = block(j, origin, 1 - core)
        return remote(ref, ref, core_send.at[origin, j], core_recv.at[origin, j], (d, partner))

    def launch(j, src=None):
        @pl.when(z < n_z - 1)
        def _():
            up(j, z, src).start()

        @pl.when(z > 0)
        def _():
            down(j, z, src).start()

        across(j, z, src).start()

    for k in range(1, n_f):
        w1(k).start()
    for k in range(1, n_dp):
        tok_dp(k).start()
    launch(0, tok_ref.at[d])
    for k in range(1, n_f):
        g1(k).start()
    for k in range(1, n_dp):
        pk(k).start()
    for k in range(1, n_dp):
        cot_dp(k).start()
    for load, store in zip(loads, stores):
        load.wait()
        store.start()
    for k in range(1, n_dp):
        tok_dp_arrival(k).wait_recv()
        launch(k)
    for store in stores:
        store.wait()
    for k in range(1, n_f):
        w1_arrival(k).wait_recv()
        g1_arrival(k).wait_recv()
    for k in range(1, n_dp):
        w2(k).start()
        g2(k).start()
    for far in range(1, n_z):
        for j in range(n_dp):

            @pl.when(z >= far)
            def _():
                origin = z - far
                up(j, origin).wait_recv()

                @pl.when(z < n_z - 1)
                def _():
                    up(j, origin).start()

                across(j, origin).start()

            @pl.when(z + far < n_z)
            def _():
                origin = z + far
                down(j, origin).wait_recv()

                @pl.when(z > 0)
                def _():
                    down(j, origin).start()

                across(j, origin).start()

    for origin in range(n_z):
        for j in range(n_dp):
            across_arrival(j, origin).wait_recv()
            across(j, origin).wait_send()
    for origin in range(n_z):
        for j in range(n_dp):

            @pl.when((origin <= z) & (z < n_z - 1))
            def _():
                up(j, origin).wait_send()

            @pl.when((origin >= z) & (z > 0))
            def _():
                down(j, origin).wait_send()

    for k in range(1, n_dp):
        pk_arrival(k).wait_recv()
        cot_dp_arrival(k).wait_recv()
        cot_dp(k).wait_send()
        w2_arrival(k).wait_recv()
        g2_arrival(k).wait_recv()
        tok_dp(k).wait_send()
        w2(k).wait_send()
        g2(k).wait_send()
        pk(k).wait_send()
    for k in range(1, n_f):
        w1(k).wait_send()
        g1(k).wait_send()


def pack_rows(out_ref, base, main, rest, chunk):
    part = chunk // 4
    for q in range(main.shape[0] // chunk):
        out_ref[base + q, 0:chunk, :] = main[q * chunk : (q + 1) * chunk, :]
        for j in range(4):
            first = q * chunk + j * part
            out_ref[base + q, chunk : chunk + part, j * 32 : (j + 1) * 32] = rest[first : first + part, :]


def combiner(scratch, main_ref, rest_ref, n_f):
    (
        part, own, one, sums, two, tops, rests, one_send, one_recv, two_send, two_recv, top_send, top_recv,
        rest_send, rest_recv, ctop_send, ctop_recv, crest_send, crest_recv,
    ) = scratch
    d = lax.axis_index("dp")
    f = lax.axis_index("fsdp")
    n_z = n_f // 2
    z = f // 2
    core = f % 2
    other = 1 - core
    partner = z * 2 + other
    chunk = tops.shape[2]

    def first(q):
        return remote(part.at[q], one.at[q // 2], one_send.at[q // 2], one_recv.at[q // 2], (d, partner))

    def second(to, k):
        return remote(sums.at[to], two.at[k], two_send.at[k], two_recv.at[k], (d, to * 2 + core))

    def third(k):
        to = ((z + k) % n_z * 2 + core,)
        return (
            remote(tops.at[z, core], tops.at[z, core], top_send.at[k], top_recv.at[k], (d,) + to),
            remote(rests.at[z, core], rests.at[z, core], rest_send.at[k], rest_recv.at[k], (d,) + to),
        )

    def third_arrival(k):
        src = (z - k + n_z) % n_z
        to = (src * 2 + core,)
        return (
            remote(tops.at[src, core], tops.at[src, core], top_send.at[k], top_recv.at[k], (d,) + to),
            remote(rests.at[src, core], rests.at[src, core], rest_send.at[k], rest_recv.at[k], (d,) + to),
        )

    def fourth(k, side):
        src = (z - k + n_z) % n_z
        return (
            remote(tops.at[src, side], tops.at[src, side], ctop_send.at[k], ctop_recv.at[k], (d, partner)),
            remote(rests.at[src, side], rests.at[src, side], crest_send.at[k], crest_recv.at[k], (d, partner)),
        )

    def enter(peers=()):
        barrier = pltpu.get_barrier_semaphore()
        for peer in peers:
            pl.semaphore_signal(barrier, inc=1, device_id=peer, device_id_type=pl.DeviceIdType.MESH)
        pl.semaphore_signal(barrier, inc=1, device_id=(d, partner), device_id_type=pl.DeviceIdType.MESH)
        for k in range(1, n_z):
            pl.semaphore_signal(
                barrier, inc=1, device_id=(d, (z + k) % n_z * 2 + core), device_id_type=pl.DeviceIdType.MESH
            )
        pl.semaphore_wait(barrier, n_z + len(peers))

    def send(q):
        @pl.when(q % 2 == other)
        def _():
            first(q).start()

    def relay(q):
        @pl.when(q % 2 == core)
        def _():
            to = q // 2
            first(q).wait_recv()
            total = part[q] + one[to]

            @pl.when(to == z)
            def _():
                own[...] = total

            @pl.when(to != z)
            def _():
                sums[to] = total.astype(sums.dtype)
                second(to, (to - z + n_z) % n_z).start()

    def close():
        total = own[...]
        for k in range(1, n_z):
            second(z, k).wait_recv()
            total = total + two[k].astype(F32)
        tops[z, core] = total[0:chunk, :].astype(tops.dtype)
        rests[z, core] = total[chunk:, :].astype(rests.dtype)
        for k in range(1, n_z):
            for copy in third(k):
                copy.start()
        for copy in fourth(0, core):
            copy.start()
        for k in range(1, n_z):
            for copy in third_arrival(k):
                copy.wait_recv()
            for copy in fourth(k, core):
                copy.start()
        for k in range(n_z):
            for copy in fourth(k, other):
                copy.wait_recv()
        quarter = chunk // 4
        for a in range(n_z):
            for b in range(2):
                at = (a * 2 + b) * chunk
                main_ref[at : at + chunk, :] = tops[a, b]
                rest = rests[a, b]
                for j in range(4):
                    rest_ref[at + j * quarter : at + (j + 1) * quarter, :] = rest[:, j * 32 : (j + 1) * 32]
        for k in range(n_z):
            first(k * 2 + other).wait_send()
            for copy in fourth(k, core):
                copy.wait_send()
            if k:
                second((z + k) % n_z, k).wait_send()
                for copy in third(k):
                    copy.wait_send()

    return enter, send, relay, close


def combine_scratch(n_f, length, rest_type):
    n_z = n_f // 2
    packed_rows = length + length // 4
    return [
        pltpu.VMEM((n_f, packed_rows, 128), F32), pltpu.VMEM((packed_rows, 128), F32),
        pltpu.VMEM((n_z, packed_rows, 128), F32), pltpu.VMEM((n_z, packed_rows, 128), HOP),
        pltpu.VMEM((n_z, packed_rows, 128), HOP), pltpu.VMEM((n_z, 2, length, 128), BF16),
        pltpu.VMEM((n_z, 2, length // 4, 128), rest_type),
    ] + [pltpu.SemaphoreType.DMA((n_z,))] * 12


def finish_kernel(
    gdtl_ref, gbc_ref, inp_ref, gis_ref, ggate_ref, inner_ref, before_ref, x_ref, gain_ref, win_ref, xw_ref, misc_ref,
    gout_ref, gback_ref, br_ref, out_ref, brout_ref, gin_out, gout_out,
    gx_out, gcw_out, gcb_out, gdt_out, gdtb_out, gdec_out, gskip_out, gg_out,
    misc_scr, tail_scr, gin_scr, gsel_scr, grest_scr, ggain_scr, pad_scr, gpad_scr, wacc_scr, cacc_scr,
    mine, theirs, passed, gin_low, side_got, line_got, side_end, line_end, gin_sum, gin_all, gout_got, gback_got, gtail_low, gtail_got,
    gg_low, gg_got, gg_sum, gg_all, br_buf, local_sem,
    one_send, one_recv, up_send, up_recv, down_send, down_recv, dp_send, dp_recv,
    r_send, r_recv, s1_send, s1_recv, l1_send, l1_recv, s2_send, s2_recv, l2_send, l2_recv, o_send, o_recv, b_send, b_recv, t_send, t_recv, g_send, g_recv,
    w2_send, w2_recv, g2_send, g2_recv, *, slots, n_dp, n_f
):
    d = lax.axis_index("dp")
    f = lax.axis_index("fsdp")
    n_z = n_f // 2
    z = f // 2
    core = f % 2
    other = 1 - core
    partner = z * 2 + other
    rows, width = inp_ref.shape
    steps = rows // slots
    halo = 3 * slots
    i = pl.program_id(0)
    blocks = mine.shape[0] * mine.shape[1] * mine.shape[2] // rows
    last = blocks - 1
    tile = mine.shape[2]
    held = rows // tile
    per = n_f // held
    pairs = held // 2
    rank = gdtl_ref.shape[1]
    d_rows, inner_rows = gin_out.shape[0], gout_out.shape[0]

    def place(q):
        return (last - q) // per, (last - q) % per * pairs

    def one(to, j):
        return remote(
            mine.at[to * 2 + other, j], theirs.at[to, j], one_send.at[to, j], one_recv.at[to, j], (d, partner)
        )

    def up(to, j):
        return remote(
            mine.at[to * 2 + core, j], passed.at[to + 1, j], up_send.at[to, j], up_recv.at[to, j], (d, f + 2)
        )

    def down(to, j):
        return remote(
            mine.at[to * 2 + core, j], passed.at[to, j], down_send.at[to, j], down_recv.at[to, j], (d, f - 2)
        )

    def dp(k):
        to = (d + k) % n_dp
        return remote(mine.at[f, to], out_ref.at[d], dp_send.at[k], dp_recv.at[k], (to, f))

    def dp_arrival(k):
        src = (d - k + n_dp) % n_dp
        return remote(mine.at[f, src], out_ref.at[src], dp_send.at[k], dp_recv.at[k], (src, f))

    def over_dp(src, dst, send, recv):
        return [
            remote(src.at[(d + k) % n_dp], dst.at[k], send.at[k], recv.at[k], ((d + k) % n_dp, f))
            for k in range(1, n_dp)
        ]

    def over_f(src, dst, send, recv, k):
        to = (f + k) % n_f
        return remote(src.at[to], dst.at[f], send.at[k], recv.at[k], (d, to))

    def over_f_arrival(src, dst, send, recv, k):
        to = (f - k + n_f) % n_f
        return remote(src.at[to], dst.at[to], send.at[k], recv.at[k], (d, to))

    def branch(k):
        to = (d + k) % n_dp
        return remote(br_ref.at[to], brout_ref.at[d], r_send.at[k], r_recv.at[k], (to, f))

    def branch_arrival(k):
        src = (d - k + n_dp) % n_dp
        return remote(br_ref.at[src], brout_ref.at[src], r_send.at[k], r_recv.at[k], (src, f))

    get_branch = pltpu.make_async_copy(br_ref.at[d], br_buf, local_sem.at[3])
    put_branch = pltpu.make_async_copy(br_buf, brout_ref.at[d], local_sem.at[4])
    outs = lambda: over_dp(gout_ref, gout_got, o_send, o_recv)
    backs = lambda: over_dp(gback_ref, gback_got, b_send, b_recv)

    n_a = n_dp // 2
    half = n_f // 2
    mine_a = d // 2
    mine_b = d % 2
    front_half, back_half = pl.ds(0, half), pl.ds(half, half)

    def side_first(a):
        return remote(
            gin_low.at[a * 2 + 1 - mine_b, front_half], side_got.at[a], s1_send.at[a], s1_recv.at[a],
            (mine_a * 2 + 1 - mine_b, f),
        )

    def line_first(k, b):
        to = (mine_a + k) % n_a
        return remote(
            gin_low.at[to * 2 + b, back_half], line_got.at[k, b], l1_send.at[k, b], l1_recv.at[k, b],
            (to * 2 + mine_b, f),
        )

    def line_second(k):
        to = (mine_a + k) % n_a
        return remote(
            gin_low.at[to * 2 + mine_b, front_half], line_end.at[k], l2_send.at[k], l2_recv.at[k], (to * 2 + mine_b, f)
        )

    def side_second():
        return remote(
            gin_low.at[mine_a * 2 + 1 - mine_b, back_half], side_end, s2_send.at[0], s2_recv.at[0],
            (mine_a * 2 + 1 - mine_b, f),
        )

    def firsts():
        return [side_first(a) for a in range(n_a)] + [line_first(k, b) for k in range(1, n_a) for b in range(2)]

    def seconds():
        return [line_second(k) for k in range(1, n_a)] + [side_second()]

    def middle():
        for copy in firsts():
            copy.wait_recv()

        def add(q, carry):
            for a in range(n_a):
                at = a * 2 + mine_b
                gin_low[at, q] = (gin_low[at, q].astype(F32) + side_got[a, q].astype(F32)).astype(gin_low.dtype)
            for b in range(2):
                at = mine_a * 2 + b
                total = gin_low[at, half + q].astype(F32)
                for k in range(1, n_a):
                    total = total + line_got[k, b, q].astype(F32)
                gin_low[at, half + q] = total.astype(gin_low.dtype)
            return carry

        lax.fori_loop(0, half, add, 0)
        for copy in seconds():
            copy.start()

    tails = lambda: over_dp(gtail_low, gtail_got, t_send, t_recv)
    gains = lambda: over_dp(gg_low, gg_got, g_send, g_recv)
    own_out = pltpu.make_async_copy(gout_ref.at[d], gout_got.at[0], local_sem.at[0])
    own_back = pltpu.make_async_copy(gback_ref.at[d], gback_got.at[0], local_sem.at[1])
    put = pltpu.make_async_copy(mine.at[f, d], out_ref.at[d], local_sem.at[2])

    def send_halves(q):
        j, first = place(q)
        for a in range(pairs):
            one(first + a, j).start()

    def pair(to, j):
        one(to, j).wait_recv()
        return mine[to * 2 + core, j].astype(F32) + theirs[to, j].astype(F32)

    def hops(step):
        q_up = step - 1 - LAG * z
        q_down = step - 1 - LAG * (n_z - 1 - z)
        q_end = step - 1 - LAG * jnp.maximum(z, n_z - 1 - z)

        @pl.when((q_up >= 0) & (q_up < blocks))
        def _():
            j, first = place(q_up)
            for a in range(pairs):
                to = first + a

                @pl.when(to > z)
                def _():
                    mine[to * 2 + core, j] = pair(to, j).astype(mine.dtype)

                    @pl.when(z > 0)
                    def _():
                        up(to, j).wait_recv()
                        mine[to * 2 + core, j] = (
                            mine[to * 2 + core, j].astype(F32) + passed[to + 1, j].astype(F32)
                        ).astype(mine.dtype)

            for a in range(pairs):

                @pl.when(first + a > z)
                def _():
                    up(first + a, j).start()

        @pl.when((q_down >= 0) & (q_down < blocks))
        def _():
            j, first = place(q_down)
            for a in range(pairs):
                to = first + a

                @pl.when(to < z)
                def _():
                    mine[to * 2 + core, j] = pair(to, j).astype(mine.dtype)

                    @pl.when(z < n_z - 1)
                    def _():
                        down(to, j).wait_recv()
                        mine[to * 2 + core, j] = (
                            mine[to * 2 + core, j].astype(F32) + passed[to, j].astype(F32)
                        ).astype(mine.dtype)

            for a in range(pairs):

                @pl.when(first + a < z)
                def _():
                    down(first + a, j).start()

        @pl.when((q_end >= 0) & (q_end < blocks))
        def _():
            j, first = place(q_end)

            @pl.when((z >= first) & (z < first + pairs))
            def _():
                mine[f, j] = pair(z, j).astype(mine.dtype)

                @pl.when(z > 0)
                def _():
                    up(z, j).wait_recv()
                    mine[f, j] = (mine[f, j].astype(F32) + passed[z + 1, j].astype(F32)).astype(mine.dtype)

                @pl.when(z < n_z - 1)
                def _():
                    down(z, j).wait_recv()
                    mine[f, j] = (mine[f, j].astype(F32) + passed[z, j].astype(F32)).astype(mine.dtype)

                for k in range(n_dp):

                    @pl.when(j == (d + k) % n_dp)
                    def _():
                        if k:
                            dp(k).start()
                        else:
                            put.start()

    @pl.when(i == 0)
    def _():
        barrier = pltpu.get_barrier_semaphore()
        for k in range(1, n_f):
            pl.semaphore_signal(barrier, inc=1, device_id=(d, (f + k) % n_f), device_id_type=pl.DeviceIdType.MESH)
        for k in range(1, n_dp):
            pl.semaphore_signal(barrier, inc=1, device_id=((d + k) % n_dp, f), device_id_type=pl.DeviceIdType.MESH)
        pl.semaphore_wait(barrier, n_f + n_dp - 2)
        for copy in outs() + backs():
            copy.start()
        for k in range(1, n_dp):
            branch(k).start()
        get_branch.start()
        own_out.start()
        own_back.start()
        gpad_scr[rows : rows + halo, :] = jnp.zeros((halo, width), F32)
        wacc_scr[...] = jnp.zeros_like(wacc_scr)
        cacc_scr[...] = jnp.zeros_like(cacc_scr)
        gin_scr[...] = jnp.zeros_like(gin_scr)
        gsel_scr[...] = jnp.zeros_like(gsel_scr)
        grest_scr[...] = jnp.zeros_like(grest_scr)
        ggain_scr[...] = jnp.zeros_like(ggain_scr)
        misc_scr[...] = jnp.transpose(misc_ref[...].astype(F32))

    @pl.when(i > 0)
    def _():
        send_halves(i - 1)

    gdtl = gdtl_ref[...]
    gbc = gbc_ref[...]
    inp = inp_ref[...]
    gsel_scr[...] += dot(inp, gdtl, ((0,), (0,)))
    grest_scr[:, :DECAY] += dot(inp, gbc, ((0,), (0,)))
    g_inputs = (
        gis_ref[...]
        + dot(gdtl, xw_ref[...], ((1,), (1,)))
        + dot(gbc, misc_ref[:, :DECAY], ((1,), (1,)))
    )
    pad_scr[0:halo, :] = before_ref[slots : slots + halo, :] * (i < last).astype(F32)
    pad_scr[halo : halo + rows, :] = inner_ref[...]
    total = jnp.broadcast_to(misc_scr[CONV_BIAS : CONV_BIAS + 1, :], (rows, width))
    for tap in range(4):
        total = total + misc_scr[TAPS + tap : TAPS + tap + 1, :] * pad_scr[tap * slots : tap * slots + rows, :]
    sig = sigmoid(total)
    g_conv = g_inputs * (sig * (1.0 + total * (1.0 - sig)))
    gpad_scr[0:rows, :] = g_conv
    g_inner = jnp.zeros((rows, width), F32)
    for tap in range(4):
        back = (3 - tap) * slots
        g_inner = g_inner + misc_scr[TAPS + tap : TAPS + tap + 1, :] * gpad_scr[back : back + rows, :]
        wacc_scr[tap] += jnp.sum(
            (g_conv * pad_scr[tap * slots : tap * slots + rows, :]).reshape(steps, slots, width), axis=0
        )
    cacc_scr[...] += jnp.sum(g_conv.reshape(steps, slots, width), axis=0)
    gpad_scr[rows : rows + halo, :] = gpad_scr[0:halo, :]
    g_both = jnp.concatenate([g_inner.astype(BF16), ggate_ref[...]], axis=1)
    x = x_ref[...].astype(F32)
    scaled = x * lax.rsqrt(jnp.mean(x * x, axis=-1, keepdims=True) + EPSILON)
    gin_scr[...] += dot((scaled * gain_ref[...]).astype(BF16), g_both, ((0,), (0,)))
    g_normed = dot(g_both, win_ref[...], ((1,), (1,)))
    ggain_scr[...] += jnp.sum(g_normed * scaled, axis=0, keepdims=True)
    block, first = place(i)
    for a in range(held):
        mine[first * 2 + a, block] = g_normed[a * tile : (a + 1) * tile, :].astype(mine.dtype)
    hops(i)

    @pl.when(i == last)
    def _():
        for a in range(n_dp):
            for b in range(n_f):
                at = (a * n_f + b) * d_rows
                gin_low[a, b] = gin_scr[at : at + d_rows, :].astype(gin_low.dtype)
                gg_low[a, b] = jnp.zeros((8, 128), F32)
                gg_low[a, b, 0:1, 0:d_rows] = ggain_scr[:, at : at + d_rows]
        tail_scr[...] = jnp.zeros_like(tail_scr)
        for tap in range(4):
            tail_scr[TAPS + tap : TAPS + tap + 1, :] = jnp.sum(wacc_scr[tap], axis=0, keepdims=True)
        tail_scr[CONV_BIAS : CONV_BIAS + 1, :] = jnp.sum(cacc_scr[...], axis=0, keepdims=True)
        grest_scr[:, DECAY:] = jnp.transpose(tail_scr[...])[:, DECAY:]
        for a in range(n_dp):
            at = a * inner_rows
            gtail_low[a, :, :rank] = gsel_scr[at : at + inner_rows, :]
            gtail_low[a, :, rank:] = grest_scr[at : at + inner_rows, :]
        send_halves(last)
        for copy in firsts() + tails() + gains():
            copy.start()
        hops(blocks)
        get_branch.wait()
        put_branch.start()
        own_out.wait()
        own_back.wait()
        for copy in outs() + backs():
            copy.wait_recv()
        total = gout_got[0].astype(F32)
        for k in range(1, n_dp):
            total = total + gout_got[k].astype(F32)
        gout_out[...] = total
        total = gback_got[0]
        for k in range(1, n_dp):
            total = total + gback_got[k]
        gdt_out[...] = total[:, :rank]
        total = jnp.transpose(total[:, rank:])
        gdec_out[...] = total[DECAY:TAPS, :]
        gdtb_out[...] = total[DT_BIAS : DT_BIAS + 1, :]
        gskip_out[...] = total[SKIP : SKIP + 1, :]

        def drain(step, carry):
            hops(step)
            return carry

        lax.fori_loop(blocks + 1, blocks + 1 + MID, drain, 0)
        middle()
        lax.fori_loop(blocks + 1 + MID, blocks + 1 + LAG * (n_z - 1), drain, 0)

        for copy in seconds() + tails() + gains():
            copy.wait_recv()

        def add(q, carry):
            total = gin_low[d, q].astype(F32)
            for k in range(1, n_a):
                total = total + line_end[k, q].astype(F32)
            gin_sum[q] = total.astype(gin_sum.dtype)
            total = gin_low[d, half + q].astype(F32) + side_end[q].astype(F32)
            gin_sum[half + q] = total.astype(gin_sum.dtype)
            return carry

        lax.fori_loop(0, half, add, 0)

        def add_gain(q, carry):
            total = gg_low[d, q]
            for k in range(1, n_dp):
                total = total + gg_got[k, q]
            gg_sum[q] = total
            return carry

        lax.fori_loop(0, n_f, add_gain, 0)
        for k in range(1, n_f):
            over_f(gin_sum, gin_all, w2_send, w2_recv, k).start()
            over_f(gg_sum, gg_all, g2_send, g2_recv, k).start()
        gin_all[f] = gin_sum[f]
        gg_all[f] = gg_sum[f]
        total = gtail_low[d]
        for k in range(1, n_dp):
            total = total + gtail_got[k]
        gx_out[:rank, :] = jnp.transpose(total[:, :rank])
        total = jnp.transpose(total[:, rank:])
        gx_out[rank:, :] = total[:DECAY, :]
        gcw_out[...] = total[TAPS:CONV_BIAS, :]
        gcb_out[...] = total[CONV_BIAS : CONV_BIAS + 1, :]
        for k in range(1, n_f):
            over_f_arrival(gin_sum, gin_all, w2_send, w2_recv, k).wait_recv()
            over_f_arrival(gg_sum, gg_all, g2_send, g2_recv, k).wait_recv()
        total = gg_all[0]
        for b in range(1, n_f):
            total = total + gg_all[b]
        gg_out[...] = total[0:1, 0:d_rows]
        for b in range(n_f):
            for h in range(2):
                for a in range(n_dp):
                    to = (h * n_dp + a) * n_f * inner_rows + b * inner_rows
                    at = (h * n_dp + a) * inner_rows
                    gin_out[:, to : to + inner_rows] = gin_all[b, :, at : at + inner_rows].astype(F32)
        for k in range(1, n_dp):
            dp_arrival(k).wait_recv()
            dp(k).wait_send()
        put.wait()
        put_branch.wait()
        for k in range(1, n_dp):
            branch_arrival(k).wait_recv()
            branch(k).wait_send()
        for copy in outs() + backs() + firsts() + seconds() + tails() + gains():
            copy.wait_send()
        for k in range(1, n_f):
            over_f(gin_sum, gin_all, w2_send, w2_recv, k).wait_send()
            over_f(gg_sum, gg_all, g2_send, g2_recv, k).wait_send()
        for to in range(n_z):
            for j in range(n_dp):
                one(to, j).wait_send()

                @pl.when(z < to)
                def _():
                    up(to, j).wait_send()

                @pl.when(z > to)
                def _():
                    down(to, j).wait_send()


def whole(shape):
    return pl.BlockSpec(shape, lambda i: (0,) * len(shape))


def cost(micros):
    return pl.CostEstimate(flops=int(micros * 1.15e9), bytes_accessed=1 << 20, transcendentals=0)


def params(number=None):
    if number is None:
        return pltpu.CompilerParams(vmem_limit_bytes=VMEM_BYTES, dimension_semantics=("arbitrary",))
    return pltpu.CompilerParams(
        vmem_limit_bytes=FULL_VMEM, dimension_semantics=("arbitrary",), collective_id=number, has_side_effects=True
    )


def body(
    tokens, cotangent, lengths, deal_order, norm_gain, in_weight, conv_weight, conv_bias,
    x_weight, dt_weight, dt_bias, decay_log, skip_gain, out_weight, *, n_dp, n_f
):
    seqs, own, model = tokens.shape
    slots = seqs // n_dp
    inner_rows, states = decay_log.shape
    rank = dt_weight.shape[1]
    width = inner_rows * n_dp
    length = own * n_dp * n_f
    d_rows = in_weight.shape[0]
    total_rows = length * slots
    group = lax.axis_index("dp")
    member = lax.axis_index("fsdp")

    low = lambda v: v.astype(BF16)
    slot_ids = jnp.arange(seqs, dtype=jnp.int32)
    seq_len = jnp.sum(jnp.where(deal_order[:, None] == slot_ids[None, :], lengths[:, None], 0), axis=0)
    own_pos = (group * n_f + member) * own + jnp.arange(own, dtype=jnp.int32)
    own_mask = own_pos[None, :] < seq_len[:, None]

    def by_group(v):
        return v.reshape(n_dp, slots, own, model).transpose(0, 2, 1, 3).reshape(n_dp, own * slots, model)

    def by_seq(v):
        return v.reshape(n_dp, own, slots, model).transpose(0, 2, 1, 3).reshape(seqs, own, model).astype(F32)

    masked = by_group(jnp.where(own_mask[:, :, None], cotangent, jnp.zeros_like(cotangent)))

    tok = by_group(tokens)
    win = low(in_weight).reshape(d_rows, 2, n_dp, n_f, inner_rows).transpose(3, 0, 1, 2, 4)
    win = win.reshape(n_f, d_rows, 2 * width)
    gain_tile = jnp.zeros((8, 128), F32).at[0, :d_rows].set(low(norm_gain).astype(F32))
    misc = jnp.concatenate(
        [x_weight[:, rank:], decay_log, conv_weight, conv_bias[:, None], dt_bias[:, None], skip_gain[:, None]], axis=1
    )
    misc = jnp.pad(misc, ((0, 0), (0, 128 - misc.shape[1])))
    packed = low(jnp.concatenate([x_weight[:, :rank], misc, dt_weight], axis=1))
    ow = out_weight
    n_z = n_f // 2
    dma = pltpu.SemaphoreType.DMA
    hbm = pl.BlockSpec(memory_space=pl.ANY)
    x, g_branch, win, gain, packed = pl.pallas_call(
        functools.partial(gather_kernel, n_dp=n_dp, n_f=n_f),
        in_specs=[hbm] * 5,
        out_specs=[hbm] * 5,
        out_shape=[
            jax.ShapeDtypeStruct((n_dp, n_f) + tok.shape[1:], BF16),
            jax.ShapeDtypeStruct(tok.shape, BF16),
            jax.ShapeDtypeStruct((n_dp, n_f) + win.shape[1:], BF16),
            jax.ShapeDtypeStruct((n_dp, n_f, 8, 128), F32),
            jax.ShapeDtypeStruct((n_dp,) + packed.shape, BF16),
        ],
        scratch_shapes=[
            pltpu.VMEM(tok.shape[1:], BF16), pltpu.VMEM(tok.shape[1:], BF16), pltpu.VMEM(win.shape[1:], BF16),
            pltpu.VMEM((8, 128), F32), pltpu.VMEM(packed.shape, BF16), dma((10,)),
            dma((n_dp,)), dma((n_dp,)), dma((n_dp,)), dma((n_dp,)),
        ]
        + [dma((n_z, n_dp))] * 6
        + [dma((n_f,)), dma((n_f,)), dma((n_dp,)), dma((n_dp,)), dma((n_f,)), dma((n_f,))]
        + [dma((n_dp,))] * 4,
        compiler_params=pltpu.CompilerParams(collective_id=1, has_side_effects=True),
        cost_estimate=cost(90),
        name="gather",
    )(tok, masked, win, gain_tile, packed)
    x = x.reshape(total_rows, model)
    win = win.reshape(model, 2 * width)
    gain = gain[:, :, 0, :d_rows].reshape(1, model)
    packed = packed.reshape(width, -1)
    span = ROWS // slots
    rows = span * slots
    blocks = length // span
    grid = (blocks,)
    row_spec = lambda cols: pl.BlockSpec((rows, cols), lambda i: (i, 0))
    rev_spec = lambda cols: pl.BlockSpec((rows, cols), lambda i: (blocks - 1 - i, 0))
    once = dict(pipeline_mode=pl.Buffered(1))
    ow_spec = pl.BlockSpec((width, model), lambda i: (0, 0), **once)
    xw_spec = pl.BlockSpec((width, 128), lambda i: (0, 0), **once)
    misc_spec = pl.BlockSpec((width, 128), lambda i: (0, 1), **once)
    dtw_spec = pl.BlockSpec((width, 128), lambda i: (0, 2), **once)
    win_spec = pl.BlockSpec((model, 2 * width), lambda i: (0, 0), **once)
    misc_shape = pltpu.VMEM((128, width), F32)
    like = jax.ShapeDtypeStruct
    held = span // own
    per = n_f // held
    piece = (held, 1, own * slots, model)
    piece_spec = pl.BlockSpec(piece, lambda i: (i % per, i // per, 0, 0))
    rev_piece_spec = pl.BlockSpec(piece, lambda i: ((blocks - 1 - i) % per, (blocks - 1 - i) // per, 0, 0))
    pieces_shape = like((n_f, n_dp, own * slots, model), BF16)
    inner, gate, inp, dtl, bc, ow, g_branch = pl.pallas_call(
        functools.partial(front_kernel, slots=slots, length=length, n_dp=n_dp, n_f=n_f),
        grid=grid,
        in_specs=[
            row_spec(model), whole((1, model)), win_spec, xw_spec, misc_spec, hbm, hbm,
        ],
        out_specs=[
            row_spec(width), row_spec(width), row_spec(width), whole((total_rows, rank)), whole((total_rows, 2 * states)),
            hbm, hbm,
        ],
        out_shape=[
            like((total_rows, width), F32), like((total_rows, width), F32), like((total_rows, width), BF16),
            like((total_rows, rank), BF16), like((total_rows, 2 * states), F32), like((n_dp,) + ow.shape, BF16), pieces_shape,
        ],
        scratch_shapes=[
            pltpu.VMEM((rows + 3 * slots, width), F32), misc_shape, pltpu.VMEM(ow.shape, F32), pltpu.VMEM(ow.shape, BF16),
            dma((n_dp,)), dma((n_dp,)), dma((2,)), pltpu.VMEM((n_dp, own * slots, model), BF16), dma((2,)),
        ]
        + [dma((n_dp,))] * 6
        + combine_scratch(n_f, length, F32),
        compiler_params=params(2),
        cost_estimate=cost(42),
        name="front",
    )(x, gain, win, packed, packed, ow, g_branch)
    ow = ow.reshape(width, model)


    y, ck, branch, g_branch = pl.pallas_call(
        functools.partial(mix_kernel, slots=slots, n_dp=n_dp, n_f=n_f),
        grid=grid,
        in_specs=[
            row_spec(rank), row_spec(2 * states), row_spec(width), row_spec(width), dtw_spec, misc_spec, ow_spec, hbm,
        ],
        out_specs=[
            row_spec(width), pl.BlockSpec((1, states, slots, width), lambda i: (i, 0, 0, 0)), piece_spec, hbm,
        ],
        out_shape=[
            like((total_rows, width), F32), like((blocks, states, slots, width), F32), pieces_shape,
            pieces_shape,
        ],
        scratch_shapes=[
            pltpu.VMEM((states, slots, width), F32), pltpu.VMEM((rows, width), F32), pltpu.VMEM((rows, width), F32),
            pltpu.VMEM((states, slots, width), F32), pltpu.VMEM((PAIR, 2 * states, slots, 128), F32),
            pltpu.VMEM((PAIR, 2 * states, slots, 128), F32), misc_shape,
        ]
        + [dma((n_z, n_dp))] * 6,
        input_output_aliases={7: 3},
        compiler_params=params(5),
        cost_estimate=cost(36),
        name="mix",
    )(dtl, bc, inp, gate, packed, packed, ow, g_branch)

    gis, ggate, gdtl, gbc, gout, gmisc, branch = pl.pallas_call(
        functools.partial(back_kernel, slots=slots, length=length, n_dp=n_dp, n_f=n_f),
        grid=grid,
        in_specs=[
            rev_piece_spec, rev_spec(rank), rev_spec(2 * states), rev_spec(width), rev_spec(width), rev_spec(width),
            pl.BlockSpec((1, states, slots, width), lambda i: (blocks - 1 - i, 0, 0, 0)), dtw_spec, misc_spec, ow_spec,
            hbm,
        ],
        out_specs=[
            rev_spec(width), rev_spec(width), whole((total_rows, rank)), whole((total_rows, 2 * states)),
            whole((width, model)), whole((width, 256)), hbm,
        ],
        out_shape=[
            like((total_rows, width), F32), like((total_rows, width), BF16), like((total_rows, rank), BF16),
            like((total_rows, 2 * states), BF16), like((width, model), BF16), like((width, 256), F32),
            like((n_dp, own * slots, model), BF16),
        ],
        scratch_shapes=[
            pltpu.VMEM((states, slots, width), F32), pltpu.VMEM((states, slots, width), F32),
            pltpu.VMEM((slots, width), F32), pltpu.VMEM((slots, width), F32), pltpu.VMEM((states, slots, width), F32),
        ]
        + [pltpu.VMEM((rows, width), F32)] * 5
        + [
            pltpu.VMEM((span, states, slots, width), F32), pltpu.VMEM((span, states, slots, width), F32),
            pltpu.VMEM((2 * states, rows, 128), F32), pltpu.VMEM((PAIR, 2 * states, slots, 128), F32),
            pltpu.VMEM((PAIR, 2 * states, slots, 128), F32), pltpu.VMEM((2 * states, rows), F32),
            pltpu.VMEM((states, slots, width), F32), pltpu.VMEM((rows, 2 * states), F32), misc_shape, misc_shape,
            pltpu.VMEM((width, model), F32), pltpu.VMEM((n_z, n_dp, own * slots, model), BF16),
            pltpu.VMEM((n_z, n_dp, own * slots, model), BF16), pltpu.VMEM((n_z + 1, n_dp, own * slots, model), BF16),
            dma((n_z, n_dp)), dma((1,)),
        ]
        + [dma((n_z, n_dp))] * 6
        + combine_scratch(n_f, length, BF16),
        compiler_params=params(3),
        cost_estimate=cost(100),
        name="back",
    )(g_branch, dtl, bc, inp, gate, y, ck, packed, packed, ow, branch)


    tile = own * slots
    vmem = pltpu.VMEM
    g_normed, branch, gin, gout, gx, gcw, gcb, gdt, gdtb, gdec, gskip, ggain = pl.pallas_call(
        functools.partial(finish_kernel, slots=slots, n_dp=n_dp, n_f=n_f),
        grid=grid,
        in_specs=[
            rev_spec(rank), rev_spec(2 * states), rev_spec(width), rev_spec(width), rev_spec(width), rev_spec(width),
            pl.BlockSpec((4 * slots, width), lambda i: (jnp.maximum((blocks - 1 - i) * (span // 4) - 1, 0), 0)),
            rev_spec(model), whole((1, model)), win_spec, xw_spec, misc_spec, hbm, hbm, hbm,
        ],
        out_specs=[
            hbm, hbm, whole((d_rows, 2 * width * n_f)), whole((inner_rows, model)),
            whole((rank + 2 * states, inner_rows)), whole((4, inner_rows)), whole((1, inner_rows)),
            whole((inner_rows, rank)), whole((1, inner_rows)), whole((states, inner_rows)), whole((1, inner_rows)),
            whole((1, d_rows)),
        ],
        out_shape=[
            like((n_dp, tile, model), BF16), like((n_dp, tile, model), BF16), like((d_rows, 2 * width * n_f), F32), like((inner_rows, model), F32),
            like((rank + 2 * states, inner_rows), F32), like((4, inner_rows), F32), like((1, inner_rows), F32),
            like((inner_rows, rank), F32), like((1, inner_rows), F32), like((states, inner_rows), F32),
            like((1, inner_rows), F32), like((1, d_rows), F32),
        ],
        scratch_shapes=[
            misc_shape, misc_shape, vmem((model, 2 * width), F32), vmem((width, 128), F32), vmem((width, 128), F32),
            vmem((1, model), F32), vmem((rows + 3 * slots, width), F32), vmem((rows + 3 * slots, width), F32),
            vmem((4, slots, width), F32), vmem((slots, width), F32),
            vmem((n_f, n_dp, tile, model), BF16), vmem((n_z, n_dp, tile, model), BF16),
            vmem((n_z + 1, n_dp, tile, model), BF16),
            vmem((n_dp, n_f, d_rows, 2 * width), BF16), vmem((n_dp // 2, n_z, d_rows, 2 * width), BF16),
            vmem((n_dp // 2, 2, n_z, d_rows, 2 * width), BF16), vmem((n_z, d_rows, 2 * width), BF16),
            vmem((n_dp // 2, n_z, d_rows, 2 * width), BF16),
            vmem((n_f, d_rows, 2 * width), BF16), vmem((n_f, d_rows, 2 * width), BF16),
            vmem((n_dp, inner_rows, model), BF16), vmem((n_dp, inner_rows, 256), F32),
            vmem((n_dp, inner_rows, 256), F32), vmem((n_dp, inner_rows, 256), F32),
            vmem((n_dp, n_f, 8, 128), F32), vmem((n_dp, n_f, 8, 128), F32), vmem((n_f, 8, 128), F32),
            vmem((n_f, 8, 128), F32), vmem((tile, model), BF16), dma((5,)),
        ]
        + [dma((n_z, n_dp))] * 6
        + [dma((n_dp,))] * 4
        + [dma((n_dp // 2,))] * 2
        + [dma((n_dp // 2, 2))] * 2
        + [dma((1,))] * 2
        + [dma((n_dp // 2,))] * 2
        + [dma((n_dp,))] * 8
        + [dma((n_f,))] * 4,
        compiler_params=params(4),
        cost_estimate=cost(105),
        name="finish",
    )(
        gdtl, gbc, inp, gis, ggate, inner, inner, x, gain, win, packed, packed,
        gout.reshape(n_dp, inner_rows, model), gmisc.reshape(n_dp, inner_rows, 256), branch,
    )

    hidden = tokens.astype(F32)
    upstream = cotangent.astype(F32)
    output = (hidden + jnp.where(own_mask[:, :, None], by_seq(branch), 0.0)).astype(BF16)
    g_normed = by_seq(g_normed)
    factor = lax.rsqrt(jnp.mean(hidden * hidden, axis=-1, keepdims=True) + EPSILON)
    weighted = gain * g_normed
    input_grad = (
        upstream + factor * weighted - hidden * factor**3 * jnp.mean(hidden * weighted, axis=-1, keepdims=True)
    ).astype(BF16)
    return (
        output, input_grad, ggain.reshape(d_rows), gin, gcw.T, gcb.reshape(inner_rows), gx.T, gdt,
        gdtb.reshape(inner_rows), gdec.T, gskip.reshape(inner_rows), gout,
    )


def solution(mesh):
    rows1, rows2, pos = P(BOTH), P(BOTH, None), P(None, BOTH, None)
    return jax.shard_map(
        functools.partial(body, n_dp=mesh.shape["dp"], n_f=mesh.shape["fsdp"]),
        mesh=mesh,
        in_specs=(pos, pos, P(), P(), rows1, rows2, rows2, rows1, rows2, rows2, rows1, rows2, rows1, rows2),
        out_specs=(pos, pos, rows1, rows2, rows2, rows1, rows2, rows2, rows1, rows2, rows1, rows2),
        check_vma=False,
    )
```

```python
import functools
import jax
import jax.numpy as jnp
from jax import lax
from jax.experimental import pallas as pl
from jax.experimental.pallas import tpu as pltpu
from jax.sharding import PartitionSpec as P

EPSILON = 1e-05
ROWS = 256
PAIR = 2
LAG = 4
MID = 3
HOP = jnp.bfloat16
LANES = 8
TOGETHER = 8
LOG2E = 1.4426950408889634
BOTH = ("dp", "fsdp")
F32 = jnp.float32
BF16 = jnp.bfloat16
VMEM_BYTES = 60 * 1024 * 1024
FULL_VMEM = 63 * 1024 * 1024
DECAY, TAPS, CONV_BIAS, DT_BIAS, SKIP = 32, 48, 52, 53, 54


def dot(a, b, dims=((1,), (0,))):
    return lax.dot_general(a, b, (dims, ((), ())), preferred_element_type=F32)


def sigmoid(v):
    return 1.0 / (1.0 + jnp.exp(-v))


def softplus(v):
    return jnp.maximum(v, 0.0) + jnp.log1p(jnp.exp(-jnp.abs(v)))


def rms_normed(x, gain):
    factor = lax.rsqrt(jnp.mean(x * x, axis=-1, keepdims=True) + EPSILON)
    return (x * factor * gain).astype(BF16)


def front_kernel(
    x_ref, gain_ref, win_ref, xw_ref, misc_ref, ow_ref, cin_ref, inner_ref, gate_ref, inp_ref, dtl_ref, bc_ref, owf_ref, c_ref,
    pad_ref, misc_scr, ow_raw, ow_buf, ow_send, ow_recv, ow_local, c_buf, c_local,
    cu_send, cu_recv, cd_send, cd_recv, ca_send, ca_recv, *scratch, slots, length, n_dp, n_f
):
    d = lax.axis_index("dp")
    f = lax.axis_index("fsdp")

    def ow(k):
        return remote(ow_buf, owf_ref.at[d], ow_send.at[k], ow_recv.at[k], ((d + k) % n_dp, f))

    def ow_arrival(k):
        src = (d - k + n_dp) % n_dp
        return remote(ow_buf, owf_ref.at[src], ow_send.at[k], ow_recv.at[k], (src, f))

    n_z = n_f // 2
    z = f // 2
    partner = z * 2 + 1 - f % 2

    def c_up(j, src):
        return remote(cin_ref.at[j], c_ref.at[src, j], cu_send.at[j], cu_recv.at[j], (d, f + 2))

    def c_down(j, src):
        return remote(cin_ref.at[j], c_ref.at[src, j], cd_send.at[j], cd_recv.at[j], (d, f - 2))

    def c_across(j, src):
        return remote(cin_ref.at[j], c_ref.at[src, j], ca_send.at[j], ca_recv.at[j], (d, partner))

    c_get = pltpu.make_async_copy(cin_ref, c_buf, c_local.at[0])
    c_put = pltpu.make_async_copy(c_buf, c_ref.at[f], c_local.at[1])
    ow_get = pltpu.make_async_copy(ow_ref, ow_raw, ow_local.at[0])
    ow_put = pltpu.make_async_copy(ow_buf, owf_ref.at[d], ow_local.at[1])
    enter, send, relay, close = combiner(scratch, dtl_ref, bc_ref, n_f)
    i = pl.program_id(0)
    last = pl.num_programs(0) - 1
    rows = x_ref.shape[0]
    width = inner_ref.shape[1]
    halo = 3 * slots
    parts = rows // length

    @pl.when(i == 0)
    def _():
        enter([((d + k) % n_dp, f) for k in range(1, n_dp)])
        ow_get.start()
        c_get.start()
        for j in range(n_dp):

            @pl.when(z < n_z - 1)
            def _():
                c_up(j, f).start()

            @pl.when(z > 0)
            def _():
                c_down(j, f).start()

            c_across(j, f).start()

    @pl.when(i == 1)
    def _():
        ow_get.wait()
        ow_buf[...] = ow_raw[...].astype(BF16)
        c_get.wait()
        c_put.start()

    @pl.when(i == 2)
    def _():
        ow_put.start()
        for k in range(1, n_dp):
            ow(k).start()

    @pl.when(i > 0)
    def _():
        for a in range(parts):
            send((i - 1) * parts + a)

    normed = rms_normed(x_ref[...].astype(F32), gain_ref[...])
    both = dot(normed, win_ref[...])
    gate_ref[...] = both[:, width:]
    inner = both[:, :width]
    inner_ref[...] = inner

    @pl.when(pl.program_id(0) == 0)
    def _():
        pad_ref[0:halo, :] = jnp.zeros((halo, width), F32)
        misc_scr[...] = jnp.transpose(misc_ref[...].astype(F32))

    pad_ref[halo : halo + rows, :] = inner
    total = jnp.broadcast_to(misc_scr[CONV_BIAS : CONV_BIAS + 1, :], (rows, width))
    for tap in range(4):
        total = total + misc_scr[TAPS + tap : TAPS + tap + 1, :] * pad_ref[tap * slots : tap * slots + rows, :]
    inp = (total * sigmoid(total)).astype(BF16)
    inp_ref[...] = inp
    pack_rows(scratch[0], i * parts, dot(inp, xw_ref[...]), dot(inp, misc_ref[...])[:, :DECAY], length)
    pad_ref[0:halo, :] = pad_ref[rows : rows + halo, :]

    @pl.when(i > 0)
    def _():
        for a in range(parts):
            relay((i - 1) * parts + a)

    @pl.when(i == last)
    def _():
        for a in range(parts):
            send(i * parts + a)
        for a in range(parts):
            relay(i * parts + a)
        close()
        c_put.wait()
        for j in range(n_dp):

            @pl.when(z > 0)
            def _():
                c_up(j, f - 2).wait_recv()
                c_down(j, f).wait_send()

            @pl.when(z < n_z - 1)
            def _():
                c_down(j, f + 2).wait_recv()
                c_up(j, f).wait_send()

            c_across(j, partner).wait_recv()
            c_across(j, f).wait_send()

        ow_put.wait()
        for k in range(1, n_dp):
            ow_arrival(k).wait_recv()
            ow(k).wait_send()


def spread_lanes(bc_ref, out_ref, k, slots, steps):
    for j in range(PAIR):
        t = jnp.minimum(k * PAIR + j, steps - 1)
        at = pl.ds(pl.multiple_of(t * slots, slots), slots)
        for n in range(out_ref.shape[1]):
            out_ref[j, n] = jnp.broadcast_to(bc_ref[at, n : n + 1], (slots, 128))


def widen(piece, width):
    return jnp.concatenate([piece] * (width // 128), axis=1)


def narrow(value):
    total = value[:, :128]
    for first in range(128, value.shape[1], 128):
        total = total + value[:, first : first + 128]
    return total


def mix_kernel(
    dtl_ref, bc_ref, inp_ref, gate_ref, dtw_ref, misc_ref, ow_ref, near_ref,
    y_ref, ck_ref, br_ref, c_ref, h_scr, delta_scr, u_scr, rate_scr, even_scr, odd_scr, misc_scr,
    up_send, up_recv, down_send, down_recv, core_send, core_recv, *, slots, n_dp, n_f
):
    d = lax.axis_index("dp")
    f = lax.axis_index("fsdp")
    n_z = n_f // 2
    z = f // 2
    core = f % 2
    partner = z * 2 + 1 - core
    i = pl.program_id(0)
    last = pl.num_programs(0) - 1

    def up(j, o):
        ref = c_ref.at[o * 2 + core, j]
        return remote(ref, ref, up_send.at[o, j], up_recv.at[o, j], (d, f + 2))

    def down(j, o):
        ref = c_ref.at[o * 2 + core, j]
        return remote(ref, ref, down_send.at[o, j], down_recv.at[o, j], (d, f - 2))

    def across(j, o, side):
        ref = c_ref.at[o * 2 + side, j]
        return remote(ref, ref, core_send.at[o, j], core_recv.at[o, j], (d, partner))

    def far(k, js):
        for j in js:

            @pl.when(z >= k)
            def _():
                if k > 1:
                    up(j, z - k).wait_recv()

                @pl.when(z < n_z - 1)
                def _():
                    up(j, z - k).start()

                across(j, z - k, core).start()

            @pl.when(z + k < n_z)
            def _():
                if k > 1:
                    down(j, z + k).wait_recv()

                @pl.when(z > 0)
                def _():
                    down(j, z + k).start()

                across(j, z + k, core).start()

    @pl.when(i == 0)
    def _():
        barrier = pltpu.get_barrier_semaphore()
        pl.semaphore_signal(barrier, inc=1, device_id=(d, partner), device_id_type=pl.DeviceIdType.MESH)
        for k in range(1, n_z):
            pl.semaphore_signal(
                barrier, inc=1, device_id=(d, (z + k) % n_z * 2 + core), device_id_type=pl.DeviceIdType.MESH
            )
        pl.semaphore_wait(barrier, n_z)
        far(1, range(n_dp))

    @pl.when(i == 3)
    def _():
        far(2, range(n_dp // 2))

    @pl.when(i == 5)
    def _():
        far(2, range(n_dp // 2, n_dp))

    rows, width = inp_ref.shape
    steps = rows // slots
    states = h_scr.shape[0]

    @pl.when(pl.program_id(0) == 0)
    def _():
        h_scr[...] = jnp.zeros_like(h_scr)
        misc_scr[...] = jnp.transpose(misc_ref[...].astype(F32))
        for n in range(states):
            rate_scr[n] = jnp.broadcast_to(-jnp.exp(misc_scr[DECAY + n : DECAY + n + 1, :]) * LOG2E, (slots, width))

    ck_ref[0] = h_scr[...]
    delta = softplus(dot(dtl_ref[...], dtw_ref[...], ((1,), (1,))) + misc_scr[DT_BIAS : DT_BIAS + 1, :])
    delta_scr[...] = delta
    u_scr[...] = delta * inp_ref[...].astype(F32)
    spread_lanes(bc_ref, even_scr, 0, slots, steps)

    def step(k, bcb_scr, next_scr):
        spread_lanes(bc_ref, next_scr, k + 1, slots, steps)
        ats, ds, us, ys = [], [], [], []
        for j in range(PAIR):
            at = pl.ds(pl.multiple_of((k * PAIR + j) * slots, slots), slots)
            ats.append(at)
            ds.append(delta_scr[at, :])
            us.append(u_scr[at, :])
            ys.append(None)
        for n in range(states):
            rate = rate_scr[n]
            h = h_scr[n]
            for j in range(PAIR):
                h = jnp.exp2(ds[j] * rate) * h + us[j] * widen(bcb_scr[j, n], width)
                term = h * widen(bcb_scr[j, states + n], width)
                ys[j] = term if n == 0 else ys[j] + term
            h_scr[n] = h
        for j in range(PAIR):
            y_ref[ats[j], :] = ys[j]

    def steps_twice(k, carry):
        step(2 * k, even_scr, odd_scr)
        step(2 * k + 1, odd_scr, even_scr)
        return carry

    lax.fori_loop(0, steps // PAIR // 2, steps_twice, 0)
    y = y_ref[...] + misc_scr[SKIP : SKIP + 1, :] * inp_ref[...].astype(F32)
    y_ref[...] = y
    gate = gate_ref[...]
    gated = (y * (gate * sigmoid(gate))).astype(BF16)
    br_ref[...] = dot(gated, ow_ref[...]).astype(br_ref.dtype).reshape(br_ref.shape)

    @pl.when(i == last)
    def _():
        for k in range(3, n_z):
            far(k, range(n_dp))
        for o in range(n_z):
            for j in range(n_dp):

                @pl.when(o != z)
                def _():
                    across(j, o, 1 - core).wait_recv()
                    across(j, o, core).wait_send()

                @pl.when((o < z) & (z < n_z - 1))
                def _():
                    up(j, o).wait_send()

                @pl.when((o > z) & (z > 0))
                def _():
                    down(j, o).wait_send()


def lane_sums(parts):
    lane = lax.broadcasted_iota(jnp.int32, parts[0].shape, 1)
    bit = 1
    while len(parts) > 1:
        low = (lane & bit) == 0
        merged = []
        for j in range(0, len(parts), 2):
            kept = jnp.where(low, parts[j], parts[j + 1])
            moved = jnp.where(low, parts[j + 1], parts[j])
            merged.append(kept + pltpu.roll(moved, bit, 1))
        parts = merged
        bit *= 2
    total = parts[0]
    while bit < total.shape[1]:
        total = total + pltpu.roll(total, bit, 1)
        bit *= 2
    return total


def back_kernel(
    gb_ref, dtl_ref, bc_ref, inp_ref, gate_ref, y_ref, ck_ref, dtw_ref, misc_ref, ow_ref, br_ref,
    gis_ref, ggate_ref, gdtl_ref, gbcs_ref, gout_ref, gmisc_ref, brr_ref,
    lam_scr, dacc_scr, sacc_scr, bacc_scr, rate_scr, delta_scr, u_scr, gy_scr, gu_scr, gd_scr, h_scr, a_scr, gbt_scr,
    even_scr, odd_scr, sums_scr, h_now, gbc_ref, misc_scr, back_scr, gout_scr,
    mine, theirs, passed, b_local, b_done, one_send, one_recv, up_send, up_recv, down_send, down_recv, *scratch,
    slots, length, n_dp, n_f
):
    enter, send, relay, close = combiner(scratch, gdtl_ref, gbcs_ref, n_f)
    d = lax.axis_index("dp")
    f = lax.axis_index("fsdp")
    n_z = n_f // 2
    z = f // 2
    core = f % 2
    other = 1 - core

    def one(to, j):
        return remote(
            br_ref.at[to * 2 + other, j], theirs.at[to, j], one_send.at[to, j], one_recv.at[to, j], (d, z * 2 + other)
        )

    def up(to, j):
        return remote(mine.at[to, j], passed.at[to + 1, j], up_send.at[to, j], up_recv.at[to, j], (d, f + 2))

    def down(to, j):
        return remote(mine.at[to, j], passed.at[to, j], down_send.at[to, j], down_recv.at[to, j], (d, f - 2))

    def load(to, j):
        return pltpu.make_async_copy(br_ref.at[to * 2 + core, j], mine.at[to, j], b_local.at[to, j])

    done = pltpu.make_async_copy(mine.at[z], brr_ref, b_done.at[0])

    def pair(to, j):
        one(to, j).wait_recv()
        load(to, j).wait()
        mine[to, j] = (mine[to, j].astype(F32) + theirs[to, j].astype(F32)).astype(mine.dtype)

    def take(to, j, slot):
        mine[to, j] = (mine[to, j].astype(F32) + passed[slot, j].astype(F32)).astype(mine.dtype)

    def hop(u):
        above = z + n_z - 1 - u
        below = u - (n_z - 1 - z)

        @pl.when((above > z) & (above < n_z))
        def _():
            def block(j, carry):
                pair(above, j)

                @pl.when(z > 0)
                def _():
                    up(above, j).wait_recv()
                    take(above, j, above + 1)

                up(above, j).start()
                return carry

            lax.fori_loop(0, n_dp, block, 0)

        @pl.when((below < z) & (below >= 0))
        def _():
            def block(j, carry):
                pair(below, j)

                @pl.when(z < n_z - 1)
                def _():
                    down(below, j).wait_recv()
                    take(below, j, below)

                down(below, j).start()
                return carry

            lax.fori_loop(0, n_dp, block, 0)

    def settle():
        def block(j, carry):
            pair(z, j)

            @pl.when(z > 0)
            def _():
                up(z, j).wait_recv()
                take(z, j, z + 1)

            @pl.when(z < n_z - 1)
            def _():
                down(z, j).wait_recv()
                take(z, j, z)

            return carry

        lax.fori_loop(0, n_dp, block, 0)
        done.start()

    rows, width = inp_ref.shape
    steps = rows // slots
    states = lam_scr.shape[0]
    rank = dtl_ref.shape[1]
    step_id = pl.program_id(0)
    final = pl.num_programs(0) - 1
    parts = rows // length

    @pl.when(step_id == 0)
    def _():
        enter()
        for to in range(n_z):
            for j in range(n_dp):
                one(to, j).start()
                load(to, j).start()

    for u in range(n_z - 1):

        @pl.when(step_id == 1 + 2 * u)
        def _():
            hop(u)

    @pl.when(step_id > 0)
    def _():
        for a in range(parts):
            send((final - step_id + 1) * parts + a)

    @pl.when(step_id == 0)
    def _():
        lam_scr[...] = jnp.zeros_like(lam_scr)
        dacc_scr[...] = jnp.zeros_like(dacc_scr)
        sacc_scr[...] = jnp.zeros_like(sacc_scr)
        bacc_scr[...] = jnp.zeros_like(bacc_scr)
        gout_scr[...] = jnp.zeros_like(gout_scr)
        gmisc_ref[...] = jnp.zeros_like(gmisc_ref)
        misc_scr[...] = jnp.transpose(misc_ref[...].astype(F32))
        for n in range(states):
            rate_scr[n] = jnp.broadcast_to(-jnp.exp(misc_scr[DECAY + n : DECAY + n + 1, :]) * LOG2E, (slots, width))

    gb = gb_ref[...].reshape(rows, gb_ref.shape[-1])
    gate = gate_ref[...]
    sig = sigmoid(gate)
    silu = gate * sig
    y = y_ref[...]
    inp = inp_ref[...].astype(F32)
    g_gated = dot(gb, ow_ref[...], ((1,), (1,)))
    g_y = g_gated * silu
    gy_scr[...] = g_y
    ggate_ref[...] = (g_gated * y * (sig * (1.0 + gate * (1.0 - sig)))).astype(BF16)
    gout_scr[...] += dot((y * silu).astype(BF16), gb, ((0,), (0,)))
    sacc_scr[...] += jnp.sum((g_y * inp).reshape(steps, slots, width), axis=0)
    pre = dot(dtl_ref[...], dtw_ref[...], ((1,), (1,))) + misc_scr[DT_BIAS : DT_BIAS + 1, :]
    delta = softplus(pre)
    delta_scr[...] = delta
    u_scr[...] = delta * inp

    last = steps // PAIR - 1
    spread_lanes(bc_ref, even_scr, 0, slots, steps)
    h_now[...] = ck_ref[0]

    def replay(k, bcb_scr, next_scr):
        spread_lanes(bc_ref, next_scr, k + 1, slots, steps)
        ds, us, gys = [], [], []
        for j in range(PAIR):
            at = pl.ds(pl.multiple_of((k * PAIR + j) * slots, slots), slots)
            ds.append(delta_scr[at, :])
            us.append(u_scr[at, :])
            gys.append(gy_scr[at, :])
        for n in range(states):
            rate = rate_scr[n]
            h = h_now[n]
            for j in range(PAIR):
                t = k * PAIR + j
                h_scr[t, n] = h
                decay = jnp.exp2(ds[j] * rate)
                a_scr[t, n] = decay
                h = decay * h + us[j] * widen(bcb_scr[j, n], width)
                gbt_scr[states + n, pl.ds(pl.multiple_of(t * slots, slots), slots), :] = narrow(h * gys[j])
            h_now[n] = h

    def replay_twice(k, carry):
        replay(2 * k, even_scr, odd_scr)
        replay(2 * k + 1, odd_scr, even_scr)
        return carry

    lax.fori_loop(0, steps // PAIR // 2, replay_twice, 0)
    spread_lanes(bc_ref, even_scr, last, slots, steps)

    def reverse(k, bcb_scr, next_scr):
        spread_lanes(bc_ref, next_scr, jnp.maximum(k - 1, 0), slots, steps)
        ats, ds, us, gys, gus, gds, ts = [], [], [], [], [], [], []
        for j in range(PAIR):
            t = k * PAIR + j
            at = pl.ds(pl.multiple_of(t * slots, slots), slots)
            ts.append(t)
            ats.append(at)
            ds.append(delta_scr[at, :])
            us.append(u_scr[at, :])
            gys.append(gy_scr[at, :])
            gus.append(None)
            gds.append(None)
        for n in range(states):
            rate = rate_scr[n]
            carried = lam_scr[n]
            total = dacc_scr[n]
            for j in reversed(range(PAIR)):
                t = ts[j]
                lam = carried + gys[j] * widen(bcb_scr[j, states + n], width)
                term = lam * widen(bcb_scr[j, n], width)
                gus[j] = term if n == 0 else gus[j] + term
                gbt_scr[n, ats[j], :] = narrow(lam * us[j])
                carried = a_scr[t, n] * lam
                q = carried * h_scr[t, n]
                term = q * rate
                gds[j] = term if n == 0 else gds[j] + term
                total = total + q * ds[j]
            lam_scr[n] = carried
            dacc_scr[n] = total
        for j in range(PAIR):
            gu_scr[ats[j], :] = gus[j]
            gd_scr[ats[j], :] = gds[j]

    def reverse_twice(i, carry):
        k = last - 2 * i
        reverse(k, even_scr, odd_scr)
        reverse(k - 1, odd_scr, even_scr)
        return carry

    lax.fori_loop(0, steps // PAIR // 2, reverse_twice, 0)

    def reduce_lanes(k, carry):
        for j in range(LANES):
            n = k * LANES + j
            sums_scr[pl.ds(n, 1), :] = jnp.sum(jnp.transpose(gbt_scr[n]), axis=0, keepdims=True)
        return carry

    lax.fori_loop(0, 2 * states // LANES, reduce_lanes, 0)
    gbc_ref[...] = jnp.transpose(sums_scr[...])
    gu = gu_scr[...]
    gis_ref[...] = gu * delta_scr[...] + misc_scr[SKIP : SKIP + 1, :] * gy_scr[...]
    g_pre = (gd_scr[...] * (1.0 / LOG2E) + gu * inp) * sigmoid(pre)
    bacc_scr[...] += jnp.sum(g_pre.reshape(steps, slots, width), axis=0)
    g_low = g_pre.astype(BF16)
    gmisc_ref[:, :rank] += dot(g_low, dtl_ref[...], ((0,), (0,)))
    pack_rows(scratch[0], (final - step_id) * parts, dot(g_low, dtw_ref[...]), gbc_ref[...], length)

    @pl.when(step_id > 0)
    def _():
        for a in range(parts):
            relay((final - step_id + 1) * parts + a)

    @pl.when(step_id == pl.num_programs(0) - 1)
    def _():
        back_scr[...] = jnp.zeros_like(back_scr)
        for n in range(states):
            rate = -jnp.exp(misc_scr[DECAY + n : DECAY + n + 1, :])
            back_scr[DECAY + n : DECAY + n + 1, :] = jnp.sum(dacc_scr[n], axis=0, keepdims=True) * rate
        back_scr[SKIP : SKIP + 1, :] = jnp.sum(sacc_scr[...], axis=0, keepdims=True)
        back_scr[DT_BIAS : DT_BIAS + 1, :] = jnp.sum(bacc_scr[...], axis=0, keepdims=True)
        for a in range(parts):
            send(a)
        gmisc_ref[:, rank:] = jnp.transpose(back_scr[...])
        gout_ref[...] = gout_scr[...].astype(gout_ref.dtype)
        for a in range(parts):
            relay(a)
        steps_run = pl.num_programs(0)
        lax.fori_loop(jnp.minimum(steps_run // 2, n_z - 1), n_z - 1, lambda u, c: (hop(u), c)[1], 0)
        settle()
        close()
        done.wait()
        for to in range(n_z):
            for j in range(n_dp):
                one(to, j).wait_send()

                @pl.when(z < to)
                def _():
                    up(to, j).wait_send()

                @pl.when(z > to)
                def _():
                    down(to, j).wait_send()


def remote(src, dst, send, recv, where):
    return pltpu.make_async_remote_copy(
        src_ref=src, dst_ref=dst, send_sem=send, recv_sem=recv, device_id=where, device_id_type=pl.DeviceIdType.MESH
    )


def gather_kernel(
    tok_ref, cot_ref, win_ref, gain_ref, pk_ref, x_ref, c_ref, w_ref, g_ref, p_ref,
    tok_buf, cot_buf, win_buf, gain_buf, pk_buf, local_sem,
    tdp_send, tdp_recv, cdp_send, cdp_recv, up_send, up_recv, down_send, down_recv, core_send, core_recv,
    w1_send, w1_recv, w2_send, w2_recv, g1_send, g1_recv, g2_send, g2_recv, p_send, p_recv, *, n_dp, n_f
):
    d = lax.axis_index("dp")
    f = lax.axis_index("fsdp")
    n_z = n_f // 2
    z = f // 2
    core = f % 2
    partner = z * 2 + (1 - core)

    barrier = pltpu.get_barrier_semaphore()
    for k in range(1, n_f):
        pl.semaphore_signal(barrier, inc=1, device_id=(d, (f + k) % n_f), device_id_type=pl.DeviceIdType.MESH)
    for k in range(1, n_dp):
        pl.semaphore_signal(barrier, inc=1, device_id=((d + k) % n_dp, f), device_id_type=pl.DeviceIdType.MESH)
    pl.semaphore_wait(barrier, n_f + n_dp - 2)

    loads = (
        pltpu.make_async_copy(tok_ref.at[d], tok_buf, local_sem.at[0]),
        pltpu.make_async_copy(win_ref.at[f], win_buf, local_sem.at[1]),
        pltpu.make_async_copy(gain_ref, gain_buf, local_sem.at[2]),
        pltpu.make_async_copy(pk_ref, pk_buf, local_sem.at[3]),
        pltpu.make_async_copy(cot_ref.at[d], cot_buf, local_sem.at[8]),
    )
    stores = (
        pltpu.make_async_copy(tok_buf, x_ref.at[d, f], local_sem.at[4]),
        pltpu.make_async_copy(win_buf, w_ref.at[d, f], local_sem.at[5]),
        pltpu.make_async_copy(gain_buf, g_ref.at[d, f], local_sem.at[6]),
        pltpu.make_async_copy(pk_buf, p_ref.at[d], local_sem.at[7]),
        pltpu.make_async_copy(cot_buf, c_ref.at[d], local_sem.at[9]),
    )
    for load in loads:
        load.start()

    def tok_dp(k):
        to = (d + k) % n_dp
        return remote(tok_ref.at[to], x_ref.at[d, f], tdp_send.at[k], tdp_recv.at[k], (to, f))

    def tok_dp_arrival(k):
        src = (d - k + n_dp) % n_dp
        return remote(tok_ref.at[d], x_ref.at[src, f], tdp_send.at[k], tdp_recv.at[k], (src, f))

    def cot_dp(k):
        to = (d + k) % n_dp
        return remote(cot_ref.at[to], c_ref.at[d], cdp_send.at[k], cdp_recv.at[k], (to, f))

    def cot_dp_arrival(k):
        src = (d - k + n_dp) % n_dp
        return remote(cot_ref.at[d], c_ref.at[src], cdp_send.at[k], cdp_recv.at[k], (src, f))

    def w1(k):
        to = (f + k) % n_f
        return remote(win_ref.at[to], w_ref.at[d, f], w1_send.at[k], w1_recv.at[k], (d, to))

    def w1_arrival(k):
        src = (f - k + n_f) % n_f
        return remote(win_ref.at[f], w_ref.at[d, src], w1_send.at[k], w1_recv.at[k], (d, src))

    def g1(k):
        to = (f + k) % n_f
        return remote(gain_ref, g_ref.at[d, f], g1_send.at[k], g1_recv.at[k], (d, to))

    def g1_arrival(k):
        src = (f - k + n_f) % n_f
        return remote(gain_ref, g_ref.at[d, src], g1_send.at[k], g1_recv.at[k], (d, src))

    def w2(k):
        to = (d + k) % n_dp
        return remote(w_ref.at[d], w_ref.at[d], w2_send.at[k], w2_recv.at[k], (to, f))

    def w2_arrival(k):
        src = (d - k + n_dp) % n_dp
        return remote(w_ref.at[src], w_ref.at[src], w2_send.at[k], w2_recv.at[k], (src, f))

    def g2(k):
        to = (d + k) % n_dp
        return remote(g_ref.at[d], g_ref.at[d], g2_send.at[k], g2_recv.at[k], (to, f))

    def g2_arrival(k):
        src = (d - k + n_dp) % n_dp
        return remote(g_ref.at[src], g_ref.at[src], g2_send.at[k], g2_recv.at[k], (src, f))

    def pk(k):
        to = (d + k) % n_dp
        return remote(pk_ref, p_ref.at[d], p_send.at[k], p_recv.at[k], (to, f))

    def pk_arrival(k):
        src = (d - k + n_dp) % n_dp
        return remote(pk_ref, p_ref.at[src], p_send.at[k], p_recv.at[k], (src, f))

    def block(j, origin, side):
        at = (d - j + n_dp) % n_dp
        return x_ref.at[at, origin * 2 + side]

    def up(j, origin, src=None):
        ref = block(j, origin, core)
        return remote(ref if src is None else src, ref, up_send.at[origin, j], up_recv.at[origin, j], (d, f + 2))

    def down(j, origin, src=None):
        ref = block(j, origin, core)
        return remote(ref if src is None else src, ref, down_send.at[origin, j], down_recv.at[origin, j], (d, f - 2))

    def across(j, origin, src=None):
        ref = block(j, origin, core)
        return remote(
            ref if src is None else src, ref, core_send.at[origin, j], core_recv.at[origin, j], (d, partner)
        )

    def across_arrival(j, origin):
        ref = block(j, origin, 1 - core)
        return remote(ref, ref, core_send.at[origin, j], core_recv.at[origin, j], (d, partner))

    def launch(j, src=None):
        @pl.when(z < n_z - 1)
        def _():
            up(j, z, src).start()

        @pl.when(z > 0)
        def _():
            down(j, z, src).start()

        across(j, z, src).start()

    for k in range(1, n_f):
        w1(k).start()
    for k in range(1, n_dp):
        tok_dp(k).start()
    launch(0, tok_ref.at[d])
    for k in range(1, n_f):
        g1(k).start()
    for k in range(1, n_dp):
        pk(k).start()
    for load, store in zip(loads, stores):
        load.wait()
        store.start()
    for k in range(1, n_dp):
        tok_dp_arrival(k).wait_recv()
        launch(k)
    for store in stores:
        store.wait()
    for k in range(1, n_f):
        w1_arrival(k).wait_recv()
        g1_arrival(k).wait_recv()
    for k in range(1, n_dp):
        w2(k).start()
        g2(k).start()
    for k in range(1, n_dp):
        cot_dp(k).start()
    for far in range(1, n_z):
        for j in range(n_dp):

            @pl.when(z >= far)
            def _():
                origin = z - far
                up(j, origin).wait_recv()

                @pl.when(z < n_z - 1)
                def _():
                    up(j, origin).start()

                across(j, origin).start()

            @pl.when(z + far < n_z)
            def _():
                origin = z + far
                down(j, origin).wait_recv()

                @pl.when(z > 0)
                def _():
                    down(j, origin).start()

                across(j, origin).start()

    for origin in range(n_z):
        for j in range(n_dp):
            across_arrival(j, origin).wait_recv()
            across(j, origin).wait_send()
    for origin in range(n_z):
        for j in range(n_dp):

            @pl.when((origin <= z) & (z < n_z - 1))
            def _():
                up(j, origin).wait_send()

            @pl.when((origin >= z) & (z > 0))
            def _():
                down(j, origin).wait_send()

    for k in range(1, n_dp):
        pk_arrival(k).wait_recv()
        cot_dp_arrival(k).wait_recv()
        cot_dp(k).wait_send()
        w2_arrival(k).wait_recv()
        g2_arrival(k).wait_recv()
        tok_dp(k).wait_send()
        w2(k).wait_send()
        g2(k).wait_send()
        pk(k).wait_send()
    for k in range(1, n_f):
        w1(k).wait_send()
        g1(k).wait_send()


def pack_rows(out_ref, base, main, rest, chunk):
    part = chunk // 4
    for q in range(main.shape[0] // chunk):
        out_ref[base + q, 0:chunk, :] = main[q * chunk : (q + 1) * chunk, :]
        for j in range(4):
            first = q * chunk + j * part
            out_ref[base + q, chunk : chunk + part, j * 32 : (j + 1) * 32] = rest[first : first + part, :]


def combiner(scratch, main_ref, rest_ref, n_f):
    (
        part, own, one, sums, two, tops, rests, one_send, one_recv, two_send, two_recv, top_send, top_recv,
        rest_send, rest_recv, ctop_send, ctop_recv, crest_send, crest_recv,
    ) = scratch
    d = lax.axis_index("dp")
    f = lax.axis_index("fsdp")
    n_z = n_f // 2
    z = f // 2
    core = f % 2
    other = 1 - core
    partner = z * 2 + other
    chunk = tops.shape[2]

    def first(q):
        return remote(part.at[q], one.at[q // 2], one_send.at[q // 2], one_recv.at[q // 2], (d, partner))

    def second(to, k):
        return remote(sums.at[to], two.at[k], two_send.at[k], two_recv.at[k], (d, to * 2 + core))

    def third(k):
        to = ((z + k) % n_z * 2 + core,)
        return (
            remote(tops.at[z, core], tops.at[z, core], top_send.at[k], top_recv.at[k], (d,) + to),
            remote(rests.at[z, core], rests.at[z, core], rest_send.at[k], rest_recv.at[k], (d,) + to),
        )

    def third_arrival(k):
        src = (z - k + n_z) % n_z
        to = (src * 2 + core,)
        return (
            remote(tops.at[src, core], tops.at[src, core], top_send.at[k], top_recv.at[k], (d,) + to),
            remote(rests.at[src, core], rests.at[src, core], rest_send.at[k], rest_recv.at[k], (d,) + to),
        )

    def fourth(k, side):
        src = (z - k + n_z) % n_z
        return (
            remote(tops.at[src, side], tops.at[src, side], ctop_send.at[k], ctop_recv.at[k], (d, partner)),
            remote(rests.at[src, side], rests.at[src, side], crest_send.at[k], crest_recv.at[k], (d, partner)),
        )

    def enter(peers=()):
        barrier = pltpu.get_barrier_semaphore()
        for peer in peers:
            pl.semaphore_signal(barrier, inc=1, device_id=peer, device_id_type=pl.DeviceIdType.MESH)
        pl.semaphore_signal(barrier, inc=1, device_id=(d, partner), device_id_type=pl.DeviceIdType.MESH)
        for k in range(1, n_z):
            pl.semaphore_signal(
                barrier, inc=1, device_id=(d, (z + k) % n_z * 2 + core), device_id_type=pl.DeviceIdType.MESH
            )
        pl.semaphore_wait(barrier, n_z + len(peers))

    def send(q):
        @pl.when(q % 2 == other)
        def _():
            first(q).start()

    def relay(q):
        @pl.when(q % 2 == core)
        def _():
            to = q // 2
            first(q).wait_recv()
            total = part[q] + one[to]

            @pl.when(to == z)
            def _():
                own[...] = total

            @pl.when(to != z)
            def _():
                sums[to] = total.astype(sums.dtype)
                second(to, (to - z + n_z) % n_z).start()

    def close():
        total = own[...]
        for k in range(1, n_z):
            second(z, k).wait_recv()
            total = total + two[k].astype(F32)
        tops[z, core] = total[0:chunk, :].astype(tops.dtype)
        rests[z, core] = total[chunk:, :].astype(rests.dtype)
        for k in range(1, n_z):
            for copy in third(k):
                copy.start()
        for copy in fourth(0, core):
            copy.start()
        for k in range(1, n_z):
            for copy in third_arrival(k):
                copy.wait_recv()
            for copy in fourth(k, core):
                copy.start()
        for k in range(n_z):
            for copy in fourth(k, other):
                copy.wait_recv()
        quarter = chunk // 4
        for a in range(n_z):
            for b in range(2):
                at = (a * 2 + b) * chunk
                main_ref[at : at + chunk, :] = tops[a, b]
                rest = rests[a, b]
                for j in range(4):
                    rest_ref[at + j * quarter : at + (j + 1) * quarter, :] = rest[:, j * 32 : (j + 1) * 32]
        for k in range(n_z):
            first(k * 2 + other).wait_send()
            for copy in fourth(k, core):
                copy.wait_send()
            if k:
                second((z + k) % n_z, k).wait_send()
                for copy in third(k):
                    copy.wait_send()

    return enter, send, relay, close


def combine_scratch(n_f, length, rest_type):
    n_z = n_f // 2
    packed_rows = length + length // 4
    return [
        pltpu.VMEM((n_f, packed_rows, 128), F32), pltpu.VMEM((packed_rows, 128), F32),
        pltpu.VMEM((n_z, packed_rows, 128), F32), pltpu.VMEM((n_z, packed_rows, 128), HOP),
        pltpu.VMEM((n_z, packed_rows, 128), HOP), pltpu.VMEM((n_z, 2, length, 128), BF16),
        pltpu.VMEM((n_z, 2, length // 4, 128), rest_type),
    ] + [pltpu.SemaphoreType.DMA((n_z,))] * 12


def finish_kernel(
    gdtl_ref, gbc_ref, inp_ref, gis_ref, ggate_ref, inner_ref, before_ref, x_ref, gain_ref, win_ref, xw_ref, misc_ref,
    gout_ref, gback_ref, br_ref, out_ref, brout_ref, gin_out, gout_out,
    gx_out, gcw_out, gcb_out, gdt_out, gdtb_out, gdec_out, gskip_out, gg_out,
    misc_scr, tail_scr, gin_scr, gsel_scr, grest_scr, ggain_scr, pad_scr, gpad_scr, wacc_scr, cacc_scr,
    mine, theirs, passed, gin_low, side_got, line_got, side_end, line_end, gin_sum, gin_all, gout_got, gback_got, gtail_low, gtail_got,
    gg_low, gg_got, gg_sum, gg_all, br_buf, local_sem,
    one_send, one_recv, up_send, up_recv, down_send, down_recv, dp_send, dp_recv,
    r_send, r_recv, s1_send, s1_recv, l1_send, l1_recv, s2_send, s2_recv, l2_send, l2_recv, o_send, o_recv, b_send, b_recv, t_send, t_recv, g_send, g_recv,
    w2_send, w2_recv, g2_send, g2_recv, *, slots, n_dp, n_f
):
    d = lax.axis_index("dp")
    f = lax.axis_index("fsdp")
    n_z = n_f // 2
    z = f // 2
    core = f % 2
    other = 1 - core
    partner = z * 2 + other
    rows, width = inp_ref.shape
    steps = rows // slots
    halo = 3 * slots
    i = pl.program_id(0)
    blocks = mine.shape[0] * mine.shape[1] * mine.shape[2] // rows
    last = blocks - 1
    tile = mine.shape[2]
    held = rows // tile
    per = n_f // held
    pairs = held // 2
    rank = gdtl_ref.shape[1]
    d_rows, inner_rows = gin_out.shape[0], gout_out.shape[0]

    def place(q):
        return (last - q) // per, (last - q) % per * pairs

    def one(to, j):
        return remote(
            mine.at[to * 2 + other, j], theirs.at[to, j], one_send.at[to, j], one_recv.at[to, j], (d, partner)
        )

    def up(to, j):
        return remote(
            mine.at[to * 2 + core, j], passed.at[to + 1, j], up_send.at[to, j], up_recv.at[to, j], (d, f + 2)
        )

    def down(to, j):
        return remote(
            mine.at[to * 2 + core, j], passed.at[to, j], down_send.at[to, j], down_recv.at[to, j], (d, f - 2)
        )

    def dp(k):
        to = (d + k) % n_dp
        return remote(mine.at[f, to], out_ref.at[d], dp_send.at[k], dp_recv.at[k], (to, f))

    def dp_arrival(k):
        src = (d - k + n_dp) % n_dp
        return remote(mine.at[f, src], out_ref.at[src], dp_send.at[k], dp_recv.at[k], (src, f))

    def over_dp(src, dst, send, recv):
        return [
            remote(src.at[(d + k) % n_dp], dst.at[k], send.at[k], recv.at[k], ((d + k) % n_dp, f))
            for k in range(1, n_dp)
        ]

    def over_f(src, dst, send, recv, k):
        to = (f + k) % n_f
        return remote(src.at[to], dst.at[f], send.at[k], recv.at[k], (d, to))

    def over_f_arrival(src, dst, send, recv, k):
        to = (f - k + n_f) % n_f
        return remote(src.at[to], dst.at[to], send.at[k], recv.at[k], (d, to))

    def branch(k):
        to = (d + k) % n_dp
        return remote(br_ref.at[to], brout_ref.at[d], r_send.at[k], r_recv.at[k], (to, f))

    def branch_arrival(k):
        src = (d - k + n_dp) % n_dp
        return remote(br_ref.at[src], brout_ref.at[src], r_send.at[k], r_recv.at[k], (src, f))

    get_branch = pltpu.make_async_copy(br_ref.at[d], br_buf, local_sem.at[3])
    put_branch = pltpu.make_async_copy(br_buf, brout_ref.at[d], local_sem.at[4])
    outs = lambda: over_dp(gout_ref, gout_got, o_send, o_recv)
    backs = lambda: over_dp(gback_ref, gback_got, b_send, b_recv)

    n_a = n_dp // 2
    half = n_f // 2
    mine_a = d // 2
    mine_b = d % 2
    front_half, back_half = pl.ds(0, half), pl.ds(half, half)

    def side_first(a):
        return remote(
            gin_low.at[a * 2 + 1 - mine_b, front_half], side_got.at[a], s1_send.at[a], s1_recv.at[a],
            (mine_a * 2 + 1 - mine_b, f),
        )

    def line_first(k, b):
        to = (mine_a + k) % n_a
        return remote(
            gin_low.at[to * 2 + b, back_half], line_got.at[k, b], l1_send.at[k, b], l1_recv.at[k, b],
            (to * 2 + mine_b, f),
        )

    def line_second(k):
        to = (mine_a + k) % n_a
        return remote(
            gin_low.at[to * 2 + mine_b, front_half], line_end.at[k], l2_send.at[k], l2_recv.at[k], (to * 2 + mine_b, f)
        )

    def side_second():
        return remote(
            gin_low.at[mine_a * 2 + 1 - mine_b, back_half], side_end, s2_send.at[0], s2_recv.at[0],
            (mine_a * 2 + 1 - mine_b, f),
        )

    def firsts():
        return [side_first(a) for a in range(n_a)] + [line_first(k, b) for k in range(1, n_a) for b in range(2)]

    def seconds():
        return [line_second(k) for k in range(1, n_a)] + [side_second()]

    def middle():
        for copy in firsts():
            copy.wait_recv()

        def add(q, carry):
            for a in range(n_a):
                at = a * 2 + mine_b
                gin_low[at, q] = (gin_low[at, q].astype(F32) + side_got[a, q].astype(F32)).astype(gin_low.dtype)
            for b in range(2):
                at = mine_a * 2 + b
                total = gin_low[at, half + q].astype(F32)
                for k in range(1, n_a):
                    total = total + line_got[k, b, q].astype(F32)
                gin_low[at, half + q] = total.astype(gin_low.dtype)
            return carry

        lax.fori_loop(0, half, add, 0)
        for copy in seconds():
            copy.start()

    tails = lambda: over_dp(gtail_low, gtail_got, t_send, t_recv)
    gains = lambda: over_dp(gg_low, gg_got, g_send, g_recv)
    own_out = pltpu.make_async_copy(gout_ref.at[d], gout_got.at[0], local_sem.at[0])
    own_back = pltpu.make_async_copy(gback_ref.at[d], gback_got.at[0], local_sem.at[1])
    put = pltpu.make_async_copy(mine.at[f, d], out_ref.at[d], local_sem.at[2])

    def send_halves(q):
        j, first = place(q)
        for a in range(pairs):
            one(first + a, j).start()

    def pair(to, j):
        one(to, j).wait_recv()
        return mine[to * 2 + core, j].astype(F32) + theirs[to, j].astype(F32)

    def hops(step):
        q_up = step - 1 - LAG * z
        q_down = step - 1 - LAG * (n_z - 1 - z)
        q_end = step - 1 - LAG * jnp.maximum(z, n_z - 1 - z)

        @pl.when((q_up >= 0) & (q_up < blocks))
        def _():
            j, first = place(q_up)
            for a in range(pairs):
                to = first + a

                @pl.when(to > z)
                def _():
                    mine[to * 2 + core, j] = pair(to, j).astype(mine.dtype)

                    @pl.when(z > 0)
                    def _():
                        up(to, j).wait_recv()
                        mine[to * 2 + core, j] = (
                            mine[to * 2 + core, j].astype(F32) + passed[to + 1, j].astype(F32)
                        ).astype(mine.dtype)

            for a in range(pairs):

                @pl.when(first + a > z)
                def _():
                    up(first + a, j).start()

        @pl.when((q_down >= 0) & (q_down < blocks))
        def _():
            j, first = place(q_down)
            for a in range(pairs):
                to = first + a

                @pl.when(to < z)
                def _():
                    mine[to * 2 + core, j] = pair(to, j).astype(mine.dtype)

                    @pl.when(z < n_z - 1)
                    def _():
                        down(to, j).wait_recv()
                        mine[to * 2 + core, j] = (
                            mine[to * 2 + core, j].astype(F32) + passed[to, j].astype(F32)
                        ).astype(mine.dtype)

            for a in range(pairs):

                @pl.when(first + a < z)
                def _():
                    down(first + a, j).start()

        @pl.when((q_end >= 0) & (q_end < blocks))
        def _():
            j, first = place(q_end)

            @pl.when((z >= first) & (z < first + pairs))
            def _():
                mine[f, j] = pair(z, j).astype(mine.dtype)

                @pl.when(z > 0)
                def _():
                    up(z, j).wait_recv()
                    mine[f, j] = (mine[f, j].astype(F32) + passed[z + 1, j].astype(F32)).astype(mine.dtype)

                @pl.when(z < n_z - 1)
                def _():
                    down(z, j).wait_recv()
                    mine[f, j] = (mine[f, j].astype(F32) + passed[z, j].astype(F32)).astype(mine.dtype)

                for k in range(n_dp):

                    @pl.when(j == (d + k) % n_dp)
                    def _():
                        if k:
                            dp(k).start()
                        else:
                            put.start()

    @pl.when(i == 0)
    def _():
        barrier = pltpu.get_barrier_semaphore()
        for k in range(1, n_f):
            pl.semaphore_signal(barrier, inc=1, device_id=(d, (f + k) % n_f), device_id_type=pl.DeviceIdType.MESH)
        for k in range(1, n_dp):
            pl.semaphore_signal(barrier, inc=1, device_id=((d + k) % n_dp, f), device_id_type=pl.DeviceIdType.MESH)
        pl.semaphore_wait(barrier, n_f + n_dp - 2)
        for copy in outs() + backs():
            copy.start()
        for k in range(1, n_dp):
            branch(k).start()
        get_branch.start()
        own_out.start()
        own_back.start()
        gpad_scr[rows : rows + halo, :] = jnp.zeros((halo, width), F32)
        wacc_scr[...] = jnp.zeros_like(wacc_scr)
        cacc_scr[...] = jnp.zeros_like(cacc_scr)
        gin_scr[...] = jnp.zeros_like(gin_scr)
        gsel_scr[...] = jnp.zeros_like(gsel_scr)
        grest_scr[...] = jnp.zeros_like(grest_scr)
        ggain_scr[...] = jnp.zeros_like(ggain_scr)
        misc_scr[...] = jnp.transpose(misc_ref[...].astype(F32))

    @pl.when(i > 0)
    def _():
        send_halves(i - 1)

    gdtl = gdtl_ref[...]
    gbc = gbc_ref[...]
    inp = inp_ref[...]
    gsel_scr[...] += dot(inp, gdtl, ((0,), (0,)))
    grest_scr[:, :DECAY] += dot(inp, gbc, ((0,), (0,)))
    g_inputs = (
        gis_ref[...]
        + dot(gdtl, xw_ref[...], ((1,), (1,)))
        + dot(gbc, misc_ref[:, :DECAY], ((1,), (1,)))
    )
    pad_scr[0:halo, :] = before_ref[slots : slots + halo, :] * (i < last).astype(F32)
    pad_scr[halo : halo + rows, :] = inner_ref[...]
    total = jnp.broadcast_to(misc_scr[CONV_BIAS : CONV_BIAS + 1, :], (rows, width))
    for tap in range(4):
        total = total + misc_scr[TAPS + tap : TAPS + tap + 1, :] * pad_scr[tap * slots : tap * slots + rows, :]
    sig = sigmoid(total)
    g_conv = g_inputs * (sig * (1.0 + total * (1.0 - sig)))
    gpad_scr[0:rows, :] = g_conv
    g_inner = jnp.zeros((rows, width), F32)
    for tap in range(4):
        back = (3 - tap) * slots
        g_inner = g_inner + misc_scr[TAPS + tap : TAPS + tap + 1, :] * gpad_scr[back : back + rows, :]
        wacc_scr[tap] += jnp.sum(
            (g_conv * pad_scr[tap * slots : tap * slots + rows, :]).reshape(steps, slots, width), axis=0
        )
    cacc_scr[...] += jnp.sum(g_conv.reshape(steps, slots, width), axis=0)
    gpad_scr[rows : rows + halo, :] = gpad_scr[0:halo, :]
    g_both = jnp.concatenate([g_inner.astype(BF16), ggate_ref[...]], axis=1)
    x = x_ref[...].astype(F32)
    scaled = x * lax.rsqrt(jnp.mean(x * x, axis=-1, keepdims=True) + EPSILON)
    gin_scr[...] += dot((scaled * gain_ref[...]).astype(BF16), g_both, ((0,), (0,)))
    g_normed = dot(g_both, win_ref[...], ((1,), (1,)))
    ggain_scr[...] += jnp.sum(g_normed * scaled, axis=0, keepdims=True)
    block, first = place(i)
    for a in range(held):
        mine[first * 2 + a, block] = g_normed[a * tile : (a + 1) * tile, :].astype(mine.dtype)
    hops(i)

    @pl.when(i == last)
    def _():
        for a in range(n_dp):
            for b in range(n_f):
                at = (a * n_f + b) * d_rows
                gin_low[a, b] = gin_scr[at : at + d_rows, :].astype(gin_low.dtype)
                gg_low[a, b] = jnp.zeros((8, 128), F32)
                gg_low[a, b, 0:1, 0:d_rows] = ggain_scr[:, at : at + d_rows]
        tail_scr[...] = jnp.zeros_like(tail_scr)
        for tap in range(4):
            tail_scr[TAPS + tap : TAPS + tap + 1, :] = jnp.sum(wacc_scr[tap], axis=0, keepdims=True)
        tail_scr[CONV_BIAS : CONV_BIAS + 1, :] = jnp.sum(cacc_scr[...], axis=0, keepdims=True)
        grest_scr[:, DECAY:] = jnp.transpose(tail_scr[...])[:, DECAY:]
        for a in range(n_dp):
            at = a * inner_rows
            gtail_low[a, :, :rank] = gsel_scr[at : at + inner_rows, :]
            gtail_low[a, :, rank:] = grest_scr[at : at + inner_rows, :]
        send_halves(last)
        for copy in firsts() + tails() + gains():
            copy.start()
        hops(blocks)
        get_branch.wait()
        put_branch.start()
        own_out.wait()
        own_back.wait()
        for copy in outs() + backs():
            copy.wait_recv()
        total = gout_got[0].astype(F32)
        for k in range(1, n_dp):
            total = total + gout_got[k].astype(F32)
        gout_out[...] = total
        total = gback_got[0]
        for k in range(1, n_dp):
            total = total + gback_got[k]
        gdt_out[...] = total[:, :rank]
        total = jnp.transpose(total[:, rank:])
        gdec_out[...] = total[DECAY:TAPS, :]
        gdtb_out[...] = total[DT_BIAS : DT_BIAS + 1, :]
        gskip_out[...] = total[SKIP : SKIP + 1, :]

        def drain(step, carry):
            hops(step)
            return carry

        lax.fori_loop(blocks + 1, blocks + 1 + MID, drain, 0)
        middle()
        lax.fori_loop(blocks + 1 + MID, blocks + 1 + LAG * (n_z - 1), drain, 0)

        for copy in seconds() + tails() + gains():
            copy.wait_recv()

        def add(q, carry):
            total = gin_low[d, q].astype(F32)
            for k in range(1, n_a):
                total = total + line_end[k, q].astype(F32)
            gin_sum[q] = total.astype(gin_sum.dtype)
            total = gin_low[d, half + q].astype(F32) + side_end[q].astype(F32)
            gin_sum[half + q] = total.astype(gin_sum.dtype)
            return carry

        lax.fori_loop(0, half, add, 0)

        def add_gain(q, carry):
            total = gg_low[d, q]
            for k in range(1, n_dp):
                total = total + gg_got[k, q]
            gg_sum[q] = total
            return carry

        lax.fori_loop(0, n_f, add_gain, 0)
        for k in range(1, n_f):
            over_f(gin_sum, gin_all, w2_send, w2_recv, k).start()
            over_f(gg_sum, gg_all, g2_send, g2_recv, k).start()
        gin_all[f] = gin_sum[f]
        gg_all[f] = gg_sum[f]
        total = gtail_low[d]
        for k in range(1, n_dp):
            total = total + gtail_got[k]
        gx_out[:rank, :] = jnp.transpose(total[:, :rank])
        total = jnp.transpose(total[:, rank:])
        gx_out[rank:, :] = total[:DECAY, :]
        gcw_out[...] = total[TAPS:CONV_BIAS, :]
        gcb_out[...] = total[CONV_BIAS : CONV_BIAS + 1, :]
        for k in range(1, n_f):
            over_f_arrival(gin_sum, gin_all, w2_send, w2_recv, k).wait_recv()
            over_f_arrival(gg_sum, gg_all, g2_send, g2_recv, k).wait_recv()
        total = gg_all[0]
        for b in range(1, n_f):
            total = total + gg_all[b]
        gg_out[...] = total[0:1, 0:d_rows]
        for b in range(n_f):
            for h in range(2):
                for a in range(n_dp):
                    to = (h * n_dp + a) * n_f * inner_rows + b * inner_rows
                    at = (h * n_dp + a) * inner_rows
                    gin_out[:, to : to + inner_rows] = gin_all[b, :, at : at + inner_rows].astype(F32)
        for k in range(1, n_dp):
            dp_arrival(k).wait_recv()
            dp(k).wait_send()
        put.wait()
        put_branch.wait()
        for k in range(1, n_dp):
            branch_arrival(k).wait_recv()
            branch(k).wait_send()
        for copy in outs() + backs() + firsts() + seconds() + tails() + gains():
            copy.wait_send()
        for k in range(1, n_f):
            over_f(gin_sum, gin_all, w2_send, w2_recv, k).wait_send()
            over_f(gg_sum, gg_all, g2_send, g2_recv, k).wait_send()
        for to in range(n_z):
            for j in range(n_dp):
                one(to, j).wait_send()

                @pl.when(z < to)
                def _():
                    up(to, j).wait_send()

                @pl.when(z > to)
                def _():
                    down(to, j).wait_send()


def whole(shape):
    return pl.BlockSpec(shape, lambda i: (0,) * len(shape))


def cost(micros):
    return pl.CostEstimate(flops=int(micros * 1.15e9), bytes_accessed=1 << 20, transcendentals=0)


def params(number=None):
    if number is None:
        return pltpu.CompilerParams(vmem_limit_bytes=VMEM_BYTES, dimension_semantics=("arbitrary",))
    return pltpu.CompilerParams(
        vmem_limit_bytes=FULL_VMEM, dimension_semantics=("arbitrary",), collective_id=number, has_side_effects=True
    )


def body(
    tokens, cotangent, lengths, deal_order, norm_gain, in_weight, conv_weight, conv_bias,
    x_weight, dt_weight, dt_bias, decay_log, skip_gain, out_weight, *, n_dp, n_f
):
    seqs, own, model = tokens.shape
    slots = seqs // n_dp
    inner_rows, states = decay_log.shape
    rank = dt_weight.shape[1]
    width = inner_rows * n_dp
    length = own * n_dp * n_f
    d_rows = in_weight.shape[0]
    total_rows = length * slots
    group = lax.axis_index("dp")
    member = lax.axis_index("fsdp")

    low = lambda v: v.astype(BF16)
    slot_ids = jnp.arange(seqs, dtype=jnp.int32)
    seq_len = jnp.sum(jnp.where(deal_order[:, None] == slot_ids[None, :], lengths[:, None], 0), axis=0)
    own_pos = (group * n_f + member) * own + jnp.arange(own, dtype=jnp.int32)
    own_mask = own_pos[None, :] < seq_len[:, None]

    def by_group(v):
        return v.reshape(n_dp, slots, own, model).transpose(0, 2, 1, 3).reshape(n_dp, own * slots, model)

    def by_seq(v):
        return v.reshape(n_dp, own, slots, model).transpose(0, 2, 1, 3).reshape(seqs, own, model).astype(F32)

    masked = by_group(jnp.where(own_mask[:, :, None], cotangent, jnp.zeros_like(cotangent)))

    tok = by_group(tokens)
    win = low(in_weight).reshape(d_rows, 2, n_dp, n_f, inner_rows).transpose(3, 0, 1, 2, 4)
    win = win.reshape(n_f, d_rows, 2 * width)
    gain_tile = jnp.zeros((8, 128), F32).at[0, :d_rows].set(low(norm_gain).astype(F32))
    misc = jnp.concatenate(
        [x_weight[:, rank:], decay_log, conv_weight, conv_bias[:, None], dt_bias[:, None], skip_gain[:, None]], axis=1
    )
    misc = jnp.pad(misc, ((0, 0), (0, 128 - misc.shape[1])))
    packed = low(jnp.concatenate([x_weight[:, :rank], misc, dt_weight], axis=1))
    ow = out_weight
    n_z = n_f // 2
    dma = pltpu.SemaphoreType.DMA
    hbm = pl.BlockSpec(memory_space=pl.ANY)
    x, g_branch, win, gain, packed = pl.pallas_call(
        functools.partial(gather_kernel, n_dp=n_dp, n_f=n_f),
        in_specs=[hbm] * 5,
        out_specs=[hbm] * 5,
        out_shape=[
            jax.ShapeDtypeStruct((n_dp, n_f) + tok.shape[1:], BF16),
            jax.ShapeDtypeStruct(tok.shape, BF16),
            jax.ShapeDtypeStruct((n_dp, n_f) + win.shape[1:], BF16),
            jax.ShapeDtypeStruct((n_dp, n_f, 8, 128), F32),
            jax.ShapeDtypeStruct((n_dp,) + packed.shape, BF16),
        ],
        scratch_shapes=[
            pltpu.VMEM(tok.shape[1:], BF16), pltpu.VMEM(tok.shape[1:], BF16), pltpu.VMEM(win.shape[1:], BF16),
            pltpu.VMEM((8, 128), F32), pltpu.VMEM(packed.shape, BF16), dma((10,)),
            dma((n_dp,)), dma((n_dp,)), dma((n_dp,)), dma((n_dp,)),
        ]
        + [dma((n_z, n_dp))] * 6
        + [dma((n_f,)), dma((n_f,)), dma((n_dp,)), dma((n_dp,)), dma((n_f,)), dma((n_f,))]
        + [dma((n_dp,))] * 4,
        compiler_params=pltpu.CompilerParams(collective_id=1, has_side_effects=True),
        cost_estimate=cost(90),
        name="gather",
    )(tok, masked, win, gain_tile, packed)
    x = x.reshape(total_rows, model)
    win = win.reshape(model, 2 * width)
    gain = gain[:, :, 0, :d_rows].reshape(1, model)
    packed = packed.reshape(width, -1)
    span = ROWS // slots
    rows = span * slots
    blocks = length // span
    grid = (blocks,)
    row_spec = lambda cols: pl.BlockSpec((rows, cols), lambda i: (i, 0))
    rev_spec = lambda cols: pl.BlockSpec((rows, cols), lambda i: (blocks - 1 - i, 0))
    once = dict(pipeline_mode=pl.Buffered(1))
    ow_spec = pl.BlockSpec((width, model), lambda i: (0, 0), **once)
    xw_spec = pl.BlockSpec((width, 128), lambda i: (0, 0), **once)
    misc_spec = pl.BlockSpec((width, 128), lambda i: (0, 1), **once)
    dtw_spec = pl.BlockSpec((width, 128), lambda i: (0, 2), **once)
    win_spec = pl.BlockSpec((model, 2 * width), lambda i: (0, 0), **once)
    misc_shape = pltpu.VMEM((128, width), F32)
    like = jax.ShapeDtypeStruct
    held = span // own
    per = n_f // held
    piece = (held, 1, own * slots, model)
    piece_spec = pl.BlockSpec(piece, lambda i: (i % per, i // per, 0, 0))
    rev_piece_spec = pl.BlockSpec(piece, lambda i: ((blocks - 1 - i) % per, (blocks - 1 - i) // per, 0, 0))
    pieces_shape = like((n_f, n_dp, own * slots, model), BF16)
    inner, gate, inp, dtl, bc, ow, g_branch = pl.pallas_call(
        functools.partial(front_kernel, slots=slots, length=length, n_dp=n_dp, n_f=n_f),
        grid=grid,
        in_specs=[
            row_spec(model), whole((1, model)), win_spec, xw_spec, misc_spec, hbm, hbm,
        ],
        out_specs=[
            row_spec(width), row_spec(width), row_spec(width), whole((total_rows, rank)), whole((total_rows, 2 * states)),
            hbm, hbm,
        ],
        out_shape=[
            like((total_rows, width), F32), like((total_rows, width), F32), like((total_rows, width), BF16),
            like((total_rows, rank), BF16), like((total_rows, 2 * states), F32), like((n_dp,) + ow.shape, BF16), pieces_shape,
        ],
        scratch_shapes=[
            pltpu.VMEM((rows + 3 * slots, width), F32), misc_shape, pltpu.VMEM(ow.shape, F32), pltpu.VMEM(ow.shape, BF16),
            dma((n_dp,)), dma((n_dp,)), dma((2,)), pltpu.VMEM((n_dp, own * slots, model), BF16), dma((2,)),
        ]
        + [dma((n_dp,))] * 6
        + combine_scratch(n_f, length, F32),
        compiler_params=params(2),
        cost_estimate=cost(42),
        name="front",
    )(x, gain, win, packed, packed, ow, g_branch)
    ow = ow.reshape(width, model)


    y, ck, branch, g_branch = pl.pallas_call(
        functools.partial(mix_kernel, slots=slots, n_dp=n_dp, n_f=n_f),
        grid=grid,
        in_specs=[
            row_spec(rank), row_spec(2 * states), row_spec(width), row_spec(width), dtw_spec, misc_spec, ow_spec, hbm,
        ],
        out_specs=[
            row_spec(width), pl.BlockSpec((1, states, slots, width), lambda i: (i, 0, 0, 0)), piece_spec, hbm,
        ],
        out_shape=[
            like((total_rows, width), F32), like((blocks, states, slots, width), F32), pieces_shape,
            pieces_shape,
        ],
        scratch_shapes=[
            pltpu.VMEM((states, slots, width), F32), pltpu.VMEM((rows, width), F32), pltpu.VMEM((rows, width), F32),
            pltpu.VMEM((states, slots, width), F32), pltpu.VMEM((PAIR, 2 * states, slots, 128), F32),
            pltpu.VMEM((PAIR, 2 * states, slots, 128), F32), misc_shape,
        ]
        + [dma((n_z, n_dp))] * 6,
        input_output_aliases={7: 3},
        compiler_params=params(5),
        cost_estimate=cost(36),
        name="mix",
    )(dtl, bc, inp, gate, packed, packed, ow, g_branch)

    gis, ggate, gdtl, gbc, gout, gmisc, branch = pl.pallas_call(
        functools.partial(back_kernel, slots=slots, length=length, n_dp=n_dp, n_f=n_f),
        grid=grid,
        in_specs=[
            rev_piece_spec, rev_spec(rank), rev_spec(2 * states), rev_spec(width), rev_spec(width), rev_spec(width),
            pl.BlockSpec((1, states, slots, width), lambda i: (blocks - 1 - i, 0, 0, 0)), dtw_spec, misc_spec, ow_spec,
            hbm,
        ],
        out_specs=[
            rev_spec(width), rev_spec(width), whole((total_rows, rank)), whole((total_rows, 2 * states)),
            whole((width, model)), whole((width, 256)), hbm,
        ],
        out_shape=[
            like((total_rows, width), F32), like((total_rows, width), BF16), like((total_rows, rank), BF16),
            like((total_rows, 2 * states), BF16), like((width, model), BF16), like((width, 256), F32),
            like((n_dp, own * slots, model), BF16),
        ],
        scratch_shapes=[
            pltpu.VMEM((states, slots, width), F32), pltpu.VMEM((states, slots, width), F32),
            pltpu.VMEM((slots, width), F32), pltpu.VMEM((slots, width), F32), pltpu.VMEM((states, slots, width), F32),
        ]
        + [pltpu.VMEM((rows, width), F32)] * 5
        + [
            pltpu.VMEM((span, states, slots, width), F32), pltpu.VMEM((span, states, slots, width), F32),
            pltpu.VMEM((2 * states, rows, 128), F32), pltpu.VMEM((PAIR, 2 * states, slots, 128), F32),
            pltpu.VMEM((PAIR, 2 * states, slots, 128), F32), pltpu.VMEM((2 * states, rows), F32),
            pltpu.VMEM((states, slots, width), F32), pltpu.VMEM((rows, 2 * states), F32), misc_shape, misc_shape,
            pltpu.VMEM((width, model), F32), pltpu.VMEM((n_z, n_dp, own * slots, model), BF16),
            pltpu.VMEM((n_z, n_dp, own * slots, model), BF16), pltpu.VMEM((n_z + 1, n_dp, own * slots, model), BF16),
            dma((n_z, n_dp)), dma((1,)),
        ]
        + [dma((n_z, n_dp))] * 6
        + combine_scratch(n_f, length, BF16),
        compiler_params=params(3),
        cost_estimate=cost(100),
        name="back",
    )(g_branch, dtl, bc, inp, gate, y, ck, packed, packed, ow, branch)


    tile = own * slots
    vmem = pltpu.VMEM
    g_normed, branch, gin, gout, gx, gcw, gcb, gdt, gdtb, gdec, gskip, ggain = pl.pallas_call(
        functools.partial(finish_kernel, slots=slots, n_dp=n_dp, n_f=n_f),
        grid=grid,
        in_specs=[
            rev_spec(rank), rev_spec(2 * states), rev_spec(width), rev_spec(width), rev_spec(width), rev_spec(width),
            pl.BlockSpec((4 * slots, width), lambda i: (jnp.maximum((blocks - 1 - i) * (span // 4) - 1, 0), 0)),
            rev_spec(model), whole((1, model)), win_spec, xw_spec, misc_spec, hbm, hbm, hbm,
        ],
        out_specs=[
            hbm, hbm, whole((d_rows, 2 * width * n_f)), whole((inner_rows, model)),
            whole((rank + 2 * states, inner_rows)), whole((4, inner_rows)), whole((1, inner_rows)),
            whole((inner_rows, rank)), whole((1, inner_rows)), whole((states, inner_rows)), whole((1, inner_rows)),
            whole((1, d_rows)),
        ],
        out_shape=[
            like((n_dp, tile, model), BF16), like((n_dp, tile, model), BF16), like((d_rows, 2 * width * n_f), F32), like((inner_rows, model), F32),
            like((rank + 2 * states, inner_rows), F32), like((4, inner_rows), F32), like((1, inner_rows), F32),
            like((inner_rows, rank), F32), like((1, inner_rows), F32), like((states, inner_rows), F32),
            like((1, inner_rows), F32), like((1, d_rows), F32),
        ],
        scratch_shapes=[
            misc_shape, misc_shape, vmem((model, 2 * width), F32), vmem((width, 128), F32), vmem((width, 128), F32),
            vmem((1, model), F32), vmem((rows + 3 * slots, width), F32), vmem((rows + 3 * slots, width), F32),
            vmem((4, slots, width), F32), vmem((slots, width), F32),
            vmem((n_f, n_dp, tile, model), BF16), vmem((n_z, n_dp, tile, model), BF16),
            vmem((n_z + 1, n_dp, tile, model), BF16),
            vmem((n_dp, n_f, d_rows, 2 * width), BF16), vmem((n_dp // 2, n_z, d_rows, 2 * width), BF16),
            vmem((n_dp // 2, 2, n_z, d_rows, 2 * width), BF16), vmem((n_z, d_rows, 2 * width), BF16),
            vmem((n_dp // 2, n_z, d_rows, 2 * width), BF16),
            vmem((n_f, d_rows, 2 * width), BF16), vmem((n_f, d_rows, 2 * width), BF16),
            vmem((n_dp, inner_rows, model), BF16), vmem((n_dp, inner_rows, 256), F32),
            vmem((n_dp, inner_rows, 256), F32), vmem((n_dp, inner_rows, 256), F32),
            vmem((n_dp, n_f, 8, 128), F32), vmem((n_dp, n_f, 8, 128), F32), vmem((n_f, 8, 128), F32),
            vmem((n_f, 8, 128), F32), vmem((tile, model), BF16), dma((5,)),
        ]
        + [dma((n_z, n_dp))] * 6
        + [dma((n_dp,))] * 4
        + [dma((n_dp // 2,))] * 2
        + [dma((n_dp // 2, 2))] * 2
        + [dma((1,))] * 2
        + [dma((n_dp // 2,))] * 2
        + [dma((n_dp,))] * 8
        + [dma((n_f,))] * 4,
        compiler_params=params(4),
        cost_estimate=cost(105),
        name="finish",
    )(
        gdtl, gbc, inp, gis, ggate, inner, inner, x, gain, win, packed, packed,
        gout.reshape(n_dp, inner_rows, model), gmisc.reshape(n_dp, inner_rows, 256), branch,
    )

    hidden = tokens.astype(F32)
    upstream = cotangent.astype(F32)
    output = (hidden + jnp.where(own_mask[:, :, None], by_seq(branch), 0.0)).astype(BF16)
    g_normed = by_seq(g_normed)
    factor = lax.rsqrt(jnp.mean(hidden * hidden, axis=-1, keepdims=True) + EPSILON)
    weighted = gain * g_normed
    input_grad = (
        upstream + factor * weighted - hidden * factor**3 * jnp.mean(hidden * weighted, axis=-1, keepdims=True)
    ).astype(BF16)
    return (
        output, input_grad, ggain.reshape(d_rows), gin, gcw.T, gcb.reshape(inner_rows), gx.T, gdt,
        gdtb.reshape(inner_rows), gdec.T, gskip.reshape(inner_rows), gout,
    )


def solution(mesh):
    rows1, rows2, pos = P(BOTH), P(BOTH, None), P(None, BOTH, None)
    return jax.shard_map(
        functools.partial(body, n_dp=mesh.shape["dp"], n_f=mesh.shape["fsdp"]),
        mesh=mesh,
        in_specs=(pos, pos, P(), P(), rows1, rows2, rows2, rows1, rows2, rows2, rows1, rows2, rows1, rows2),
        out_specs=(pos, pos, rows1, rows2, rows2, rows1, rows2, rows2, rows1, rows2, rows1, rows2),
        check_vma=False,
    )
```
